32 devices in a mesh: scen: 8 (over z, x), row: 2 (over core), col: 2 (over y).
Axes of the slice: x: 2, y: 2, z: 4, core: 2. Of those that a mesh axis runs over, the one named last changes fastest.
Arguments:
- kkt: float32 [24, 768, 768], P('scen', ('row', 'col')), as said below
- border: float32 [24, 768, 4096], P('scen', None, ('row', 'col')), may hold values from -0.21875 to 0.21875
- first_diag: float32 [4096], P('scen'), may hold values from 0.5 to 1.5
- assignment: int32 [24], P('scen'), may hold values from 0 to 23, as said below
- panel: int32 [8], replicated, may hold values from 0 to 7, each once
Outputs:
- schur: float32 [4096, 4096], P('scen', ('row', 'col'))
- panel_factor: float32 [4096, 512], P('scen', ('row', 'col'))
The draws below stay inside these ranges and needn't reach their ends.
Inputs may be any that keep to these rules, and one draw needn't show every extreme that they name: assignment is a permutation; with k = d * 3 + j (0 <= j < 3), assignment[k] is either k or (d XOR 1) * 3 + j, and the two scenarios of such a pair are either both fixed or swapped. panel is a permutation. Each kkt block is symmetric positive definite; after scaling by its diagonal, the off-diagonal part has spectral norm about one half.
All inputs are finite; a program needn't handle non-finite values.
Results may differ from the reference program's by a relative error of at most 0.00015.
Values sent between devices are 32-bit elements; how exact they have to be, the bound alone decides.
A program may use at most 192 MiB of HBM per device.

```python
import math
import jax
import jax.numpy as jnp
from jax import lax

NK = 768
NF = 4096
PW = 512
NEWTON = 3
S_DEV = 3
NSCEN = 24


def draw_kkt(key, part):
    first_key, second_key, third_key = jax.random.split(jax.random.fold_in(key, 11), 3)
    entry_scale = jnp.exp(jax.random.uniform(first_key, (NSCEN, NK), minval=math.log(0.5), maxval=math.log(4.0)))
    scen_scale = jnp.exp(jax.random.uniform(third_key, (NSCEN, 1), minval=math.log(0.5), maxval=math.log(4.0)))
    scales = entry_scale * scen_scale
    noise = jax.random.normal(second_key, (NSCEN, NK, NK))
    paired = (noise + jnp.swapaxes(noise, 1, 2)) * (0.25 / math.sqrt(2.0 * NK))
    paired = paired * (1.0 - jnp.eye(NK, dtype=jnp.float32))[None]
    roots = jnp.sqrt(scales)
    blocks = roots[:, :, None] * paired * roots[:, None, :]
    blocks = blocks + jnp.eye(NK, dtype=jnp.float32)[None] * scales[:, :, None]
    return blocks.astype(jnp.float32)


def draw_assignment(key, part):
    groups = NSCEN // S_DEV
    flips = jax.random.randint(jax.random.fold_in(key, 23), (groups // 2, S_DEV), 0, 2)
    flips = jnp.repeat(flips, 2, axis=0)
    device_ids = jnp.arange(groups, dtype=jnp.int32)[:, None]
    slot_ids = jnp.arange(S_DEV, dtype=jnp.int32)[None, :]
    own = device_ids * S_DEV + slot_ids
    other = (device_ids + 1 - 2 * (device_ids % 2)) * S_DEV + slot_ids
    chosen = jnp.where(flips == 1, other, own)
    return chosen.reshape(-1).astype(jnp.int32)


def block_levels(key, extent, cuts, low, high):
    loudness, own = 1.0, jax.random.fold_in(key, 6)
    for position, parts in cuts:
        draws = jnp.exp(jax.random.uniform(jax.random.fold_in(own, position), (parts,), jnp.float32, low / len(cuts), high / len(cuts)))
        loudness = loudness * jnp.repeat(draws, extent[position] // parts).reshape([-1 if axis == position else 1 for axis in range(len(extent))])
    return loudness


def bell_draw(stream_key, dims, scale, most, shards=(), kind=jnp.bfloat16):
    loudness = block_levels(stream_key, dims, shards, -0.22, 0.18) if shards else 1.0
    array = jax.random.normal(stream_key, dims, jnp.float32) * scale * loudness
    return jnp.minimum(jnp.maximum(array, -most), most).astype(kind)


def setup_inputs(seed: int = 0) -> dict:
    keys = jax.random.split(jax.random.key(seed), 6)
    kkt = draw_kkt(jax.random.fold_in(keys[5], 71), 0)
    border = bell_draw(keys[1], (NSCEN, NK, NF), (2.0 * (NK * NSCEN) ** -0.5), 0.21875, ((0, 8), (2, 4)), jnp.float32)
    first_diag = jnp.clip(0.5 + 1.0 * jax.random.uniform(keys[2], (NF,), jnp.float32) ** block_levels(keys[2], (NF,), ((0, 8),), -0.2, 0.2), 0.5, 1.5)
    assignment = draw_assignment(jax.random.fold_in(keys[5], 71), 0)
    panel = jax.random.permutation(keys[4], NF // PW).astype(jnp.int32)
    return {"kkt": kkt, "border": border, "first_diag": first_diag, "assignment": assignment, "panel": panel}


HIGH = lax.Precision.HIGHEST

def invert(kkt_block):
    inv_diag = 1.0 / jnp.diagonal(kkt_block)
    approx = jnp.diag(inv_diag)
    for step in range(NEWTON):
        left = jnp.dot(approx.astype(jnp.float32), kkt_block.astype(jnp.float32), precision=HIGH, preferred_element_type=jnp.float32)
        approx = 2.0 * approx - jnp.dot(left.astype(jnp.float32), approx.astype(jnp.float32), precision=HIGH, preferred_element_type=jnp.float32)
    return approx

def reference(kkt, border, first_diag, assignment, panel):
    start_schur = jnp.diag(first_diag)

    def add_scenario(index, schur):
        block = lax.dynamic_index_in_dim(kkt, index, 0, keepdims=False)
        approx = invert(block)
        chosen = lax.dynamic_index_in_dim(border, assignment[index], 0, keepdims=False)
        solved = jnp.dot(approx.astype(jnp.float32), chosen.astype(jnp.float32), precision=HIGH, preferred_element_type=jnp.float32)
        return schur + lax.dot_general(chosen.astype(jnp.float32), solved.astype(jnp.float32), (((0,), (0,)), ((), ())), precision=HIGH, preferred_element_type=jnp.float32)
    schur = lax.fori_loop(0, NSCEN, add_scenario, start_schur)
    start = panel[0] * PW
    columns = lax.dynamic_slice_in_dim(schur, start, PW, 1)
    block = lax.dynamic_slice_in_dim(columns, start, PW, 0)
    symmetric = 0.5 * (block + block.T)
    lower_factor = jnp.linalg.cholesky(symmetric)
    factor = lax.linalg.triangular_solve(lower_factor, columns, left_side=False, lower=True, transpose_a=True)
    return (schur, factor)
```

```python
import jax
import jax.numpy as jnp
from jax import lax
from jax.sharding import PartitionSpec as P

PW = 512
NEWTON = 3


HIGH = lax.Precision.HIGH
GROUP = ("row", "col")
ALL = ("scen", "row", "col")
CHUNKS = 2


def swapped(value, axis, distance):
    mask = 2**distance
    pairs = [(source, source ^ mask) for source in range(lax.axis_size(axis))]
    return lax.ppermute(value, axis, pairs)


def gathered_rows(value, axis):
    count = lax.axis_size(axis)
    index = lax.axis_index(axis)
    rows = value.shape[1]
    whole = jnp.zeros((value.shape[0], rows * count, value.shape[2]), value.dtype)
    whole = lax.dynamic_update_slice_in_dim(whole, value, index * rows, 1)
    for shift in range(1, count):
        pairs = [(source, (source + shift) % count) for source in range(count)]
        origin = lax.rem(index - shift + count, count)
        whole = lax.dynamic_update_slice_in_dim(
            whole, lax.ppermute(value, axis, pairs), origin * rows, 1
        )
    return whole


def matmul(left, right, precision=HIGH):
    return jnp.dot(left, right, precision=precision, preferred_element_type=jnp.float32)


def contract(left, right):
    return lax.dot_general(
        left, right, (((0,), (0,)), ((), ())), precision=HIGH, preferred_element_type=jnp.float32
    )


def plain_body(kkt, border, first_diag, assignment, panel):
    scen_index = lax.axis_index("scen")
    own_index = lax.axis_index(GROUP)
    group_size = lax.axis_size(GROUP)
    slots, order, col_count = border.shape
    width = col_count * group_size
    scenario_ids = scen_index * slots + jnp.arange(slots, dtype=jnp.int32)
    kkt = jnp.where((assignment == scenario_ids)[:, None, None], kkt, swapped(kkt, "scen", 0))
    kkt_all = gathered_rows(gathered_rows(kkt, "col"), "row")
    gathered = lax.all_gather(border, GROUP, axis=2, tiled=True)
    eye = jnp.eye(order, dtype=jnp.bool_)
    inverses = []
    for slot in range(slots):
        full = kkt_all[slot]
        diag = jnp.where(eye, full, 0.0)
        row_inv = 1.0 / jnp.sum(diag, axis=1, keepdims=True)
        col_inv = 1.0 / jnp.sum(diag, axis=0, keepdims=True)
        approx = jnp.where(eye, 2.0 * row_inv, 0.0) - row_inv * full * col_inv
        for step in range(NEWTON - 1):
            approx = 2.0 * approx - matmul(matmul(approx, full), approx)
        inverses.append(approx)
    solved = jnp.concatenate([matmul(inverses[slot], border[slot]) for slot in range(slots)], 0)
    border_all = gathered.reshape(slots * order, width)

    panel_start = panel[0] * PW
    share = PW // group_size
    own_start = panel_start + own_index * share

    share_solved = jnp.concatenate(
        [
            matmul(inverses[slot], lax.dynamic_slice_in_dim(gathered[slot], own_start, share, 1))
            for slot in range(slots)
        ],
        0,
    )
    panel_border = lax.dynamic_slice_in_dim(border_all, panel_start, PW, 1)
    block = contract(panel_border, share_solved)
    row_span = first_diag.shape[0]
    global_rows = scen_index * row_span + jnp.arange(row_span, dtype=jnp.int32)
    share_ids = own_start + jnp.arange(share, dtype=jnp.int32)
    owned = global_rows[:, None] == share_ids[None, :]
    share_diag = jnp.sum(jnp.where(owned, first_diag[:, None], 0.0), axis=0)
    panel_ids = panel_start + jnp.arange(PW, dtype=jnp.int32)
    block = block + jnp.where(panel_ids[:, None] == share_ids[None, :], share_diag[None, :], 0.0)
    block = lax.psum(block, "scen")
    block = lax.all_gather(block, GROUP, axis=1, tiled=True)
    symmetric = 0.5 * (block + block.T)
    lower_factor = jnp.linalg.cholesky(symmetric)
    lower_inverse = lax.linalg.triangular_solve(
        lower_factor, jnp.eye(PW, dtype=jnp.float32), left_side=True, lower=True
    )
    own_inverse = lax.dynamic_slice_in_dim(lower_inverse, own_index * share, share, 0)

    def schur_columns(start, count, solved):
        tile = contract(border_all, lax.dynamic_slice_in_dim(solved, start, count, 1))
        summed = lax.psum_scatter(tile, "scen", scatter_dimension=0, tiled=True)
        global_cols = own_index * col_count + start + jnp.arange(count, dtype=jnp.int32)
        on_diag = global_rows[:, None] == global_cols[None, :]
        return summed + jnp.where(on_diag, first_diag[:, None], 0.0)

    if col_count >= PW:
        pieces = col_count // PW
        first = lax.rem(panel[0], pieces)
        schur = jnp.zeros((row_span, col_count), jnp.float32)
        panel_rows = None
        for piece in range(pieces):
            start = lax.rem(first + piece, pieces) * PW
            columns = schur_columns(start, PW, solved)
            if piece == 0:
                owns = own_index == panel[0] // pieces
                columns, solved = lax.optimization_barrier((columns, solved))
                panel_rows = lax.psum(jnp.where(owns, columns, 0.0), GROUP)
            schur = lax.dynamic_update_slice_in_dim(schur, columns, start, 1)
    else:
        schur = schur_columns(jnp.int32(0), col_count, solved)
        parts = PW // col_count
        position = own_index - panel[0] * parts
        owns = (position >= 0) & (position < parts)
        placed = jnp.zeros((row_span, PW), jnp.float32)
        placed = lax.dynamic_update_slice_in_dim(
            placed, jnp.where(owns, schur, 0.0), jnp.clip(position, 0, parts - 1) * col_count, 1
        )
        panel_rows = lax.psum(placed, GROUP)
    own_cols = lax.dot_general(
        panel_rows,
        own_inverse,
        (((1,), (1,)), ((), ())),
        precision=lax.Precision.HIGHEST,
        preferred_element_type=jnp.float32,
    )
    return (schur, own_cols)


def newton_inverse(full, eye):
    diag = jnp.where(eye, full, 0.0)
    row_inv = 1.0 / jnp.sum(diag, axis=1, keepdims=True)
    col_inv = 1.0 / jnp.sum(diag, axis=0, keepdims=True)
    first = jnp.where(eye, 0.0, -row_inv * full)
    second = matmul(first, first)
    third = matmul(first, second)
    fourth = matmul(second, second, lax.Precision.DEFAULT)
    head = jnp.where(eye, 1.0, 0.0) + first + second + third
    tail = matmul(head, fourth, lax.Precision.DEFAULT)
    return (head + tail) * col_inv


def lower_inverse_of(symmetric, size):
    count = symmetric.shape[0] // size
    eye = jnp.eye(size, dtype=jnp.float32)
    best = lax.Precision.HIGHEST
    work = [
        [symmetric[i * size : (i + 1) * size, j * size : (j + 1) * size] for j in range(i + 1)]
        for i in range(count)
    ]
    inverse = [[None] * count for _ in range(count)]
    lower = [[None] * count for _ in range(count)]
    for k in range(count):
        factor = lax.linalg.cholesky(work[k][k], symmetrize_input=False)
        inv = lax.linalg.triangular_solve(factor, eye, left_side=True, lower=True)
        inverse[k][k] = inv
        if k + 1 < count:
            below = jnp.concatenate([work[i][k] for i in range(k + 1, count)], 0)
            below = matmul(below, inv.T, best)
            for i in range(k + 1, count):
                lower[i][k] = below[(i - k - 1) * size : (i - k) * size]
            update = matmul(below, below.T, best)
            for i in range(k + 1, count):
                for j in range(k + 1, i + 1):
                    work[i][j] = work[i][j] - update[
                        (i - k - 1) * size : (i - k) * size, (j - k - 1) * size : (j - k) * size
                    ]
    for i in range(1, count):
        left = jnp.concatenate(lower[i][:i], 1)
        right = jnp.concatenate(
            [
                jnp.concatenate(
                    [
                        inverse[r][c] if c <= r else jnp.zeros((size, size), jnp.float32)
                        for c in range(i)
                    ],
                    1,
                )
                for r in range(i)
            ],
            0,
        )
        row = -matmul(inverse[i][i], matmul(left, right, best), best)
        for c in range(i):
            inverse[i][c] = row[:, c * size : (c + 1) * size]
    return jnp.concatenate(
        [
            jnp.concatenate(
                [
                    inverse[r][c] if c <= r else jnp.zeros((size, size), jnp.float32)
                    for c in range(count)
                ],
                1,
            )
            for r in range(count)
        ],
        0,
    )


def over_all(value, route, scen_size, group_size):
    pairs = []
    for s in range(scen_size):
        for g in range(group_size):
            to = route(s, g)
            if to is not None and to != (s, g):
                pairs.append((s * group_size + g, to[0] * group_size + to[1]))
    return lax.ppermute(value, ALL, pairs)


def folded_body(kkt, border, first_diag, assignment, panel):
    s = lax.axis_index("scen")
    g = lax.axis_index(GROUP)
    S = lax.axis_size("scen")
    G = lax.axis_size(GROUP)
    x = lax.rem(s, 2)
    z = s // 2
    y = lax.rem(g, 2)
    core = g // 2
    slots, order, width = border.shape
    half = width // 2
    depth = slots * order
    flip = [(a, a ^ 1) for a in range(S)]
    next_group = [((g0 + 1) % G, g0) for g0 in range(G)]
    across = [(g0, (g0 + 2) % G) for g0 in range(G)]

    flat = border.reshape(depth, width)
    split = flat.reshape(depth, 2, half)

    eye = jnp.eye(order, dtype=jnp.bool_)
    ids = s * slots + jnp.arange(slots, dtype=jnp.int32)
    same = assignment == ids
    pieces = []
    for slot in range(slots):
        own = kkt[slot]
        other = lax.ppermute(own, "scen", flip)
        own = jnp.where(same[slot], own, other)
        other = lax.ppermute(own, "col", [(0, 1), (1, 0)])
        rows = jnp.where(
            y == 0, jnp.concatenate([own, other], 0), jnp.concatenate([other, own], 0)
        )
        other = lax.ppermute(rows, "row", [(0, 1), (1, 0)])
        pieces.append(
            jnp.where(
                core == 0, jnp.concatenate([rows, other], 0), jnp.concatenate([other, rows], 0)
            )
        )
    far = lax.ppermute(flat, GROUP, across)
    step = half // CHUNKS
    nexts = [
        lax.ppermute(split[:, :, c * step : (c + 1) * step], GROUP, next_group)
        for c in range(CHUNKS)
    ]

    solved = jnp.concatenate(
        [matmul(newton_inverse(pieces[slot], eye), border[slot]) for slot in range(slots)], 0
    )

    chosen = panel[0]
    owner = chosen // 2
    owns = g == owner
    start = lax.rem(chosen, 2) * PW
    block = contract(
        lax.dynamic_slice_in_dim(flat, start, PW, 1), lax.dynamic_slice_in_dim(solved, start, PW, 1)
    )
    small_eye = jnp.eye(PW, dtype=jnp.bool_)
    block = block + jnp.where(small_eye & (s == chosen), first_diag[:, None], 0.0)
    block = lax.psum(jnp.where(owns, block, 0.0), ALL)
    lower_inverse = lower_inverse_of(0.5 * (block + block.T), 128)
    share = PW // G
    own_inverse = lax.dynamic_slice_in_dim(lower_inverse, g * share, share, 0)

    def over_x(tile):
        keep = lax.dynamic_index_in_dim(tile, x, 0, keepdims=False)
        give = lax.dynamic_index_in_dim(tile, 1 - x, 0, keepdims=False)
        return keep + lax.ppermute(give, "scen", flip)

    def over_z(value, shift):
        def stand_in(z0, target):
            base = z0 - z0 % 2
            return min(max(target, base), base + 1)

        def first(s0, g0):
            z0, target = s0 // 2, (g0 + shift) % G
            return (stand_in(z0, target) * 2 + s0 % 2, g0)

        def second(s0, g0):
            z0, target = s0 // 2, (g0 + shift) % G
            return (target * 2 + s0 % 2, g0) if stand_in(z0, target) == z0 else None

        value = value + over_all(value, first, S, G)
        return value + over_all(value, second, S, G)

    own_tile = contract(flat, solved).reshape(2, half, width)
    far_split = far.reshape(depth, 2, half)
    near = g < G // 2
    far_tiles = []
    for parity in range(2):
        left = solved[:, parity * half : (parity + 1) * half]
        right = solved[:, (1 - parity) * half : (2 - parity) * half]
        far_tiles.append(contract(far_split[:, parity], jnp.where(near, left, right)))
    tile = over_x(jnp.concatenate([own_tile, jnp.stack(far_tiles)], 2))
    own_rows = over_z(tile[:, :width], 0)
    far_block = over_z(tile[:, width:], 2)
    offset = lax.rem(z - g + G, G)
    diag_ids = x * half + jnp.arange(half, dtype=jnp.int32)
    own_rows = own_rows + jnp.where(
        diag_ids[:, None] == jnp.arange(width, dtype=jnp.int32)[None, :], first_diag[:, None], 0.0
    )

    def far_route(s0, g0):
        z0, x0 = s0 // 2, s0 % 2
        if (z0 - g0) % G != 2:
            return None
        return (2 * g0 + (x0 if g0 < G // 2 else 1 - x0), z0)

    turned = over_all(far_block.T, far_route, S, G)
    held = jnp.where(near, x, 1 - x)
    far_rows = jnp.where(
        held == 0,
        jnp.concatenate([far_block, turned], 1),
        jnp.concatenate([turned, far_block], 1),
    )

    def turn_route(m):
        def route(s0, g0):
            z0, x0 = s0 // 2, s0 % 2
            if (z0 - g0) % G != 1:
                return None
            return (2 * g0 + (x0 ^ m), z0)

        return route

    next_rows, turned_cols = [], []
    for c in range(CHUNKS):
        strip = nexts[c].reshape(depth, 2 * step)
        value = over_z(over_x(contract(strip, solved).reshape(2, step, width)), 1)
        next_rows.append(value)
        cols = value.reshape(step, 2, half)
        got = []
        for m in range(2):
            give = lax.dynamic_index_in_dim(cols, x ^ m, 1, keepdims=False)
            got.append(over_all(give.T, turn_route(m), S, G))
        turned_cols.append(
            (jnp.where(x == 0, got[0], got[1]), jnp.where(x == 0, got[1], got[0]))
        )
    next_rows = jnp.concatenate(next_rows, 0)
    back_rows = jnp.concatenate(
        [turned_cols[c][parity] for parity in range(2) for c in range(CHUNKS)], 1
    )
    schur = jnp.where(
        offset == 0,
        own_rows,
        jnp.where(offset == 1, next_rows, jnp.where(offset == 2, far_rows, back_rows)),
    )
    panel_rows = lax.dynamic_slice_in_dim(schur, start, PW, 1)
    panel_rows = lax.psum(jnp.where(owns, panel_rows, 0.0), GROUP)
    own_cols = lax.dot_general(
        panel_rows,
        own_inverse,
        (((1,), (1,)), ((), ())),
        precision=lax.Precision.HIGHEST,
        preferred_element_type=jnp.float32,
    )
    return (schur, own_cols)


def body(kkt, border, first_diag, assignment, panel):
    groups = lax.axis_size(GROUP)
    foldable = (
        groups == 4
        and lax.axis_size("row") == 2
        and lax.axis_size("scen") == 2 * groups
        and border.shape[2] == 2 * first_diag.shape[0]
        and first_diag.shape[0] == PW
    )
    chosen = folded_body if foldable else plain_body
    return chosen(kkt, border, first_diag, assignment, panel)


def solution(mesh):
    in_specs = (
        P("scen", ("row", "col"), None),
        P("scen", None, ("row", "col")),
        P("scen"),
        P("scen"),
        P(),
    )
    out_specs = (P("scen", ("row", "col")), P("scen", ("row", "col")))
    return jax.shard_map(body, mesh=mesh, in_specs=in_specs, out_specs=out_specs, check_vma=False)
```

```python
import jax
import jax.numpy as jnp
from jax import lax
from jax.experimental import pallas as pl
from jax.experimental.pallas import tpu as pltpu
from jax.sharding import PartitionSpec as P

PW = 512
NEWTON = 3


HIGH = lax.Precision.HIGH
GROUP = ("row", "col")
ALL = ("scen", "row", "col")


def swapped(value, axis, distance):
    mask = 2**distance
    pairs = [(source, source ^ mask) for source in range(lax.axis_size(axis))]
    return lax.ppermute(value, axis, pairs)


def gathered_rows(value, axis):
    count = lax.axis_size(axis)
    index = lax.axis_index(axis)
    rows = value.shape[1]
    whole = jnp.zeros((value.shape[0], rows * count, value.shape[2]), value.dtype)
    whole = lax.dynamic_update_slice_in_dim(whole, value, index * rows, 1)
    for shift in range(1, count):
        pairs = [(source, (source + shift) % count) for source in range(count)]
        origin = lax.rem(index - shift + count, count)
        whole = lax.dynamic_update_slice_in_dim(
            whole, lax.ppermute(value, axis, pairs), origin * rows, 1
        )
    return whole


def matmul(left, right, precision=HIGH):
    return jnp.dot(left, right, precision=precision, preferred_element_type=jnp.float32)


def contract(left, right):
    return lax.dot_general(
        left, right, (((0,), (0,)), ((), ())), precision=HIGH, preferred_element_type=jnp.float32
    )


def plain_body(kkt, border, first_diag, assignment, panel):
    scen_index = lax.axis_index("scen")
    own_index = lax.axis_index(GROUP)
    group_size = lax.axis_size(GROUP)
    slots, order, col_count = border.shape
    width = col_count * group_size
    scenario_ids = scen_index * slots + jnp.arange(slots, dtype=jnp.int32)
    kkt = jnp.where((assignment == scenario_ids)[:, None, None], kkt, swapped(kkt, "scen", 0))
    kkt_all = gathered_rows(gathered_rows(kkt, "col"), "row")
    gathered = lax.all_gather(border, GROUP, axis=2, tiled=True)
    eye = jnp.eye(order, dtype=jnp.bool_)
    inverses = []
    for slot in range(slots):
        full = kkt_all[slot]
        diag = jnp.where(eye, full, 0.0)
        row_inv = 1.0 / jnp.sum(diag, axis=1, keepdims=True)
        col_inv = 1.0 / jnp.sum(diag, axis=0, keepdims=True)
        approx = jnp.where(eye, 2.0 * row_inv, 0.0) - row_inv * full * col_inv
        for step in range(NEWTON - 1):
            approx = 2.0 * approx - matmul(matmul(approx, full), approx)
        inverses.append(approx)
    solved = jnp.concatenate([matmul(inverses[slot], border[slot]) for slot in range(slots)], 0)
    border_all = gathered.reshape(slots * order, width)

    panel_start = panel[0] * PW
    share = PW // group_size
    own_start = panel_start + own_index * share

    share_solved = jnp.concatenate(
        [
            matmul(inverses[slot], lax.dynamic_slice_in_dim(gathered[slot], own_start, share, 1))
            for slot in range(slots)
        ],
        0,
    )
    panel_border = lax.dynamic_slice_in_dim(border_all, panel_start, PW, 1)
    block = contract(panel_border, share_solved)
    row_span = first_diag.shape[0]
    global_rows = scen_index * row_span + jnp.arange(row_span, dtype=jnp.int32)
    share_ids = own_start + jnp.arange(share, dtype=jnp.int32)
    owned = global_rows[:, None] == share_ids[None, :]
    share_diag = jnp.sum(jnp.where(owned, first_diag[:, None], 0.0), axis=0)
    panel_ids = panel_start + jnp.arange(PW, dtype=jnp.int32)
    block = block + jnp.where(panel_ids[:, None] == share_ids[None, :], share_diag[None, :], 0.0)
    block = lax.psum(block, "scen")
    block = lax.all_gather(block, GROUP, axis=1, tiled=True)
    symmetric = 0.5 * (block + block.T)
    lower_factor = jnp.linalg.cholesky(symmetric)
    lower_inverse = lax.linalg.triangular_solve(
        lower_factor, jnp.eye(PW, dtype=jnp.float32), left_side=True, lower=True
    )
    own_inverse = lax.dynamic_slice_in_dim(lower_inverse, own_index * share, share, 0)

    def schur_columns(start, count, solved):
        tile = contract(border_all, lax.dynamic_slice_in_dim(solved, start, count, 1))
        summed = lax.psum_scatter(tile, "scen", scatter_dimension=0, tiled=True)
        global_cols = own_index * col_count + start + jnp.arange(count, dtype=jnp.int32)
        on_diag = global_rows[:, None] == global_cols[None, :]
        return summed + jnp.where(on_diag, first_diag[:, None], 0.0)

    if col_count >= PW:
        pieces = col_count // PW
        first = lax.rem(panel[0], pieces)
        schur = jnp.zeros((row_span, col_count), jnp.float32)
        panel_rows = None
        for piece in range(pieces):
            start = lax.rem(first + piece, pieces) * PW
            columns = schur_columns(start, PW, solved)
            if piece == 0:
                owns = own_index == panel[0] // pieces
                columns, solved = lax.optimization_barrier((columns, solved))
                panel_rows = lax.psum(jnp.where(owns, columns, 0.0), GROUP)
            schur = lax.dynamic_update_slice_in_dim(schur, columns, start, 1)
    else:
        schur = schur_columns(jnp.int32(0), col_count, solved)
        parts = PW // col_count
        position = own_index - panel[0] * parts
        owns = (position >= 0) & (position < parts)
        placed = jnp.zeros((row_span, PW), jnp.float32)
        placed = lax.dynamic_update_slice_in_dim(
            placed, jnp.where(owns, schur, 0.0), jnp.clip(position, 0, parts - 1) * col_count, 1
        )
        panel_rows = lax.psum(placed, GROUP)
    own_cols = lax.dot_general(
        panel_rows,
        own_inverse,
        (((1,), (1,)), ((), ())),
        precision=lax.Precision.HIGHEST,
        preferred_element_type=jnp.float32,
    )
    return (schur, own_cols)


def parts(value):
    high = value.astype(jnp.bfloat16)
    return high, (value - high.astype(jnp.float32)).astype(jnp.bfloat16)


def dot(left, right):
    return jnp.dot(left, right, preferred_element_type=jnp.float32)


def dot_rows(left, right):
    return lax.dot_general(
        left, right, (((0,), (0,)), ((), ())), preferred_element_type=jnp.float32
    )


def head_kernel(
    assignment_ref,
    panel_ref,
    extra_ref,
    kkt_ref,
    border_ref,
    x_ref,
    own_ref,
    block_ref,
    far_ref,
    strip_ref,
    swap,
    full,
    loaded,
    b_hi,
    b_lo,
    e_hi,
    e_lo,
    m_hi,
    m_lo,
    p_hi,
    z_hi,
    z_lo,
    head,
    dealt,
    from_group,
    share,
    from_scen,
    total,
    gathered,
    load_sem,
    swap_sems,
    y_sems,
    core_sems,
    far_sems,
    strip_sems,
    group_sems,
    scen_sems,
    spread_sems,
    whole_sems,
):
    slots, order, _ = full.shape
    rows = kkt_ref.shape[1]
    width = x_ref.shape[1]
    half = width // 2
    groups, panel_width, piece_width = dealt.shape
    step = 256
    s = lax.axis_index("scen")
    core = lax.axis_index("row")
    y = lax.axis_index("col")
    S = lax.axis_size("scen")
    g = core * 2 + y
    flip_x = s + 1 - 2 * lax.rem(s, 2)

    def group_peer(shift):
        to = lax.rem(g + shift, groups)
        return (s, to // 2, lax.rem(to, 2))

    def scen_peer(shift):
        return (lax.rem(s + shift, S), core, y)

    barrier = pltpu.get_barrier_semaphore()
    for shift in range(1, groups):
        pl.semaphore_signal(
            barrier, inc=1, device_id=group_peer(shift), device_id_type=pl.DeviceIdType.MESH
        )
    for shift in range(1, S):
        pl.semaphore_signal(
            barrier, inc=1, device_id=scen_peer(shift), device_id_type=pl.DeviceIdType.MESH
        )
    pl.semaphore_wait(barrier, groups - 1 + S - 1)

    def remote(source, target, sems, index, device):
        return pltpu.make_async_remote_copy(
            src_ref=source,
            dst_ref=target,
            send_sem=sems.at[0, index],
            recv_sem=sems.at[1, index],
            device_id=device,
            device_id_type=pl.DeviceIdType.MESH,
        )

    def swap_copy(slot):
        return remote(kkt_ref.at[slot], swap.at[slot], swap_sems, slot, (flip_x, core, y))

    own_rows = pl.ds(pl.multiple_of(g * rows, 8), rows)
    core_rows = pl.ds(pl.multiple_of(core * (2 * rows), 8), 2 * rows)

    def y_copy(slot):
        place = full.at[slot, own_rows, :]
        return remote(place, place, y_sems, slot, (s, core, 1 - y))

    def core_copy(slot):
        place = full.at[slot, core_rows, :]
        return remote(place, place, core_sems, slot, (s, 1 - core, y))

    def load(slot):
        return pltpu.make_async_copy(
            border_ref.at[pl.ds(slot * order, order), :], loaded, load_sem
        )

    far_copy = remote(border_ref, far_ref, far_sems, 0, (s, 1 - core, y))
    strip_width = strip_ref.shape[1] // 2
    strip_copies = [
        remote(
            border_ref.at[:, pl.ds(p * half, strip_width)],
            strip_ref.at[:, pl.ds(p * strip_width, strip_width)],
            strip_sems,
            p,
            group_peer(groups - 1),
        )
        for p in range(2)
    ]

    for slot in range(slots):
        swap_copy(slot).start()
    load(0).start()

    def select_rows(slot):
        swap_copy(slot).wait_recv()
        same = assignment_ref[slot] == s * slots + slot
        full[slot, own_rows, :] = jnp.where(same, kkt_ref[slot], swap[slot])
        y_copy(slot).start()

    select_rows(0)
    select_rows(1)
    y_copy(0).wait_recv()
    core_copy(0).start()
    for slot in range(2, slots):
        select_rows(slot)
    far_copy.start()
    y_copy(1).wait_recv()
    core_copy(1).start()

    def eye_at(start):
        row = lax.broadcasted_iota(jnp.int32, (step, order), 0) + start
        return row == lax.broadcasted_iota(jnp.int32, (step, order), 1)

    @pl.loop(0, slots)
    def _(slot):
        core_copy(slot).wait_recv()
        col_diag = jnp.zeros((1, order), jnp.float32)
        for start in range(0, order, step):
            spot = pl.ds(start, step)
            block = full[slot, spot, :]
            eye = eye_at(start)
            diag = jnp.where(eye, block, 0.0)
            col_diag = col_diag + jnp.sum(diag, axis=0, keepdims=True)
            scale = 1.0 / jnp.sum(diag, axis=1, keepdims=True)
            scaled = jnp.where(eye, 0.0, -scale * block)
            head[spot, :] = scaled
            high, low = parts(scaled)
            e_hi[spot, :] = high
            e_lo[spot, :] = low
        col_inv = 1.0 / col_diag

        @pl.loop(0, order // step)
        def _(chunk):
            spot = pl.ds(pl.multiple_of(chunk * step, step), step)
            high = e_hi[spot, :]
            value = dot(high, e_hi[...]) + dot(high, e_lo[...]) + dot(e_lo[spot, :], e_hi[...])
            head[spot, :] += value
            high, low = parts(value)
            m_hi[spot, :] = high
            m_lo[spot, :] = low

        @pl.loop(0, order // step)
        def _(chunk):
            start = pl.multiple_of(chunk * step, step)
            spot = pl.ds(start, step)
            high = e_hi[spot, :]
            value = dot(high, m_hi[...]) + dot(high, m_lo[...]) + dot(e_lo[spot, :], m_hi[...])
            head[spot, :] += value + jnp.where(eye_at(start), 1.0, 0.0)
            p_hi[spot, :] = dot(m_hi[spot, :], m_hi[...]).astype(jnp.bfloat16)

        @pl.loop(0, order // step)
        def _(chunk):
            spot = pl.ds(pl.multiple_of(chunk * step, step), step)
            value = head[spot, :]
            value = (value + dot(value.astype(jnp.bfloat16), p_hi[...])) * col_inv
            high, low = parts(value)
            z_hi[spot, :] = high
            z_lo[spot, :] = low

        here = pl.ds(pl.multiple_of(slot * order, step), order)
        load(slot).wait()

        @pl.loop(0, width // step)
        def _(chunk):
            spot = pl.ds(pl.multiple_of(chunk * step, step), step)
            high, low = parts(loaded[:, spot])
            b_hi[here, spot] = high
            b_lo[here, spot] = low
            x_ref[here, spot] = dot(z_hi[...], high) + dot(z_hi[...], low) + dot(z_lo[...], high)

        @pl.when(slot < slots - 1)
        def _():
            load(slot + 1).start()

        @pl.when(slot == 0)
        def _():
            for later in range(2, slots):
                y_copy(later).wait_recv()
                core_copy(later).start()
            for copy in strip_copies:
                copy.start()

    left = lax.rem(panel_ref[0], 2) == 0
    owns = g == panel_ref[0] // 2
    eye = lax.broadcasted_iota(jnp.int32, (step, panel_width), 0)
    col = lax.broadcasted_iota(jnp.int32, (step, panel_width), 1)
    x_panel = jnp.where(left, x_ref[:, :half], x_ref[:, half:])
    x_high, x_low = parts(x_panel)
    for start in range(0, panel_width, step):
        high = jnp.where(left, b_hi[:, start : start + step], b_hi[:, half + start : half + start + step])
        low = jnp.where(left, b_lo[:, start : start + step], b_lo[:, half + start : half + start + step])
        value = dot_rows(high, x_high) + dot_rows(high, x_low) + dot_rows(low, x_high)
        value = value + jnp.where(eye + start == col, extra_ref[...], 0.0)
        value = jnp.where(owns, value, 0.0)
        for part in range(groups):
            dealt[part, start : start + step, :] = value[
                :, part * piece_width : (part + 1) * piece_width
            ]

    def own_tile(tile):
        spot = pl.ds(tile * step, step)
        high, low = b_hi[:, spot], b_lo[:, spot]

        @pl.loop(0, width // step)
        def _(chunk):
            cols = pl.ds(pl.multiple_of(chunk * step, step), step)
            x_high, x_low = parts(x_ref[:, cols])
            own_ref[spot, cols] = (
                dot_rows(high, x_high) + dot_rows(high, x_low) + dot_rows(low, x_high)
            )

    def deal(shift):
        to = lax.rem(g + shift, groups)
        return remote(
            dealt.at[to], from_group.at[shift - 1], group_sems, shift - 1, group_peer(shift)
        )

    for shift in range(1, groups):
        deal(shift).start()
    own_tile(0)
    own_tile(1)
    value = dealt[g]
    for shift in range(1, groups):
        deal(shift).wait_recv()
        value = value + from_group[shift - 1]
    share[...] = value
    part_rows = panel_width // S

    def reduce_copy(shift):
        to = lax.rem(s + shift, S)
        return remote(
            share.at[pl.ds(pl.multiple_of(to * part_rows, 8), part_rows), :],
            from_scen.at[shift - 1],
            scen_sems,
            shift - 1,
            scen_peer(shift),
        )

    for shift in range(1, S):
        reduce_copy(shift).start()
    own_tile(2)
    own_part = pl.ds(pl.multiple_of(s * part_rows, 8), part_rows)
    value = share[own_part, :]
    for shift in range(1, S):
        reduce_copy(shift).wait_recv()
        value = value + from_scen[shift - 1]
    total[own_part, :] = value

    def spread_copy(shift):
        place = total.at[own_part, :]
        return remote(place, place, spread_sems, shift - 1, scen_peer(shift))

    for shift in range(1, S):
        spread_copy(shift).start()
    own_tile(3)
    for shift in range(1, S):
        spread_copy(shift).wait_recv()
    gathered[g] = total[...]

    def whole_copy(shift):
        return remote(
            gathered.at[g], gathered.at[g], whole_sems, shift - 1, group_peer(shift)
        )

    for shift in range(1, groups):
        whole_copy(shift).start()
    for shift in range(1, groups):
        whole_copy(shift).wait_recv()
    for part in range(groups):
        block_ref[:, part * piece_width : (part + 1) * piece_width] = gathered[part]

    for slot in range(slots):
        swap_copy(slot).wait_send()
        y_copy(slot).wait_send()
        core_copy(slot).wait_send()
    for shift in range(1, groups):
        deal(shift).wait_send()
        whole_copy(shift).wait_send()
    for shift in range(1, S):
        reduce_copy(shift).wait_send()
        spread_copy(shift).wait_send()
    far_copy.wait()
    for copy in strip_copies:
        copy.wait()


def head_call(assignment, panel, extra, kkt, flat, strip_width):
    slots, rows, order = kkt.shape
    depth, width = flat.shape
    S = lax.axis_size("scen")
    G = lax.axis_size(GROUP)
    f32, bf16 = jnp.float32, jnp.bfloat16
    vmem = pl.BlockSpec(memory_space=pltpu.VMEM)
    smem = pl.BlockSpec(memory_space=pltpu.SMEM)
    hbm = pl.BlockSpec(memory_space=pl.ANY)
    share = PW // G

    def sems(count):
        return pltpu.SemaphoreType.DMA((2, count))

    return pl.pallas_call(
        head_kernel,
        in_specs=[smem, smem, vmem, vmem, hbm],
        out_specs=[vmem, vmem, vmem, hbm, hbm],
        out_shape=[
            jax.ShapeDtypeStruct((depth, width), f32),
            jax.ShapeDtypeStruct((width, width), f32),
            jax.ShapeDtypeStruct((PW, PW), f32),
            jax.ShapeDtypeStruct((depth, width), f32),
            jax.ShapeDtypeStruct((depth, strip_width), f32),
        ],
        scratch_shapes=[
            pltpu.VMEM((slots, rows, order), f32),
            pltpu.VMEM((slots, order, order), f32),
            pltpu.VMEM((order, width), f32),
            pltpu.VMEM((depth, width), bf16),
            pltpu.VMEM((depth, width), bf16),
        ]
        + [pltpu.VMEM((order, order), bf16)] * 7
        + [
            pltpu.VMEM((order, order), f32),
            pltpu.VMEM((G, PW, share), f32),
            pltpu.VMEM((G - 1, PW, share), f32),
            pltpu.VMEM((PW, share), f32),
            pltpu.VMEM((S - 1, PW // S, share), f32),
            pltpu.VMEM((PW, share), f32),
            pltpu.VMEM((G, PW, share), f32),
            pltpu.SemaphoreType.DMA,
            sems(slots),
            sems(slots),
            sems(slots),
            sems(1),
            sems(2),
            sems(G - 1),
            sems(S - 1),
            sems(S - 1),
            sems(G - 1),
        ],
        compiler_params=pltpu.CompilerParams(
            collective_id=0, has_side_effects=True, vmem_limit_bytes=60 * 1024 * 1024
        ),
        cost_estimate=pl.CostEstimate(
            flops=2 * slots * order * order * (8 * order + 3 * width) + 6 * depth * width * width,
            bytes_accessed=4 * depth * width * 3,
            transcendentals=0,
        ),
    )(assignment, panel, extra, kkt, flat)


def lower_inverse_of(symmetric, size):
    count = symmetric.shape[0] // size
    eye = jnp.eye(size, dtype=jnp.float32)
    best = lax.Precision.HIGHEST
    work = [
        [symmetric[i * size : (i + 1) * size, j * size : (j + 1) * size] for j in range(i + 1)]
        for i in range(count)
    ]
    inverse = [[None] * count for _ in range(count)]
    lower = [[None] * count for _ in range(count)]
    for k in range(count):
        factor = lax.linalg.cholesky(work[k][k], symmetrize_input=False)
        inv = lax.linalg.triangular_solve(factor, eye, left_side=True, lower=True)
        inverse[k][k] = inv
        if k + 1 < count:
            below = jnp.concatenate([work[i][k] for i in range(k + 1, count)], 0)
            below = matmul(below, inv.T, best)
            for i in range(k + 1, count):
                lower[i][k] = below[(i - k - 1) * size : (i - k) * size]
            update = matmul(below, below.T, best)
            for i in range(k + 1, count):
                for j in range(k + 1, i + 1):
                    work[i][j] = work[i][j] - update[
                        (i - k - 1) * size : (i - k) * size, (j - k - 1) * size : (j - k) * size
                    ]
    for i in range(1, count):
        left = jnp.concatenate(lower[i][:i], 1)
        right = jnp.concatenate(
            [
                jnp.concatenate(
                    [
                        inverse[r][c] if c <= r else jnp.zeros((size, size), jnp.float32)
                        for c in range(i)
                    ],
                    1,
                )
                for r in range(i)
            ],
            0,
        )
        row = -matmul(inverse[i][i], matmul(left, right, best), best)
        for c in range(i):
            inverse[i][c] = row[:, c * size : (c + 1) * size]
    return jnp.concatenate(
        [
            jnp.concatenate(
                [
                    inverse[r][c] if c <= r else jnp.zeros((size, size), jnp.float32)
                    for c in range(count)
                ],
                1,
            )
            for r in range(count)
        ],
        0,
    )


def over_all(value, route, scen_size, group_size):
    pairs = []
    for s in range(scen_size):
        for g in range(group_size):
            to = route(s, g)
            if to is not None and to != (s, g):
                pairs.append((s * group_size + g, to[0] * group_size + to[1]))
    return lax.ppermute(value, ALL, pairs)


def folded_body(kkt, border, first_diag, assignment, panel):
    s = lax.axis_index("scen")
    g = lax.axis_index(GROUP)
    S = lax.axis_size("scen")
    G = lax.axis_size(GROUP)
    x = lax.rem(s, 2)
    z = s // 2
    y = lax.rem(g, 2)
    core = g // 2
    slots, order, width = border.shape
    half = width // 2
    depth = slots * order
    flip = [(a, a ^ 1) for a in range(S)]
    next_group = [((g0 + 1) % G, g0) for g0 in range(G)]
    across = [(g0, (g0 + 2) % G) for g0 in range(G)]

    flat = border.reshape(depth, width)

    chosen = panel[0]
    owner = chosen // 2
    owns = g == owner
    start = lax.rem(chosen, 2) * PW
    extra = jnp.where(s == chosen, first_diag, 0.0)[None, :]
    edges = [0, half // 2, 3 * half // 4, half]
    solved, own_tile, block, far, strip = head_call(
        assignment, panel, extra, kkt, flat, 2 * edges[1]
    )
    flat_later, solved, own_tile, block, far, strip = lax.optimization_barrier(
        (flat, solved, own_tile, block, far, strip)
    )
    nexts = [strip]
    for low, high in zip(edges[1:-1], edges[2:]):
        piece = jnp.concatenate([flat_later[:, :half][:, low:high], flat_later[:, half:][:, low:high]], 1)
        nexts.append(lax.ppermute(piece, GROUP, next_group))
    lower_inverse = lower_inverse_of(0.5 * (block + block.T), 128)
    share = PW // G

    def over_x(tile):
        keep = lax.dynamic_index_in_dim(tile, x, 0, keepdims=False)
        give = lax.dynamic_index_in_dim(tile, 1 - x, 0, keepdims=False)
        return keep + lax.ppermute(give, "scen", flip)

    def over_z(value, shift):
        def stand_in(z0, target):
            base = z0 - z0 % 2
            return min(max(target, base), base + 1)

        def first(s0, g0):
            z0, target = s0 // 2, (g0 + shift) % G
            return (stand_in(z0, target) * 2 + s0 % 2, g0)

        def second(s0, g0):
            z0, target = s0 // 2, (g0 + shift) % G
            return (target * 2 + s0 % 2, g0) if stand_in(z0, target) == z0 else None

        value = value + over_all(value, first, S, G)
        return value + over_all(value, second, S, G)

    own_tile = own_tile.reshape(2, half, width)
    near = g < G // 2
    far_tiles = []
    for parity in range(2):
        left = solved[:, parity * half : (parity + 1) * half]
        right = solved[:, (1 - parity) * half : (2 - parity) * half]
        far_tiles.append(contract(far[:, parity * half : (parity + 1) * half], jnp.where(near, left, right)))
    tile = over_x(jnp.concatenate([own_tile, jnp.stack(far_tiles)], 2))
    own_rows = over_z(tile[:, :width], 0)
    far_block = over_z(tile[:, width:], 2)
    offset = lax.rem(z - g + G, G)
    diag_ids = x * half + jnp.arange(half, dtype=jnp.int32)
    own_rows = own_rows + jnp.where(
        diag_ids[:, None] == jnp.arange(width, dtype=jnp.int32)[None, :], first_diag[:, None], 0.0
    )

    def far_route(s0, g0):
        z0, x0 = s0 // 2, s0 % 2
        if (z0 - g0) % G != 2:
            return None
        return (2 * g0 + (x0 if g0 < G // 2 else 1 - x0), z0)

    turned = over_all(far_block.T, far_route, S, G)
    held = jnp.where(near, x, 1 - x)
    far_rows = jnp.where(
        held == 0,
        jnp.concatenate([far_block, turned], 1),
        jnp.concatenate([turned, far_block], 1),
    )

    def turn_route(m):
        def route(s0, g0):
            z0, x0 = s0 // 2, s0 % 2
            if (z0 - g0) % G != 1:
                return None
            return (2 * g0 + (x0 ^ m), z0)

        return route

    next_rows, turned_cols = [], []
    for c, strip in enumerate(nexts):
        step = strip.shape[1] // 2
        value = over_z(over_x(contract(strip, solved).reshape(2, step, width)), 1)
        next_rows.append(value)
        got = []
        for m in range(2):
            give = jnp.where((x ^ m) == 0, value[:, :half], value[:, half:])
            got.append(over_all(give.T, turn_route(m), S, G))
        turned_cols.append(
            (jnp.where(x == 0, got[0], got[1]), jnp.where(x == 0, got[1], got[0]))
        )
    next_rows = jnp.concatenate(next_rows, 0)
    back_rows = jnp.concatenate(
        [turned_cols[c][parity] for parity in range(2) for c in range(len(nexts))], 1
    )
    schur = jnp.where(
        offset == 0,
        own_rows,
        jnp.where(offset == 1, next_rows, jnp.where(offset == 2, far_rows, back_rows)),
    )
    panel_rows = jnp.where(owns, lax.dynamic_slice_in_dim(schur, start, PW, 1), 0.0)
    factor = lax.dot_general(
        panel_rows,
        lower_inverse,
        (((1,), (1,)), ((), ())),
        precision=lax.Precision.HIGHEST,
        preferred_element_type=jnp.float32,
    )
    own_cols = lax.dynamic_slice_in_dim(factor, g * share, share, 1)
    for shift in range(1, G):
        to = lax.rem(g + shift, G)
        give = lax.dynamic_slice_in_dim(factor, to * share, share, 1)
        pairs = [(g0, (g0 + shift) % G) for g0 in range(G)]
        own_cols = own_cols + lax.ppermute(give, GROUP, pairs)
    return (schur, own_cols)


def body(kkt, border, first_diag, assignment, panel):
    groups = lax.axis_size(GROUP)
    foldable = (
        groups == 4
        and lax.axis_size("row") == 2
        and lax.axis_size("scen") == 2 * groups
        and border.shape[2] == 2 * first_diag.shape[0]
        and first_diag.shape[0] == PW
    )
    chosen = folded_body if foldable else plain_body
    return chosen(kkt, border, first_diag, assignment, panel)


def solution(mesh):
    in_specs = (
        P("scen", ("row", "col"), None),
        P("scen", None, ("row", "col")),
        P("scen"),
        P("scen"),
        P(),
    )
    out_specs = (P("scen", ("row", "col")), P("scen", ("row", "col")))
    return jax.shard_map(body, mesh=mesh, in_specs=in_specs, out_specs=out_specs, check_vma=False)
```

```python
import jax
import jax.numpy as jnp
from jax import lax
from jax.experimental import pallas as pl
from jax.experimental.pallas import tpu as pltpu
from jax.sharding import PartitionSpec as P

PW = 512
NEWTON = 3


HIGH = lax.Precision.HIGH
GROUP = ("row", "col")


def swapped(value, axis, distance):
    mask = 2**distance
    pairs = [(source, source ^ mask) for source in range(lax.axis_size(axis))]
    return lax.ppermute(value, axis, pairs)


def gathered_rows(value, axis):
    count = lax.axis_size(axis)
    index = lax.axis_index(axis)
    rows = value.shape[1]
    whole = jnp.zeros((value.shape[0], rows * count, value.shape[2]), value.dtype)
    whole = lax.dynamic_update_slice_in_dim(whole, value, index * rows, 1)
    for shift in range(1, count):
        pairs = [(source, (source + shift) % count) for source in range(count)]
        origin = lax.rem(index - shift + count, count)
        whole = lax.dynamic_update_slice_in_dim(
            whole, lax.ppermute(value, axis, pairs), origin * rows, 1
        )
    return whole


def matmul(left, right, precision=HIGH):
    return jnp.dot(left, right, precision=precision, preferred_element_type=jnp.float32)


def contract(left, right):
    return lax.dot_general(
        left, right, (((0,), (0,)), ((), ())), precision=HIGH, preferred_element_type=jnp.float32
    )


def plain_body(kkt, border, first_diag, assignment, panel):
    scen_index = lax.axis_index("scen")
    own_index = lax.axis_index(GROUP)
    group_size = lax.axis_size(GROUP)
    slots, order, col_count = border.shape
    width = col_count * group_size
    scenario_ids = scen_index * slots + jnp.arange(slots, dtype=jnp.int32)
    kkt = jnp.where((assignment == scenario_ids)[:, None, None], kkt, swapped(kkt, "scen", 0))
    kkt_all = gathered_rows(gathered_rows(kkt, "col"), "row")
    gathered = lax.all_gather(border, GROUP, axis=2, tiled=True)
    eye = jnp.eye(order, dtype=jnp.bool_)
    inverses = []
    for slot in range(slots):
        full = kkt_all[slot]
        diag = jnp.where(eye, full, 0.0)
        row_inv = 1.0 / jnp.sum(diag, axis=1, keepdims=True)
        col_inv = 1.0 / jnp.sum(diag, axis=0, keepdims=True)
        approx = jnp.where(eye, 2.0 * row_inv, 0.0) - row_inv * full * col_inv
        for step in range(NEWTON - 1):
            approx = 2.0 * approx - matmul(matmul(approx, full), approx)
        inverses.append(approx)
    solved = jnp.concatenate([matmul(inverses[slot], border[slot]) for slot in range(slots)], 0)
    border_all = gathered.reshape(slots * order, width)

    panel_start = panel[0] * PW
    share = PW // group_size
    own_start = panel_start + own_index * share

    share_solved = jnp.concatenate(
        [
            matmul(inverses[slot], lax.dynamic_slice_in_dim(gathered[slot], own_start, share, 1))
            for slot in range(slots)
        ],
        0,
    )
    panel_border = lax.dynamic_slice_in_dim(border_all, panel_start, PW, 1)
    block = contract(panel_border, share_solved)
    row_span = first_diag.shape[0]
    global_rows = scen_index * row_span + jnp.arange(row_span, dtype=jnp.int32)
    share_ids = own_start + jnp.arange(share, dtype=jnp.int32)
    owned = global_rows[:, None] == share_ids[None, :]
    share_diag = jnp.sum(jnp.where(owned, first_diag[:, None], 0.0), axis=0)
    panel_ids = panel_start + jnp.arange(PW, dtype=jnp.int32)
    block = block + jnp.where(panel_ids[:, None] == share_ids[None, :], share_diag[None, :], 0.0)
    block = lax.psum(block, "scen")
    block = lax.all_gather(block, GROUP, axis=1, tiled=True)
    symmetric = 0.5 * (block + block.T)
    lower_factor = jnp.linalg.cholesky(symmetric)
    lower_inverse = lax.linalg.triangular_solve(
        lower_factor, jnp.eye(PW, dtype=jnp.float32), left_side=True, lower=True
    )
    own_inverse = lax.dynamic_slice_in_dim(lower_inverse, own_index * share, share, 0)

    def schur_columns(start, count, solved):
        tile = contract(border_all, lax.dynamic_slice_in_dim(solved, start, count, 1))
        summed = lax.psum_scatter(tile, "scen", scatter_dimension=0, tiled=True)
        global_cols = own_index * col_count + start + jnp.arange(count, dtype=jnp.int32)
        on_diag = global_rows[:, None] == global_cols[None, :]
        return summed + jnp.where(on_diag, first_diag[:, None], 0.0)

    if col_count >= PW:
        pieces = col_count // PW
        first = lax.rem(panel[0], pieces)
        schur = jnp.zeros((row_span, col_count), jnp.float32)
        panel_rows = None
        for piece in range(pieces):
            start = lax.rem(first + piece, pieces) * PW
            columns = schur_columns(start, PW, solved)
            if piece == 0:
                owns = own_index == panel[0] // pieces
                columns, solved = lax.optimization_barrier((columns, solved))
                panel_rows = lax.psum(jnp.where(owns, columns, 0.0), GROUP)
            schur = lax.dynamic_update_slice_in_dim(schur, columns, start, 1)
    else:
        schur = schur_columns(jnp.int32(0), col_count, solved)
        parts = PW // col_count
        position = own_index - panel[0] * parts
        owns = (position >= 0) & (position < parts)
        placed = jnp.zeros((row_span, PW), jnp.float32)
        placed = lax.dynamic_update_slice_in_dim(
            placed, jnp.where(owns, schur, 0.0), jnp.clip(position, 0, parts - 1) * col_count, 1
        )
        panel_rows = lax.psum(placed, GROUP)
    own_cols = lax.dot_general(
        panel_rows,
        own_inverse,
        (((1,), (1,)), ((), ())),
        precision=lax.Precision.HIGHEST,
        preferred_element_type=jnp.float32,
    )
    return (schur, own_cols)


def parts(value):
    high = value.astype(jnp.bfloat16)
    return high, (value - high.astype(jnp.float32)).astype(jnp.bfloat16)


def dot(left, right):
    return jnp.dot(left, right, preferred_element_type=jnp.float32)


def dot_rows(left, right):
    return lax.dot_general(
        left, right, (((0,), (0,)), ((), ())), preferred_element_type=jnp.float32
    )


def head_kernel(
    assignment_ref,
    panel_ref,
    extra_ref,
    kkt_ref,
    border_ref,
    x_hi,
    x_lo,
    own_ref,
    block_ref,
    far_ref,
    strip_ref,
    own_tiles,
    swap,
    full,
    loaded,
    b_hi,
    b_lo,
    e_hi,
    e_lo,
    m_hi,
    m_lo,
    p_hi,
    z_hi,
    z_lo,
    head,
    dealt,
    from_group,
    share,
    from_scen,
    total,
    gathered,
    load_sem,
    own_sems,
    swap_sems,
    y_sems,
    core_sems,
    far_sems,
    strip_sems,
    group_sems,
    scen_sems,
    spread_sems,
    whole_sems,
):
    slots, order, _ = full.shape
    rows = kkt_ref.shape[1]
    width = x_hi.shape[1]
    half = width // 2
    groups, panel_width, piece_width = dealt.shape
    step = 256
    s = lax.axis_index("scen")
    core = lax.axis_index("row")
    y = lax.axis_index("col")
    S = lax.axis_size("scen")
    g = core * 2 + y
    flip_x = s + 1 - 2 * lax.rem(s, 2)

    def group_peer(shift):
        to = lax.rem(g + shift, groups)
        return (s, to // 2, lax.rem(to, 2))

    def scen_peer(shift):
        return (lax.rem(s + shift, S), core, y)

    barrier = pltpu.get_barrier_semaphore()
    for shift in range(1, groups):
        pl.semaphore_signal(
            barrier, inc=1, device_id=group_peer(shift), device_id_type=pl.DeviceIdType.MESH
        )
    for shift in range(1, S):
        pl.semaphore_signal(
            barrier, inc=1, device_id=scen_peer(shift), device_id_type=pl.DeviceIdType.MESH
        )
    pl.semaphore_wait(barrier, groups - 1 + S - 1)

    def remote(source, target, sems, index, device):
        return pltpu.make_async_remote_copy(
            src_ref=source,
            dst_ref=target,
            send_sem=sems.at[0, index],
            recv_sem=sems.at[1, index],
            device_id=device,
            device_id_type=pl.DeviceIdType.MESH,
        )

    def swap_copy(slot):
        return remote(kkt_ref.at[slot], swap.at[slot], swap_sems, slot, (flip_x, core, y))

    own_rows = pl.ds(pl.multiple_of(g * rows, 8), rows)
    core_rows = pl.ds(pl.multiple_of(core * (2 * rows), 8), 2 * rows)

    def y_copy(slot):
        place = full.at[slot, own_rows, :]
        return remote(place, place, y_sems, slot, (s, core, 1 - y))

    def core_copy(slot):
        place = full.at[slot, core_rows, :]
        return remote(place, place, core_sems, slot, (s, 1 - core, y))

    def load(slot):
        return pltpu.make_async_copy(
            border_ref.at[pl.ds(slot * order, order), :], loaded, load_sem
        )

    far_copy = remote(border_ref, far_ref, far_sems, 0, (s, 1 - core, y))
    strip_width = strip_ref.shape[1] // 2
    strip_copies = [
        remote(
            border_ref.at[:, pl.ds(p * half, strip_width)],
            strip_ref.at[:, pl.ds(p * strip_width, strip_width)],
            strip_sems,
            p,
            group_peer(groups - 1),
        )
        for p in range(2)
    ]

    for slot in range(slots):
        swap_copy(slot).start()
    load(0).start()

    def select_rows(slot):
        swap_copy(slot).wait_recv()
        same = assignment_ref[slot] == s * slots + slot
        full[slot, own_rows, :] = jnp.where(same, kkt_ref[slot], swap[slot])
        y_copy(slot).start()

    select_rows(0)
    select_rows(1)
    y_copy(0).wait_recv()
    core_copy(0).start()
    for slot in range(2, slots):
        select_rows(slot)
    far_copy.start()
    y_copy(1).wait_recv()
    core_copy(1).start()

    def eye_at(start):
        row = lax.broadcasted_iota(jnp.int32, (step, order), 0) + start
        return row == lax.broadcasted_iota(jnp.int32, (step, order), 1)

    @pl.loop(0, slots)
    def _(slot):
        core_copy(slot).wait_recv()
        col_diag = jnp.zeros((1, order), jnp.float32)
        for start in range(0, order, step):
            spot = pl.ds(start, step)
            block = full[slot, spot, :]
            eye = eye_at(start)
            diag = jnp.where(eye, block, 0.0)
            col_diag = col_diag + jnp.sum(diag, axis=0, keepdims=True)
            scale = 1.0 / jnp.sum(diag, axis=1, keepdims=True)
            scaled = jnp.where(eye, 0.0, -scale * block)
            head[spot, :] = scaled
            high, low = parts(scaled)
            e_hi[spot, :] = high
            e_lo[spot, :] = low
        col_inv = 1.0 / col_diag

        @pl.loop(0, order // step)
        def _(chunk):
            spot = pl.ds(pl.multiple_of(chunk * step, step), step)
            high = e_hi[spot, :]
            value = dot(high, e_hi[...]) + dot(high, e_lo[...]) + dot(e_lo[spot, :], e_hi[...])
            head[spot, :] += value
            high, low = parts(value)
            m_hi[spot, :] = high
            m_lo[spot, :] = low

        @pl.loop(0, order // step)
        def _(chunk):
            start = pl.multiple_of(chunk * step, step)
            spot = pl.ds(start, step)
            high = e_hi[spot, :]
            value = dot(high, m_hi[...]) + dot(high, m_lo[...]) + dot(e_lo[spot, :], m_hi[...])
            head[spot, :] += value + jnp.where(eye_at(start), 1.0, 0.0)
            p_hi[spot, :] = dot(m_hi[spot, :], m_hi[...]).astype(jnp.bfloat16)

        @pl.loop(0, order // step)
        def _(chunk):
            spot = pl.ds(pl.multiple_of(chunk * step, step), step)
            value = head[spot, :]
            value = (value + dot(value.astype(jnp.bfloat16), p_hi[...])) * col_inv
            high, low = parts(value)
            z_hi[spot, :] = high
            z_lo[spot, :] = low

        here = pl.ds(pl.multiple_of(slot * order, step), order)
        load(slot).wait()

        @pl.loop(0, width // step)
        def _(chunk):
            spot = pl.ds(pl.multiple_of(chunk * step, step), step)
            high, low = parts(loaded[:, spot])
            b_hi[here, spot] = high
            b_lo[here, spot] = low
            high, low = parts(dot(z_hi[...], high) + dot(z_hi[...], low) + dot(z_lo[...], high))
            x_hi[here, spot] = high
            x_lo[here, spot] = low

        @pl.when(slot < slots - 1)
        def _():
            load(slot + 1).start()

        @pl.when(slot == 0)
        def _():
            for later in range(2, slots):
                y_copy(later).wait_recv()
                core_copy(later).start()
            for copy in strip_copies:
                copy.start()

    left = lax.rem(panel_ref[0], 2) == 0
    owns = g == panel_ref[0] // 2
    eye = lax.broadcasted_iota(jnp.int32, (step, panel_width), 0)
    col = lax.broadcasted_iota(jnp.int32, (step, panel_width), 1)
    x_high = jnp.where(left, x_hi[:, :half], x_hi[:, half:])
    x_low = jnp.where(left, x_lo[:, :half], x_lo[:, half:])
    for start in range(0, panel_width, step):
        high = jnp.where(left, b_hi[:, start : start + step], b_hi[:, half + start : half + start + step])
        low = jnp.where(left, b_lo[:, start : start + step], b_lo[:, half + start : half + start + step])
        value = dot_rows(high, x_high) + dot_rows(high, x_low) + dot_rows(low, x_high)
        value = value + jnp.where(eye + start == col, extra_ref[...], 0.0)
        value = jnp.where(owns, value, 0.0)
        for part in range(groups):
            dealt[part, start : start + step, :] = value[
                :, part * piece_width : (part + 1) * piece_width
            ]

    x = lax.rem(s, 2)

    def own_tile(parity, tile):
        spot = pl.ds(pl.multiple_of(parity * half + tile * step, step), step)
        high, low = b_hi[:, spot], b_lo[:, spot]
        to = pl.ds(tile * step, step)

        @pl.loop(0, width // step)
        def _(chunk):
            cols = pl.ds(pl.multiple_of(chunk * step, step), step)
            x_high, x_low = x_hi[:, cols], x_lo[:, cols]
            own_tiles[parity, to, cols] = (
                dot_rows(high, x_high) + dot_rows(high, x_low) + dot_rows(low, x_high)
            )

    own_copy = remote(own_tiles.at[1 - x], own_ref, own_sems, 0, (flip_x, core, y))

    def deal(shift):
        to = lax.rem(g + shift, groups)
        return remote(
            dealt.at[to], from_group.at[shift - 1], group_sems, shift - 1, group_peer(shift)
        )

    for shift in range(1, groups):
        deal(shift).start()
    own_tile(1 - x, 0)
    own_tile(1 - x, 1)
    own_copy.start()
    value = dealt[g]
    for shift in range(1, groups):
        deal(shift).wait_recv()
        value = value + from_group[shift - 1]
    share[...] = value
    part_rows = panel_width // S

    def reduce_copy(shift):
        to = lax.rem(s + shift, S)
        return remote(
            share.at[pl.ds(pl.multiple_of(to * part_rows, 8), part_rows), :],
            from_scen.at[shift - 1],
            scen_sems,
            shift - 1,
            scen_peer(shift),
        )

    for shift in range(1, S):
        reduce_copy(shift).start()
    own_tile(x, 0)
    own_part = pl.ds(pl.multiple_of(s * part_rows, 8), part_rows)
    value = share[own_part, :]
    for shift in range(1, S):
        reduce_copy(shift).wait_recv()
        value = value + from_scen[shift - 1]
    total[own_part, :] = value

    def spread_copy(shift):
        place = total.at[own_part, :]
        return remote(place, place, spread_sems, shift - 1, scen_peer(shift))

    for shift in range(1, S):
        spread_copy(shift).start()
    own_tile(x, 1)
    for shift in range(1, S):
        spread_copy(shift).wait_recv()
    gathered[g] = total[...]

    def whole_copy(shift):
        return remote(
            gathered.at[g], gathered.at[g], whole_sems, shift - 1, group_peer(shift)
        )

    for shift in range(1, groups):
        whole_copy(shift).start()
    for shift in range(1, groups):
        whole_copy(shift).wait_recv()
    for part in range(groups):
        block_ref[:, part * piece_width : (part + 1) * piece_width] = gathered[part]

    own_copy.wait()
    own_ref[...] += own_tiles[x]
    for slot in range(slots):
        swap_copy(slot).wait_send()
        y_copy(slot).wait_send()
        core_copy(slot).wait_send()
    for shift in range(1, groups):
        deal(shift).wait_send()
        whole_copy(shift).wait_send()
    for shift in range(1, S):
        reduce_copy(shift).wait_send()
        spread_copy(shift).wait_send()
    far_copy.wait()
    for copy in strip_copies:
        copy.wait()


def head_call(assignment, panel, extra, kkt, flat, strip_width):
    slots, rows, order = kkt.shape
    depth, width = flat.shape
    S = lax.axis_size("scen")
    G = lax.axis_size(GROUP)
    f32, bf16 = jnp.float32, jnp.bfloat16
    vmem = pl.BlockSpec(memory_space=pltpu.VMEM)
    smem = pl.BlockSpec(memory_space=pltpu.SMEM)
    hbm = pl.BlockSpec(memory_space=pl.ANY)
    share = PW // G

    def sems(count):
        return pltpu.SemaphoreType.DMA((2, count))

    return pl.pallas_call(
        head_kernel,
        in_specs=[smem, smem, vmem, vmem, hbm],
        out_specs=[vmem, vmem, vmem, vmem, hbm, hbm],
        out_shape=[
            jax.ShapeDtypeStruct((depth, width), bf16),
            jax.ShapeDtypeStruct((depth, width), bf16),
            jax.ShapeDtypeStruct((PW, width), f32),
            jax.ShapeDtypeStruct((PW, PW), f32),
            jax.ShapeDtypeStruct((depth, width), f32),
            jax.ShapeDtypeStruct((depth, strip_width), f32),
        ],
        scratch_shapes=[
            pltpu.VMEM((2, PW, width), f32),
            pltpu.VMEM((slots, rows, order), f32),
            pltpu.VMEM((slots, order, order), f32),
            pltpu.VMEM((order, width), f32),
            pltpu.VMEM((depth, width), bf16),
            pltpu.VMEM((depth, width), bf16),
        ]
        + [pltpu.VMEM((order, order), bf16)] * 7
        + [
            pltpu.VMEM((order, order), f32),
            pltpu.VMEM((G, PW, share), f32),
            pltpu.VMEM((G - 1, PW, share), f32),
            pltpu.VMEM((PW, share), f32),
            pltpu.VMEM((S - 1, PW // S, share), f32),
            pltpu.VMEM((PW, share), f32),
            pltpu.VMEM((G, PW, share), f32),
            pltpu.SemaphoreType.DMA,
            sems(1),
            sems(slots),
            sems(slots),
            sems(slots),
            sems(1),
            sems(2),
            sems(G - 1),
            sems(S - 1),
            sems(S - 1),
            sems(G - 1),
        ],
        compiler_params=pltpu.CompilerParams(
            collective_id=0, has_side_effects=True, vmem_limit_bytes=60 * 1024 * 1024
        ),
        cost_estimate=pl.CostEstimate(
            flops=2 * slots * order * order * (8 * order + 3 * width) + 6 * depth * width * width,
            bytes_accessed=4 * depth * width * 3,
            transcendentals=0,
        ),
    )(assignment, panel, extra, kkt, flat)


def factor_block(s_ref, w_ref):
    size = s_ref.shape[0]
    pivots = 4
    row = lax.broadcasted_iota(jnp.int32, (size, size), 0)
    lane = lax.broadcasted_iota(jnp.int32, (size, size), 1)
    thin = lax.broadcasted_iota(jnp.int32, (1, size), 1)
    tall = lax.broadcasted_iota(jnp.int32, (size, 1), 0)
    w_ref[...] = jnp.where(row == lane, 1.0, 0.0)

    @pl.loop(0, size // pivots)
    def _(block):
        j = block * pivots
        whole = s_ref[...]
        rows = [s_ref[pl.ds(j + p, 1), :] for p in range(pivots)]
        tails = [w_ref[pl.ds(j + p, 1), :] for p in range(pivots)]
        cols = [
            jnp.sum(jnp.where(lane == j + p, whole, 0.0), axis=1, keepdims=True)
            for p in range(pivots)
        ]
        small = [
            [
                jnp.sum(jnp.where(thin == j + q, rows[p], 0.0), axis=1, keepdims=True)
                for q in range(p, pivots)
            ]
            for p in range(pivots)
        ]
        entry = lambda q, p: small[p][q - p]
        lower = {}
        tails_new, rows_new, cols_new = [], [], []
        for p in range(pivots):
            value = entry(p, p)
            for q in range(p):
                value = value - lower[p, q] * lower[p, q]
            root = lax.rsqrt(value)
            root = root * (1.5 - 0.5 * value * root * root)
            for i in range(p + 1, pivots):
                below = entry(i, p)
                for q in range(p):
                    below = below - lower[i, q] * lower[p, q]
                lower[i, p] = below * root
            u, c, v = rows[p], cols[p], tails[p]
            for q in range(p):
                u = u - lower[p, q] * rows_new[q]
                c = c - lower[p, q] * cols_new[q]
                v = v - lower[p, q] * tails_new[q]
            rows_new.append(u * root)
            cols_new.append(c * root)
            tails_new.append(v * root)
        change = jnp.zeros((size, size), jnp.float32)
        other = jnp.zeros((size, size), jnp.float32)
        for p in range(pivots):
            c = jnp.where(tall >= j + pivots, cols_new[p], 0.0)
            change = change + c * rows_new[p]
            other = other + c * tails_new[p]
        s_ref[...] = whole - change
        w_ref[...] = w_ref[...] - other
        for p in range(pivots):
            w_ref[pl.ds(j + p, 1), :] = tails_new[p]


def exact(left, right, axes=((1,), (0,))):
    return lax.dot_general(
        left,
        right,
        (axes, ((), ())),
        precision=lax.Precision.HIGHEST,
        preferred_element_type=jnp.float32,
    )


def tail_kernel(
    panel_ref,
    diag_ref,
    x_hi,
    x_lo,
    own_in,
    block_ref,
    border_ref,
    far_ref,
    early_ref,
    out_ref,
    factor_ref,
    late_ref,
    stage,
    lt_hi,
    lt_lo,
    far_tile,
    from_x_far,
    far_turned,
    cross,
    from_x,
    turned,
    own_acc,
    own_z,
    far_z,
    cross_z,
    work,
    inverse,
    s_ref,
    w_ref,
    dealt,
    from_group,
    stage_sems,
    late_sems,
    far_x_sems,
    x_sems,
    own_z_sems,
    far_z_sems,
    cross_z_sems,
    turn_send,
    turn_recv,
    far_turn_sems,
    deal_sems,
):
    depth, width = x_hi.shape
    half = width // 2
    groups = dealt.shape[0]
    strips = cross.shape[0]
    thick = cross.shape[1] // 2
    early = early_ref.shape[1] // (2 * thick)
    step = 256
    s = lax.axis_index("scen")
    core = lax.axis_index("row")
    y = lax.axis_index("col")
    S = lax.axis_size("scen")
    g = core * 2 + y
    x = lax.rem(s, 2)
    z = s // 2
    flip_x = s + 1 - 2 * x
    MESH = pl.DeviceIdType.MESH

    def group_peer(shift):
        to = lax.rem(g + shift, groups)
        return (s, to // 2, lax.rem(to, 2))

    def mirror(parity):
        return (2 * g + parity, z // 2, lax.rem(z, 2))

    barrier = pltpu.get_barrier_semaphore()
    for shift in range(1, groups):
        pl.semaphore_signal(barrier, inc=1, device_id=group_peer(shift), device_id_type=MESH)
    for shift in range(1, S):
        pl.semaphore_signal(
            barrier, inc=1, device_id=(lax.rem(s + shift, S), core, y), device_id_type=MESH
        )

    @pl.when(z != g)
    def _():
        for parity in range(2):
            pl.semaphore_signal(barrier, inc=1, device_id=mirror(parity), device_id_type=MESH)
        pl.semaphore_wait(barrier, groups + S)

    @pl.when(z == g)
    def _():
        pl.semaphore_wait(barrier, groups + S - 2)

    def remote(source, target, send, recv, device):
        return pltpu.make_async_remote_copy(
            src_ref=source,
            dst_ref=target,
            send_sem=send,
            recv_sem=recv,
            device_id=device,
            device_id_type=MESH,
        )

    class Plane:
        def __init__(self, value, first, second, sems, base, shift):
            self.value, self.first, self.second = value, first, second
            self.target = lax.rem(g + shift, groups)
            low = z - lax.rem(z, 2)
            self.keeper = jnp.minimum(jnp.maximum(self.target, low), low + 1)
            self.one = remote(
                value, first, sems.at[base], sems.at[base + 1], (self.keeper * 2 + x, core, y)
            )
            self.two = remote(
                value, second, sems.at[base + 2], sems.at[base + 3], (self.target * 2 + x, core, y)
            )

        def send(self):
            @pl.when(z != self.keeper)
            def _():
                self.one.start()

        def pass_on(self):
            @pl.when(z == self.keeper)
            def _():
                self.one.wait_recv()
                self.value[...] += self.first[...]

                @pl.when(z != self.target)
                def _():
                    self.two.start()

        def take(self):
            self.two.wait_recv()
            self.value[...] += self.second[...]

        def finish(self):
            @pl.when(z != self.keeper)
            def _():
                self.one.wait_send()

            @pl.when((z == self.keeper) & (z != self.target))
            def _():
                self.two.wait_send()

    def late_copy(strip, parity):
        return remote(
            border_ref.at[:, pl.ds(parity * half + strip * thick, thick)],
            late_ref.at[:, pl.ds(((strip - early) * 2 + parity) * thick, thick)],
            late_sems.at[0, strip - early, parity],
            late_sems.at[1, strip - early, parity],
            group_peer(groups - 1),
        )

    own = Plane(own_acc, own_z.at[0], own_z.at[1], own_z_sems, 0, 0)
    own_acc[...] = own_in[...]
    own.send()
    for parity in range(2):
        late_copy(early, parity).start()

    def stage_load(slot, source, start, count, part):
        return pltpu.make_async_copy(
            source.at[:, pl.ds(start, count)],
            stage.at[slot, :, pl.ds(part * count, count)],
            stage_sems.at[slot, part],
        )

    def strip_load(slot, strip, part):
        if strip < early:
            return stage_load(slot, early_ref, part * early * thick + strip * thick, thick, part)
        return stage_load(slot, late_ref, ((strip - early) * 2 + part) * thick, thick, part)

    def far_load(slot, parity, tile):
        return stage_load(
            slot, far_ref, pl.multiple_of(parity * half + tile * step, step), step, 0
        )

    def product(slot, target, base, count):
        @pl.loop(0, depth // step)
        def _(chunk):
            spot = pl.ds(pl.multiple_of(chunk * step, step), step)
            high, low = parts(stage[slot, spot, :].T)
            lt_hi[:, spot] = high
            lt_lo[:, spot] = low

        @pl.loop(0, count // step)
        def _(chunk):
            start = pl.multiple_of(chunk * step, step)
            cols = pl.ds(pl.multiple_of(base + start, step), step)
            high, low = x_hi[:, cols], x_lo[:, cols]
            target[:, pl.ds(start, step)] = (
                dot(lt_hi[...], high) + dot(lt_hi[...], low) + dot(lt_lo[...], high)
            )

    near = g < groups // 2

    def far_side(parity):
        return jnp.where(near, parity, 1 - parity)

    def far_product(slot, parity, tile):
        product(
            slot, far_tile.at[parity, pl.ds(tile * step, step), :], far_side(parity) * half, half
        )

    far_x = remote(
        far_tile.at[1 - x], from_x_far, far_x_sems.at[0], far_x_sems.at[1], (flip_x, core, y)
    )
    loads = [
        [far_load(0, 1 - x, 0)],
        [far_load(1, 1 - x, 1)],
        [far_load(0, x, 0)],
        [far_load(1, x, 1)],
    ]
    for strip in range(early):
        loads.append([strip_load(strip % 2, strip, part) for part in range(2)])

    def begin(index):
        for copy in loads[index]:
            copy.start()

    def ready(index):
        for copy in loads[index]:
            copy.wait()
        if index + 1 < len(loads):
            begin(index + 1)

    def kept(strip):
        return cross.at[strip, pl.ds(pl.multiple_of(x * thick, 8), thick), :]

    def cross_x(strip):
        return remote(
            cross.at[strip, pl.ds(pl.multiple_of((1 - x) * thick, 8), thick), :],
            from_x.at[strip],
            x_sems.at[0, strip],
            x_sems.at[1, strip],
            (flip_x, core, y),
        )

    planes = [
        Plane(kept(i), cross_z.at[i, 0], cross_z.at[i, 1], cross_z_sems, 4 * i, 1)
        for i in range(strips)
    ]
    far = Plane(far_tile.at[x], far_z.at[0], far_z.at[1], far_z_sems, 0, 2)

    def join_x(strip):
        cross_x(strip).wait_recv()
        kept(strip)[...] += from_x[strip]
        planes[strip].send()

    def turn(strip, parity):
        place = out_ref.at[:, pl.ds(pl.multiple_of(x * half + strip * thick, thick), thick)]
        return remote(
            turned.at[strip, parity],
            place,
            turn_send.at[strip, parity],
            turn_recv.at[strip, x],
            mirror(parity),
        )

    offset = lax.rem(z - g + groups, groups)

    def settle(strip):
        @pl.when(offset == 1)
        def _():
            planes[strip].take()
            value = kept(strip)[...]
            out_ref[pl.ds(strip * thick, thick), :] = value
            for parity in range(2):
                turned[strip, parity] = value[:, parity * half : (parity + 1) * half].T
                turn(strip, parity).start()

    mine = far_side(x)
    far_turn = remote(
        far_turned,
        out_ref.at[:, pl.ds(pl.multiple_of(x * half, half), half)],
        far_turn_sems.at[0],
        far_turn_sems.at[1],
        (2 * g + mine, z // 2, lax.rem(z, 2)),
    )

    size = s_ref.shape[0]
    count = work.shape[0] // size

    def spot(index):
        return slice(index * size, (index + 1) * size)

    def eliminate(k):
        s_ref[...] = work[spot(k), spot(k)]
        factor_block(s_ref, w_ref)
        inverse[spot(k), spot(k)] = w_ref[...]
        if k + 1 < count:
            rest = slice((k + 1) * size, count * size)
            below = exact(work[rest, spot(k)], w_ref[...], ((1,), (1,)))
            work[rest, spot(k)] = below
            work[rest, rest] = work[rest, rest] - exact(below, below, ((1,), (1,)))
        if k > 0:
            known = slice(0, k * size)
            row = exact(work[spot(k), known], inverse[known, known])
            inverse[spot(k), known] = -exact(w_ref[...], row)

    begin(0)
    work[...] = 0.5 * (block_ref[...] + block_ref[...].T)
    inverse[...] = jnp.zeros(inverse.shape, jnp.float32)
    for tile in range(2):
        ready(tile)
        far_product(tile, 1 - x, tile)
    far_x.start()
    for tile in range(2):
        ready(2 + tile)
        far_product(tile, x, tile)
    for strip in range(early):
        ready(4 + strip)
        product(strip % 2, cross.at[strip], 0, width)
        cross_x(strip).start()
    own.pass_on()
    eliminate(0)
    far_x.wait_recv()
    far_tile[x] += from_x_far[...]
    far.send()
    for strip in range(early + 1, strips):
        for parity in range(2):
            late_copy(strip, parity).start()
    for strip in range(early):
        join_x(strip)
    eliminate(1)

    @pl.when(offset == 0)
    def _():
        own.take()
        row = lax.broadcasted_iota(jnp.int32, (half, width), 0) + x * half
        col = lax.broadcasted_iota(jnp.int32, (half, width), 1)
        out_ref[...] = own_acc[...] + jnp.where(row == col, diag_ref[...].T, 0.0)

    far.pass_on()
    for strip in range(early):
        planes[strip].pass_on()
    eliminate(2)

    @pl.when(offset == 2)
    def _():
        far.take()
        value = far_tile[x]
        out_ref[:, pl.ds(pl.multiple_of(mine * half, half), half)] = value
        far_turned[...] = value.T
        far_turn.start()

    for strip in range(early):
        settle(strip)
    eliminate(3)
    for strip in range(early, strips):
        for parity in range(2):
            late_copy(strip, parity).wait_recv()
        for part in range(2):
            strip_load(strip % 2, strip, part).start()
        for part in range(2):
            strip_load(strip % 2, strip, part).wait()
        product(strip % 2, cross.at[strip], 0, width)
        cross_x(strip).start()
    for strip in range(early, strips):
        join_x(strip)
    for strip in range(early, strips):
        planes[strip].pass_on()
    for strip in range(early, strips):
        settle(strip)

    @pl.when(offset == 2)
    def _():
        remote(
            far_turned,
            out_ref.at[:, pl.ds(pl.multiple_of((1 - mine) * half, half), half)],
            far_turn_sems.at[0],
            far_turn_sems.at[1],
            mirror(0),
        ).wait_recv()
        far_turn.wait_send()

    @pl.when(offset == 3)
    def _():
        for strip in range(strips):
            for source in range(2):
                remote(
                    turned.at[strip, 0],
                    out_ref.at[:, pl.ds(source * half + strip * thick, thick)],
                    turn_send.at[strip, 0],
                    turn_recv.at[strip, source],
                    mirror(0),
                ).wait_recv()

    @pl.when(offset == 1)
    def _():
        for strip in range(strips):
            for parity in range(2):
                turn(strip, parity).wait_send()

    left = lax.rem(panel_ref[0], 2) == 0
    owner = panel_ref[0] // 2
    piece = dealt.shape[2]
    columns = jnp.where(left, out_ref[:, :half], out_ref[:, half:])
    for part in range(groups):
        dealt[part] = exact(
            columns, inverse[part * piece : (part + 1) * piece, :], ((1,), (1,))
        )

    def deal(shift):
        return remote(
            dealt.at[lax.rem(g + shift, groups)],
            from_group.at[shift - 1],
            deal_sems.at[0, shift - 1],
            deal_sems.at[1, shift - 1],
            group_peer(shift),
        )

    for shift in range(1, groups):
        deal(shift).start()
    own.finish()
    far.finish()
    far_x.wait_send()
    for strip in range(strips):
        planes[strip].finish()
        cross_x(strip).wait_send()
    for strip in range(early, strips):
        for parity in range(2):
            late_copy(strip, parity).wait_send()
    value = jnp.where(g == owner, dealt[g], 0.0)
    for shift in range(1, groups):
        deal(shift).wait_recv()
        source = lax.rem(g - shift + groups, groups)
        value = jnp.where(source == owner, from_group[shift - 1], value)
    factor_ref[...] = value
    for shift in range(1, groups):
        deal(shift).wait_send()


def tail_call(panel, first_diag, x_hi, x_lo, own, block, flat, far, early):
    depth, width = flat.shape
    half = width // 2
    G = lax.axis_size(GROUP)
    f32, bf16 = jnp.float32, jnp.bfloat16
    vmem = pl.BlockSpec(memory_space=pltpu.VMEM)
    smem = pl.BlockSpec(memory_space=pltpu.SMEM)
    hbm = pl.BlockSpec(memory_space=pl.ANY)
    thick = 128
    strips = half // thick
    late = strips - early.shape[1] // (2 * thick)
    share = PW // G
    sems = pltpu.SemaphoreType.DMA
    return pl.pallas_call(
        tail_kernel,
        in_specs=[smem, vmem, vmem, vmem, vmem, vmem, hbm, hbm, hbm],
        out_specs=[vmem, vmem, hbm],
        out_shape=[
            jax.ShapeDtypeStruct((half, width), f32),
            jax.ShapeDtypeStruct((half, share), f32),
            jax.ShapeDtypeStruct((depth, late * 2 * thick), f32),
        ],
        scratch_shapes=[
            pltpu.VMEM((2, depth, 256), f32),
            pltpu.VMEM((256, depth), bf16),
            pltpu.VMEM((256, depth), bf16),
            pltpu.VMEM((2, half, half), f32),
            pltpu.VMEM((half, half), f32),
            pltpu.VMEM((half, half), f32),
            pltpu.VMEM((strips, 2 * thick, width), f32),
            pltpu.VMEM((strips, thick, width), f32),
            pltpu.VMEM((strips, 2, half, thick), f32),
            pltpu.VMEM((half, width), f32),
            pltpu.VMEM((2, half, width), f32),
            pltpu.VMEM((2, half, half), f32),
            pltpu.VMEM((strips, 2, thick, width), f32),
            pltpu.VMEM((PW, PW), f32),
            pltpu.VMEM((PW, PW), f32),
            pltpu.VMEM((128, 128), f32),
            pltpu.VMEM((128, 128), f32),
            pltpu.VMEM((G, half, share), f32),
            pltpu.VMEM((G - 1, half, share), f32),
            sems((2, 2)),
            sems((2, late, 2)),
            sems((2,)),
            sems((2, strips)),
            sems((4,)),
            sems((4,)),
            sems((4 * strips,)),
            sems((strips, 2)),
            sems((strips, 2)),
            sems((2,)),
            sems((2, G - 1)),
        ],
        compiler_params=pltpu.CompilerParams(
            collective_id=1, has_side_effects=True, vmem_limit_bytes=60 * 1024 * 1024
        ),
        cost_estimate=pl.CostEstimate(
            flops=9 * depth * width * width, bytes_accessed=4 * depth * width * 3, transcendentals=0
        ),
    )(panel, first_diag[None, :], x_hi, x_lo, own, block, flat, far, early)


def folded_body(kkt, border, first_diag, assignment, panel):
    slots, order, width = border.shape
    flat = border.reshape(slots * order, width)
    extra = jnp.where(lax.axis_index("scen") == panel[0], first_diag, 0.0)[None, :]
    x_hi, x_lo, own, block, far, strip = head_call(
        assignment, panel, extra, kkt, flat, width // 2
    )
    schur, factor, _ = tail_call(panel, first_diag, x_hi, x_lo, own, block, flat, far, strip)
    return (schur, factor)


def body(kkt, border, first_diag, assignment, panel):
    groups = lax.axis_size(GROUP)
    foldable = (
        groups == 4
        and lax.axis_size("row") == 2
        and lax.axis_size("scen") == 2 * groups
        and border.shape[2] == 2 * first_diag.shape[0]
        and first_diag.shape[0] == PW
    )
    chosen = folded_body if foldable else plain_body
    return chosen(kkt, border, first_diag, assignment, panel)


def solution(mesh):
    in_specs = (
        P("scen", ("row", "col"), None),
        P("scen", None, ("row", "col")),
        P("scen"),
        P("scen"),
        P(),
    )
    out_specs = (P("scen", ("row", "col")), P("scen", ("row", "col")))
    return jax.shard_map(body, mesh=mesh, in_specs=in_specs, out_specs=out_specs, check_vma=False)
```

```python
import jax
import jax.numpy as jnp
from jax import lax
from jax.experimental import pallas as pl
from jax.experimental.pallas import tpu as pltpu
from jax.sharding import PartitionSpec as P

PW = 512
NEWTON = 3


HIGH = lax.Precision.HIGH
GROUP = ("row", "col")


def swapped(value, axis, distance):
    mask = 2**distance
    pairs = [(source, source ^ mask) for source in range(lax.axis_size(axis))]
    return lax.ppermute(value, axis, pairs)


def gathered_rows(value, axis):
    count = lax.axis_size(axis)
    index = lax.axis_index(axis)
    rows = value.shape[1]
    whole = jnp.zeros((value.shape[0], rows * count, value.shape[2]), value.dtype)
    whole = lax.dynamic_update_slice_in_dim(whole, value, index * rows, 1)
    for shift in range(1, count):
        pairs = [(source, (source + shift) % count) for source in range(count)]
        origin = lax.rem(index - shift + count, count)
        whole = lax.dynamic_update_slice_in_dim(
            whole, lax.ppermute(value, axis, pairs), origin * rows, 1
        )
    return whole


def matmul(left, right, precision=HIGH):
    return jnp.dot(left, right, precision=precision, preferred_element_type=jnp.float32)


def contract(left, right):
    return lax.dot_general(
        left, right, (((0,), (0,)), ((), ())), precision=HIGH, preferred_element_type=jnp.float32
    )


def plain_body(kkt, border, first_diag, assignment, panel):
    scen_index = lax.axis_index("scen")
    own_index = lax.axis_index(GROUP)
    group_size = lax.axis_size(GROUP)
    slots, order, col_count = border.shape
    width = col_count * group_size
    scenario_ids = scen_index * slots + jnp.arange(slots, dtype=jnp.int32)
    kkt = jnp.where((assignment == scenario_ids)[:, None, None], kkt, swapped(kkt, "scen", 0))
    kkt_all = gathered_rows(gathered_rows(kkt, "col"), "row")
    gathered = lax.all_gather(border, GROUP, axis=2, tiled=True)
    eye = jnp.eye(order, dtype=jnp.bool_)
    inverses = []
    for slot in range(slots):
        full = kkt_all[slot]
        diag = jnp.where(eye, full, 0.0)
        row_inv = 1.0 / jnp.sum(diag, axis=1, keepdims=True)
        col_inv = 1.0 / jnp.sum(diag, axis=0, keepdims=True)
        approx = jnp.where(eye, 2.0 * row_inv, 0.0) - row_inv * full * col_inv
        for step in range(NEWTON - 1):
            approx = 2.0 * approx - matmul(matmul(approx, full), approx)
        inverses.append(approx)
    solved = jnp.concatenate([matmul(inverses[slot], border[slot]) for slot in range(slots)], 0)
    border_all = gathered.reshape(slots * order, width)

    panel_start = panel[0] * PW
    share = PW // group_size
    own_start = panel_start + own_index * share

    share_solved = jnp.concatenate(
        [
            matmul(inverses[slot], lax.dynamic_slice_in_dim(gathered[slot], own_start, share, 1))
            for slot in range(slots)
        ],
        0,
    )
    panel_border = lax.dynamic_slice_in_dim(border_all, panel_start, PW, 1)
    block = contract(panel_border, share_solved)
    row_span = first_diag.shape[0]
    global_rows = scen_index * row_span + jnp.arange(row_span, dtype=jnp.int32)
    share_ids = own_start + jnp.arange(share, dtype=jnp.int32)
    owned = global_rows[:, None] == share_ids[None, :]
    share_diag = jnp.sum(jnp.where(owned, first_diag[:, None], 0.0), axis=0)
    panel_ids = panel_start + jnp.arange(PW, dtype=jnp.int32)
    block = block + jnp.where(panel_ids[:, None] == share_ids[None, :], share_diag[None, :], 0.0)
    block = lax.psum(block, "scen")
    block = lax.all_gather(block, GROUP, axis=1, tiled=True)
    symmetric = 0.5 * (block + block.T)
    lower_factor = jnp.linalg.cholesky(symmetric)
    lower_inverse = lax.linalg.triangular_solve(
        lower_factor, jnp.eye(PW, dtype=jnp.float32), left_side=True, lower=True
    )
    own_inverse = lax.dynamic_slice_in_dim(lower_inverse, own_index * share, share, 0)

    def schur_columns(start, count, solved):
        tile = contract(border_all, lax.dynamic_slice_in_dim(solved, start, count, 1))
        summed = lax.psum_scatter(tile, "scen", scatter_dimension=0, tiled=True)
        global_cols = own_index * col_count + start + jnp.arange(count, dtype=jnp.int32)
        on_diag = global_rows[:, None] == global_cols[None, :]
        return summed + jnp.where(on_diag, first_diag[:, None], 0.0)

    if col_count >= PW:
        pieces = col_count // PW
        first = lax.rem(panel[0], pieces)
        schur = jnp.zeros((row_span, col_count), jnp.float32)
        panel_rows = None
        for piece in range(pieces):
            start = lax.rem(first + piece, pieces) * PW
            columns = schur_columns(start, PW, solved)
            if piece == 0:
                owns = own_index == panel[0] // pieces
                columns, solved = lax.optimization_barrier((columns, solved))
                panel_rows = lax.psum(jnp.where(owns, columns, 0.0), GROUP)
            schur = lax.dynamic_update_slice_in_dim(schur, columns, start, 1)
    else:
        schur = schur_columns(jnp.int32(0), col_count, solved)
        parts = PW // col_count
        position = own_index - panel[0] * parts
        owns = (position >= 0) & (position < parts)
        placed = jnp.zeros((row_span, PW), jnp.float32)
        placed = lax.dynamic_update_slice_in_dim(
            placed, jnp.where(owns, schur, 0.0), jnp.clip(position, 0, parts - 1) * col_count, 1
        )
        panel_rows = lax.psum(placed, GROUP)
    own_cols = lax.dot_general(
        panel_rows,
        own_inverse,
        (((1,), (1,)), ((), ())),
        precision=lax.Precision.HIGHEST,
        preferred_element_type=jnp.float32,
    )
    return (schur, own_cols)


def parts(value):
    high = value.astype(jnp.bfloat16)
    return high, (value - high.astype(jnp.float32)).astype(jnp.bfloat16)


def dot(left, right):
    return jnp.dot(left, right, preferred_element_type=jnp.float32)


def dot_rows(left, right):
    return lax.dot_general(
        left, right, (((0,), (0,)), ((), ())), preferred_element_type=jnp.float32
    )


def head_kernel(
    assignment_ref,
    panel_ref,
    extra_ref,
    kkt_ref,
    border_ref,
    x_hi,
    x_lo,
    own_ref,
    total,
    far_ref,
    strip_ref,
    own_tiles,
    share,
    from_scen,
    swap,
    full,
    loaded,
    b_hi,
    b_lo,
    e_hi,
    e_lo,
    m_hi,
    m_lo,
    p_hi,
    z_hi,
    z_lo,
    head,
    load_sem,
    own_sems,
    swap_sems,
    y_sems,
    core_sems,
    far_sems,
    strip_sems,
    scen_sems,
    spread_sems,
):
    slots, order, _ = full.shape
    rows = kkt_ref.shape[1]
    width = x_hi.shape[1]
    half = width // 2
    panel_width = share.shape[0]
    groups = lax.axis_size(GROUP)
    S = lax.axis_size("scen")
    step = 256
    s = lax.axis_index("scen")
    core = lax.axis_index("row")
    y = lax.axis_index("col")
    g = core * 2 + y
    flip_x = s + 1 - 2 * lax.rem(s, 2)

    def group_peer(shift):
        to = lax.rem(g + shift, groups)
        return (s, to // 2, lax.rem(to, 2))

    def scen_peer(shift):
        return (lax.rem(s + shift, S), core, y)

    barrier = pltpu.get_barrier_semaphore()
    for shift in range(1, groups):
        pl.semaphore_signal(
            barrier, inc=1, device_id=group_peer(shift), device_id_type=pl.DeviceIdType.MESH
        )
    for shift in range(1, S):
        pl.semaphore_signal(
            barrier, inc=1, device_id=scen_peer(shift), device_id_type=pl.DeviceIdType.MESH
        )
    pl.semaphore_wait(barrier, groups + S - 2)

    def remote(source, target, sems, index, device):
        return pltpu.make_async_remote_copy(
            src_ref=source,
            dst_ref=target,
            send_sem=sems.at[0, index],
            recv_sem=sems.at[1, index],
            device_id=device,
            device_id_type=pl.DeviceIdType.MESH,
        )

    def swap_copy(slot):
        return remote(kkt_ref.at[slot], swap.at[slot], swap_sems, slot, (flip_x, core, y))

    own_rows = pl.ds(pl.multiple_of(g * rows, 8), rows)
    core_rows = pl.ds(pl.multiple_of(core * (2 * rows), 8), 2 * rows)

    def y_copy(slot):
        place = full.at[slot, own_rows, :]
        return remote(place, place, y_sems, slot, (s, core, 1 - y))

    def core_copy(slot):
        place = full.at[slot, core_rows, :]
        return remote(place, place, core_sems, slot, (s, 1 - core, y))

    def load(slot):
        return pltpu.make_async_copy(
            border_ref.at[pl.ds(slot * order, order), :], loaded, load_sem
        )

    far_copy = remote(border_ref, far_ref, far_sems, 0, (s, 1 - core, y))
    strip_width = strip_ref.shape[1] // 2
    cuts = [(0, order // 2), (order // 2, slots * order - order // 2)]
    strip_copies = [
        [
            remote(
                border_ref.at[pl.ds(low, count), pl.ds(p * half, strip_width)],
                strip_ref.at[pl.ds(low, count), pl.ds(p * strip_width, strip_width)],
                strip_sems,
                2 * index + p,
                group_peer(groups - 1),
            )
            for p in range(2)
        ]
        for index, (low, count) in enumerate(cuts)
    ]

    for slot in range(slots):
        swap_copy(slot).start()
    load(0).start()
    for copy in strip_copies[0]:
        copy.start()

    def select_rows(slot):
        swap_copy(slot).wait_recv()
        same = assignment_ref[slot] == s * slots + slot
        full[slot, own_rows, :] = jnp.where(same, kkt_ref[slot], swap[slot])
        y_copy(slot).start()

    select_rows(0)
    select_rows(1)
    y_copy(0).wait_recv()
    core_copy(0).start()
    for slot in range(2, slots):
        select_rows(slot)
    far_copy.start()
    y_copy(1).wait_recv()
    core_copy(1).start()

    def eye_at(start):
        row = lax.broadcasted_iota(jnp.int32, (step, order), 0) + start
        return row == lax.broadcasted_iota(jnp.int32, (step, order), 1)

    @pl.loop(0, slots)
    def _(slot):
        core_copy(slot).wait_recv()
        col_diag = jnp.zeros((1, order), jnp.float32)
        for start in range(0, order, step):
            spot = pl.ds(start, step)
            block = full[slot, spot, :]
            eye = eye_at(start)
            diag = jnp.where(eye, block, 0.0)
            col_diag = col_diag + jnp.sum(diag, axis=0, keepdims=True)
            scale = 1.0 / jnp.sum(diag, axis=1, keepdims=True)
            scaled = jnp.where(eye, 0.0, -scale * block)
            head[spot, :] = scaled
            high, low = parts(scaled)
            e_hi[spot, :] = high
            e_lo[spot, :] = low
        col_inv = 1.0 / col_diag

        @pl.loop(0, order // step)
        def _(chunk):
            spot = pl.ds(pl.multiple_of(chunk * step, step), step)
            high = e_hi[spot, :]
            value = dot(high, e_hi[...]) + dot(high, e_lo[...]) + dot(e_lo[spot, :], e_hi[...])
            head[spot, :] += value
            high, low = parts(value)
            m_hi[spot, :] = high
            m_lo[spot, :] = low

        @pl.loop(0, order // step)
        def _(chunk):
            start = pl.multiple_of(chunk * step, step)
            spot = pl.ds(start, step)
            high = e_hi[spot, :]
            value = dot(high, m_hi[...]) + dot(high, m_lo[...]) + dot(e_lo[spot, :], m_hi[...])
            head[spot, :] += value + jnp.where(eye_at(start), 1.0, 0.0)
            p_hi[spot, :] = dot(m_hi[spot, :], m_hi[...]).astype(jnp.bfloat16)

        @pl.loop(0, order // step)
        def _(chunk):
            spot = pl.ds(pl.multiple_of(chunk * step, step), step)
            value = head[spot, :]
            value = (value + dot(value.astype(jnp.bfloat16), p_hi[...])) * col_inv
            high, low = parts(value)
            z_hi[spot, :] = high
            z_lo[spot, :] = low

        here = pl.ds(pl.multiple_of(slot * order, step), order)
        load(slot).wait()

        @pl.loop(0, width // step)
        def _(chunk):
            spot = pl.ds(pl.multiple_of(chunk * step, step), step)
            high, low = parts(loaded[:, spot])
            b_hi[here, spot] = high
            b_lo[here, spot] = low
            high, low = parts(dot(z_hi[...], high) + dot(z_hi[...], low) + dot(z_lo[...], high))
            x_hi[here, spot] = high
            x_lo[here, spot] = low

        @pl.when(slot < slots - 1)
        def _():
            load(slot + 1).start()

        @pl.when(slot == 0)
        def _():
            for later in range(2, slots):
                y_copy(later).wait_recv()
                core_copy(later).start()
            for copy in strip_copies[1]:
                copy.start()

    x = lax.rem(s, 2)

    def own_tile(parity, tile):
        spot = pl.ds(pl.multiple_of(parity * half + tile * step, step), step)
        high, low = b_hi[:, spot], b_lo[:, spot]
        to = pl.ds(tile * step, step)

        @pl.loop(0, width // step)
        def _(chunk):
            cols = pl.ds(pl.multiple_of(chunk * step, step), step)
            x_high, x_low = x_hi[:, cols], x_lo[:, cols]
            own_tiles[parity, to, cols] = (
                dot_rows(high, x_high) + dot_rows(high, x_low) + dot_rows(low, x_high)
            )

    own_copy = remote(own_tiles.at[1 - x], own_ref, own_sems, 0, (flip_x, core, y))

    left = lax.rem(panel_ref[0], 2) == 0
    row = lax.broadcasted_iota(jnp.int32, (step, panel_width), 0)
    col = lax.broadcasted_iota(jnp.int32, (step, panel_width), 1)
    x_high = jnp.where(left, x_hi[:, :half], x_hi[:, half:])
    x_low = jnp.where(left, x_lo[:, :half], x_lo[:, half:])
    for start in range(0, panel_width, step):
        low_side = slice(start, start + step)
        high_side = slice(half + start, half + start + step)
        high = jnp.where(left, b_hi[:, low_side], b_hi[:, high_side])
        low = jnp.where(left, b_lo[:, low_side], b_lo[:, high_side])
        value = dot_rows(high, x_high) + dot_rows(high, x_low) + dot_rows(low, x_high)
        share[low_side, :] = value + jnp.where(row + start == col, extra_ref[...], 0.0)
    part_rows = panel_width // S
    own_part = pl.ds(pl.multiple_of(s * part_rows, 8), part_rows)

    def reduce_copy(shift):
        to = lax.rem(s + shift, S)
        return remote(
            share.at[pl.ds(pl.multiple_of(to * part_rows, 8), part_rows), :],
            from_scen.at[shift - 1],
            scen_sems,
            shift - 1,
            scen_peer(shift),
        )

    def spread_copy(shift):
        place = total.at[own_part, :]
        return remote(place, place, spread_sems, shift - 1, scen_peer(shift))

    for shift in range(1, S):
        reduce_copy(shift).start()
    own_tile(1 - x, 0)
    own_tile(1 - x, 1)
    own_copy.start()
    own_tile(x, 0)
    value = share[own_part, :]
    for shift in range(1, S):
        reduce_copy(shift).wait_recv()
        value = value + from_scen[shift - 1]
    total[own_part, :] = value
    for shift in range(1, S):
        spread_copy(shift).start()
    own_tile(x, 1)
    for shift in range(1, S):
        spread_copy(shift).wait_recv()
        spread_copy(shift).wait_send()
        reduce_copy(shift).wait_send()
    own_copy.wait()
    own_ref[...] += own_tiles[x]
    for slot in range(slots):
        swap_copy(slot).wait_send()
        y_copy(slot).wait_send()
        core_copy(slot).wait_send()
    far_copy.wait()
    for copies in strip_copies:
        for copy in copies:
            copy.wait()


def head_call(assignment, panel, extra, kkt, flat, strip_width):
    slots, rows, order = kkt.shape
    depth, width = flat.shape
    S = lax.axis_size("scen")
    f32, bf16 = jnp.float32, jnp.bfloat16
    vmem = pl.BlockSpec(memory_space=pltpu.VMEM)
    smem = pl.BlockSpec(memory_space=pltpu.SMEM)
    hbm = pl.BlockSpec(memory_space=pl.ANY)

    def sems(count):
        return pltpu.SemaphoreType.DMA((2, count))

    return pl.pallas_call(
        head_kernel,
        in_specs=[smem, smem, vmem, vmem, hbm],
        out_specs=[vmem, vmem, vmem, vmem, hbm, hbm],
        out_shape=[
            jax.ShapeDtypeStruct((depth, width), bf16),
            jax.ShapeDtypeStruct((depth, width), bf16),
            jax.ShapeDtypeStruct((PW, width), f32),
            jax.ShapeDtypeStruct((PW, PW), f32),
            jax.ShapeDtypeStruct((depth, width), f32),
            jax.ShapeDtypeStruct((depth, strip_width), f32),
        ],
        scratch_shapes=[
            pltpu.VMEM((2, PW, width), f32),
            pltpu.VMEM((PW, PW), f32),
            pltpu.VMEM((S - 1, PW // S, PW), f32),
            pltpu.VMEM((slots, rows, order), f32),
            pltpu.VMEM((slots, order, order), f32),
            pltpu.VMEM((order, width), f32),
            pltpu.VMEM((depth, width), bf16),
            pltpu.VMEM((depth, width), bf16),
        ]
        + [pltpu.VMEM((order, order), bf16)] * 7
        + [
            pltpu.VMEM((order, order), f32),
            pltpu.SemaphoreType.DMA,
            sems(1),
            sems(slots),
            sems(slots),
            sems(slots),
            sems(1),
            sems(4),
            sems(S - 1),
            sems(S - 1),
        ],
        compiler_params=pltpu.CompilerParams(
            collective_id=0, has_side_effects=True, vmem_limit_bytes=60 * 1024 * 1024
        ),
        cost_estimate=pl.CostEstimate(
            flops=2 * slots * order * order * (8 * order + 3 * width) + 6 * depth * width * width,
            bytes_accessed=4 * depth * width * 3,
            transcendentals=0,
        ),
    )(assignment, panel, extra, kkt, flat)


def factor_block(s_ref, w_ref):
    size = s_ref.shape[0]
    pivots = 4
    row = lax.broadcasted_iota(jnp.int32, (size, size), 0)
    lane = lax.broadcasted_iota(jnp.int32, (size, size), 1)
    thin = lax.broadcasted_iota(jnp.int32, (1, size), 1)
    tall = lax.broadcasted_iota(jnp.int32, (size, 1), 0)
    w_ref[...] = jnp.where(row == lane, 1.0, 0.0)

    @pl.loop(0, size // pivots)
    def _(block):
        j = block * pivots
        whole = s_ref[...]
        rows = [s_ref[pl.ds(j + p, 1), :] for p in range(pivots)]
        tails = [w_ref[pl.ds(j + p, 1), :] for p in range(pivots)]
        cols = [
            jnp.sum(jnp.where(lane == j + p, whole, 0.0), axis=1, keepdims=True)
            for p in range(pivots)
        ]
        small = [
            [
                jnp.sum(jnp.where(thin == j + q, rows[p], 0.0), axis=1, keepdims=True)
                for q in range(p, pivots)
            ]
            for p in range(pivots)
        ]
        entry = lambda q, p: small[p][q - p]
        lower = {}
        tails_new, rows_new, cols_new = [], [], []
        for p in range(pivots):
            value = entry(p, p)
            for q in range(p):
                value = value - lower[p, q] * lower[p, q]
            root = lax.rsqrt(value)
            root = root * (1.5 - 0.5 * value * root * root)
            for i in range(p + 1, pivots):
                below = entry(i, p)
                for q in range(p):
                    below = below - lower[i, q] * lower[p, q]
                lower[i, p] = below * root
            u, c, v = rows[p], cols[p], tails[p]
            for q in range(p):
                u = u - lower[p, q] * rows_new[q]
                c = c - lower[p, q] * cols_new[q]
                v = v - lower[p, q] * tails_new[q]
            rows_new.append(u * root)
            cols_new.append(c * root)
            tails_new.append(v * root)
        change = jnp.zeros((size, size), jnp.float32)
        other = jnp.zeros((size, size), jnp.float32)
        for p in range(pivots):
            c = jnp.where(tall >= j + pivots, cols_new[p], 0.0)
            change = change + c * rows_new[p]
            other = other + c * tails_new[p]
        s_ref[...] = whole - change
        w_ref[...] = w_ref[...] - other
        for p in range(pivots):
            w_ref[pl.ds(j + p, 1), :] = tails_new[p]


def exact(left, right, axes=((1,), (0,))):
    return lax.dot_general(
        left,
        right,
        (axes, ((), ())),
        precision=lax.Precision.HIGHEST,
        preferred_element_type=jnp.float32,
    )


def tail_kernel(
    panel_ref,
    diag_ref,
    x_hi,
    x_lo,
    own_in,
    block_ref,
    border_ref,
    far_ref,
    early_ref,
    out_ref,
    factor_ref,
    late_ref,
    stage,
    lt_hi,
    lt_lo,
    far_tile,
    from_x_far,
    far_turned,
    cross,
    from_x,
    turned,
    own_acc,
    own_z,
    far_z,
    cross_z,
    work,
    inverse,
    s_ref,
    w_ref,
    dealt,
    from_group,
    stage_sems,
    late_sems,
    far_x_sems,
    x_sems,
    own_z_sems,
    far_z_sems,
    cross_z_sems,
    turn_send,
    turn_recv,
    far_turn_sems,
    deal_sems,
):
    depth, width = x_hi.shape
    half = width // 2
    groups = dealt.shape[0]
    strips = cross.shape[0]
    thick = cross.shape[1] // 2
    early = early_ref.shape[1] // (2 * thick)
    step = 256
    s = lax.axis_index("scen")
    core = lax.axis_index("row")
    y = lax.axis_index("col")
    S = lax.axis_size("scen")
    g = core * 2 + y
    x = lax.rem(s, 2)
    z = s // 2
    flip_x = s + 1 - 2 * x
    MESH = pl.DeviceIdType.MESH

    def group_peer(shift):
        to = lax.rem(g + shift, groups)
        return (s, to // 2, lax.rem(to, 2))

    def mirror(parity):
        return (2 * g + parity, z // 2, lax.rem(z, 2))

    barrier = pltpu.get_barrier_semaphore()
    for shift in range(1, groups):
        pl.semaphore_signal(barrier, inc=1, device_id=group_peer(shift), device_id_type=MESH)
    for shift in range(1, S):
        pl.semaphore_signal(
            barrier, inc=1, device_id=(lax.rem(s + shift, S), core, y), device_id_type=MESH
        )

    @pl.when(z != g)
    def _():
        for parity in range(2):
            pl.semaphore_signal(barrier, inc=1, device_id=mirror(parity), device_id_type=MESH)
        pl.semaphore_wait(barrier, groups + S)

    @pl.when(z == g)
    def _():
        pl.semaphore_wait(barrier, groups + S - 2)

    def remote(source, target, send, recv, device):
        return pltpu.make_async_remote_copy(
            src_ref=source,
            dst_ref=target,
            send_sem=send,
            recv_sem=recv,
            device_id=device,
            device_id_type=MESH,
        )

    class Plane:
        def __init__(self, value, first, second, sems, base, shift):
            self.value, self.first, self.second = value, first, second
            self.target = lax.rem(g + shift, groups)
            low = z - lax.rem(z, 2)
            self.keeper = jnp.minimum(jnp.maximum(self.target, low), low + 1)
            self.one = remote(
                value, first, sems.at[base], sems.at[base + 1], (self.keeper * 2 + x, core, y)
            )
            self.two = remote(
                value, second, sems.at[base + 2], sems.at[base + 3], (self.target * 2 + x, core, y)
            )

        def send(self):
            @pl.when(z != self.keeper)
            def _():
                self.one.start()

        def pass_on(self):
            @pl.when(z == self.keeper)
            def _():
                self.one.wait_recv()
                self.value[...] += self.first[...]

                @pl.when(z != self.target)
                def _():
                    self.two.start()

        def take(self):
            self.two.wait_recv()
            self.value[...] += self.second[...]

        def finish(self):
            @pl.when(z != self.keeper)
            def _():
                self.one.wait_send()

            @pl.when((z == self.keeper) & (z != self.target))
            def _():
                self.two.wait_send()

    def late_copy(strip, parity):
        return remote(
            border_ref.at[:, pl.ds(parity * half + strip * thick, thick)],
            late_ref.at[:, pl.ds(((strip - early) * 2 + parity) * thick, thick)],
            late_sems.at[0, strip - early, parity],
            late_sems.at[1, strip - early, parity],
            group_peer(groups - 1),
        )

    own = Plane(own_acc, own_z.at[0], own_z.at[1], own_z_sems, 0, 0)
    own_acc[...] = own_in[...]
    own.send()
    for parity in range(2):
        late_copy(early, parity).start()

    def stage_load(slot, source, start, count, part):
        return pltpu.make_async_copy(
            source.at[:, pl.ds(start, count)],
            stage.at[slot, :, pl.ds(part * count, count)],
            stage_sems.at[slot, part],
        )

    def strip_load(slot, strip, part):
        if strip < early:
            return stage_load(slot, early_ref, part * early * thick + strip * thick, thick, part)
        return stage_load(slot, late_ref, ((strip - early) * 2 + part) * thick, thick, part)

    def far_load(slot, parity, tile):
        return stage_load(
            slot, far_ref, pl.multiple_of(parity * half + tile * step, step), step, 0
        )

    def product(slot, target, base, count):
        @pl.loop(0, depth // step)
        def _(chunk):
            spot = pl.ds(pl.multiple_of(chunk * step, step), step)
            high, low = parts(stage[slot, spot, :].T)
            lt_hi[:, spot] = high
            lt_lo[:, spot] = low

        @pl.loop(0, count // step)
        def _(chunk):
            start = pl.multiple_of(chunk * step, step)
            cols = pl.ds(pl.multiple_of(base + start, step), step)
            high, low = x_hi[:, cols], x_lo[:, cols]
            target[:, pl.ds(start, step)] = (
                dot(lt_hi[...], high) + dot(lt_hi[...], low) + dot(lt_lo[...], high)
            )

    near = g < groups // 2

    def far_side(parity):
        return jnp.where(near, parity, 1 - parity)

    def far_product(slot, parity, tile):
        product(
            slot, far_tile.at[parity, pl.ds(tile * step, step), :], far_side(parity) * half, half
        )

    far_x = remote(
        far_tile.at[1 - x], from_x_far, far_x_sems.at[0], far_x_sems.at[1], (flip_x, core, y)
    )
    loads = [
        [far_load(0, 1 - x, 0)],
        [far_load(1, 1 - x, 1)],
    ]
    for strip in range(early):
        loads.append([strip_load(strip % 2, strip, part) for part in range(2)])
    for tile in range(2):
        loads.append([far_load((early + tile) % 2, x, tile)])

    def begin(index):
        for copy in loads[index]:
            copy.start()

    def ready(index):
        for copy in loads[index]:
            copy.wait()
        if index + 1 < len(loads):
            begin(index + 1)

    def kept(strip):
        return cross.at[strip, pl.ds(pl.multiple_of(x * thick, 8), thick), :]

    def cross_x(strip):
        return remote(
            cross.at[strip, pl.ds(pl.multiple_of((1 - x) * thick, 8), thick), :],
            from_x.at[strip],
            x_sems.at[0, strip],
            x_sems.at[1, strip],
            (flip_x, core, y),
        )

    planes = [
        Plane(kept(i), cross_z.at[i, 0], cross_z.at[i, 1], cross_z_sems, 4 * i, 1)
        for i in range(strips)
    ]
    far = Plane(far_tile.at[x], far_z.at[0], far_z.at[1], far_z_sems, 0, 2)

    def join_x(strip):
        cross_x(strip).wait_recv()
        kept(strip)[...] += from_x[strip]
        planes[strip].send()

    def turn(strip, parity):
        place = out_ref.at[:, pl.ds(pl.multiple_of(x * half + strip * thick, thick), thick)]
        return remote(
            turned.at[strip, parity],
            place,
            turn_send.at[strip, parity],
            turn_recv.at[strip, x],
            mirror(parity),
        )

    offset = lax.rem(z - g + groups, groups)

    def settle(strip):
        @pl.when(offset == 1)
        def _():
            planes[strip].take()
            value = kept(strip)[...]
            out_ref[pl.ds(strip * thick, thick), :] = value
            for parity in range(2):
                turned[strip, parity] = value[:, parity * half : (parity + 1) * half].T
                turn(strip, parity).start()

    mine = far_side(x)
    far_turn = remote(
        far_turned,
        out_ref.at[:, pl.ds(pl.multiple_of(x * half, half), half)],
        far_turn_sems.at[0],
        far_turn_sems.at[1],
        (2 * g + mine, z // 2, lax.rem(z, 2)),
    )

    size = s_ref.shape[0]
    count = work.shape[0] // size

    def spot(index):
        return slice(index * size, (index + 1) * size)

    def eliminate(k):
        s_ref[...] = work[spot(k), spot(k)]
        factor_block(s_ref, w_ref)
        inverse[spot(k), spot(k)] = w_ref[...]
        if k + 1 < count:
            rest = slice((k + 1) * size, count * size)
            below = exact(work[rest, spot(k)], w_ref[...], ((1,), (1,)))
            work[rest, spot(k)] = below
            work[rest, rest] = work[rest, rest] - exact(below, below, ((1,), (1,)))
        if k > 0:
            known = slice(0, k * size)
            row = exact(work[spot(k), known], inverse[known, known])
            inverse[spot(k), known] = -exact(w_ref[...], row)

    def late_strip(strip):
        for parity in range(2):
            late_copy(strip, parity).wait_recv()
            if strip + 1 < strips:
                late_copy(strip + 1, parity).start()
        for part in range(2):
            strip_load(strip % 2, strip, part).start()
        for part in range(2):
            strip_load(strip % 2, strip, part).wait()
        product(strip % 2, cross.at[strip], 0, width)
        cross_x(strip).start()

    work[...] = 0.5 * (block_ref[...] + block_ref[...].T)
    inverse[...] = jnp.zeros(inverse.shape, jnp.float32)
    begin(0)
    for tile in range(2):
        ready(tile)
        far_product(tile, 1 - x, tile)
    far_x.start()
    for strip in range(early):
        ready(2 + strip)
        product(strip % 2, cross.at[strip], 0, width)
        cross_x(strip).start()
    for tile in range(2):
        ready(2 + early + tile)
        far_product((early + tile) % 2, x, tile)
    far_x.wait_recv()
    far_tile[x] += from_x_far[...]
    far.send()
    own.pass_on()
    for strip in range(early):
        join_x(strip)
    late_strip(early)
    eliminate(0)
    far.pass_on()
    for strip in range(early):
        planes[strip].pass_on()
    join_x(early)
    eliminate(1)

    @pl.when(offset == 0)
    def _():
        own.take()
        row = lax.broadcasted_iota(jnp.int32, (half, width), 0) + x * half
        col = lax.broadcasted_iota(jnp.int32, (half, width), 1)
        out_ref[...] = own_acc[...] + jnp.where(row == col, diag_ref[...].T, 0.0)

    @pl.when(offset == 2)
    def _():
        far.take()
        value = far_tile[x]
        out_ref[:, pl.ds(pl.multiple_of(mine * half, half), half)] = value
        far_turned[...] = value.T
        far_turn.start()

    planes[early].pass_on()
    late_strip(early + 1)
    for strip in range(early):
        settle(strip)
    eliminate(2)
    join_x(early + 1)
    settle(early)
    eliminate(3)
    planes[early + 1].pass_on()
    settle(early + 1)

    @pl.when(offset == 2)
    def _():
        remote(
            far_turned,
            out_ref.at[:, pl.ds(pl.multiple_of((1 - mine) * half, half), half)],
            far_turn_sems.at[0],
            far_turn_sems.at[1],
            mirror(0),
        ).wait_recv()
        far_turn.wait_send()

    @pl.when(offset == 3)
    def _():
        for strip in range(strips):
            for source in range(2):
                remote(
                    turned.at[strip, 0],
                    out_ref.at[:, pl.ds(source * half + strip * thick, thick)],
                    turn_send.at[strip, 0],
                    turn_recv.at[strip, source],
                    mirror(0),
                ).wait_recv()

    @pl.when(offset == 1)
    def _():
        for strip in range(strips):
            for parity in range(2):
                turn(strip, parity).wait_send()

    left = lax.rem(panel_ref[0], 2) == 0
    owner = panel_ref[0] // 2
    piece = dealt.shape[2]
    columns = jnp.where(left, out_ref[:, :half], out_ref[:, half:])
    for part in range(groups):
        dealt[part] = exact(
            columns, inverse[part * piece : (part + 1) * piece, :], ((1,), (1,))
        )

    def deal(shift):
        return remote(
            dealt.at[lax.rem(g + shift, groups)],
            from_group.at[shift - 1],
            deal_sems.at[0, shift - 1],
            deal_sems.at[1, shift - 1],
            group_peer(shift),
        )

    for shift in range(1, groups):
        deal(shift).start()
    own.finish()
    far.finish()
    far_x.wait_send()
    for strip in range(strips):
        planes[strip].finish()
        cross_x(strip).wait_send()
    for strip in range(early, strips):
        for parity in range(2):
            late_copy(strip, parity).wait_send()
    value = jnp.where(g == owner, dealt[g], 0.0)
    for shift in range(1, groups):
        deal(shift).wait_recv()
        source = lax.rem(g - shift + groups, groups)
        value = jnp.where(source == owner, from_group[shift - 1], value)
    factor_ref[...] = value
    for shift in range(1, groups):
        deal(shift).wait_send()


def tail_call(panel, first_diag, x_hi, x_lo, own, block, flat, far, early):
    depth, width = flat.shape
    half = width // 2
    G = lax.axis_size(GROUP)
    f32, bf16 = jnp.float32, jnp.bfloat16
    vmem = pl.BlockSpec(memory_space=pltpu.VMEM)
    smem = pl.BlockSpec(memory_space=pltpu.SMEM)
    hbm = pl.BlockSpec(memory_space=pl.ANY)
    thick = 128
    strips = half // thick
    late = strips - early.shape[1] // (2 * thick)
    share = PW // G
    sems = pltpu.SemaphoreType.DMA
    return pl.pallas_call(
        tail_kernel,
        in_specs=[smem, vmem, vmem, vmem, vmem, vmem, hbm, hbm, hbm],
        out_specs=[vmem, vmem, hbm],
        out_shape=[
            jax.ShapeDtypeStruct((half, width), f32),
            jax.ShapeDtypeStruct((half, share), f32),
            jax.ShapeDtypeStruct((depth, late * 2 * thick), f32),
        ],
        scratch_shapes=[
            pltpu.VMEM((2, depth, 256), f32),
            pltpu.VMEM((256, depth), bf16),
            pltpu.VMEM((256, depth), bf16),
            pltpu.VMEM((2, half, half), f32),
            pltpu.VMEM((half, half), f32),
            pltpu.VMEM((half, half), f32),
            pltpu.VMEM((strips, 2 * thick, width), f32),
            pltpu.VMEM((strips, thick, width), f32),
            pltpu.VMEM((strips, 2, half, thick), f32),
            pltpu.VMEM((half, width), f32),
            pltpu.VMEM((2, half, width), f32),
            pltpu.VMEM((2, half, half), f32),
            pltpu.VMEM((strips, 2, thick, width), f32),
            pltpu.VMEM((PW, PW), f32),
            pltpu.VMEM((PW, PW), f32),
            pltpu.VMEM((128, 128), f32),
            pltpu.VMEM((128, 128), f32),
            pltpu.VMEM((G, half, share), f32),
            pltpu.VMEM((G - 1, half, share), f32),
            sems((2, 2)),
            sems((2, late, 2)),
            sems((2,)),
            sems((2, strips)),
            sems((4,)),
            sems((4,)),
            sems((4 * strips,)),
            sems((strips, 2)),
            sems((strips, 2)),
            sems((2,)),
            sems((2, G - 1)),
        ],
        compiler_params=pltpu.CompilerParams(
            collective_id=1, has_side_effects=True, vmem_limit_bytes=60 * 1024 * 1024
        ),
        cost_estimate=pl.CostEstimate(
            flops=9 * depth * width * width, bytes_accessed=4 * depth * width * 3, transcendentals=0
        ),
    )(panel, first_diag[None, :], x_hi, x_lo, own, block, flat, far, early)


def folded_body(kkt, border, first_diag, assignment, panel):
    slots, order, width = border.shape
    flat = border.reshape(slots * order, width)
    extra = jnp.where(lax.axis_index("scen") == panel[0], first_diag, 0.0)[None, :]
    x_hi, x_lo, own, block, far, strip = head_call(
        assignment, panel, extra, kkt, flat, width // 2
    )
    schur, factor, _ = tail_call(panel, first_diag, x_hi, x_lo, own, block, flat, far, strip)
    return (schur, factor)


def body(kkt, border, first_diag, assignment, panel):
    groups = lax.axis_size(GROUP)
    foldable = (
        groups == 4
        and lax.axis_size("row") == 2
        and lax.axis_size("scen") == 2 * groups
        and border.shape[2] == 2 * first_diag.shape[0]
        and first_diag.shape[0] == PW
    )
    chosen = folded_body if foldable else plain_body
    return chosen(kkt, border, first_diag, assignment, panel)


def solution(mesh):
    in_specs = (
        P("scen", ("row", "col"), None),
        P("scen", None, ("row", "col")),
        P("scen"),
        P("scen"),
        P(),
    )
    out_specs = (P("scen", ("row", "col")), P("scen", ("row", "col")))
    return jax.shard_map(body, mesh=mesh, in_specs=in_specs, out_specs=out_specs, check_vma=False)
```

```python
import jax
import jax.numpy as jnp
from jax import lax
from jax.experimental import pallas as pl
from jax.experimental.pallas import tpu as pltpu
from jax.sharding import PartitionSpec as P

PW = 512
NEWTON = 3


HIGH = lax.Precision.HIGH
GROUP = ("row", "col")


def swapped(value, axis, distance):
    mask = 2**distance
    pairs = [(source, source ^ mask) for source in range(lax.axis_size(axis))]
    return lax.ppermute(value, axis, pairs)


def gathered_rows(value, axis):
    count = lax.axis_size(axis)
    index = lax.axis_index(axis)
    rows = value.shape[1]
    whole = jnp.zeros((value.shape[0], rows * count, value.shape[2]), value.dtype)
    whole = lax.dynamic_update_slice_in_dim(whole, value, index * rows, 1)
    for shift in range(1, count):
        pairs = [(source, (source + shift) % count) for source in range(count)]
        origin = lax.rem(index - shift + count, count)
        whole = lax.dynamic_update_slice_in_dim(
            whole, lax.ppermute(value, axis, pairs), origin * rows, 1
        )
    return whole


def matmul(left, right, precision=HIGH):
    return jnp.dot(left, right, precision=precision, preferred_element_type=jnp.float32)


def contract(left, right):
    return lax.dot_general(
        left, right, (((0,), (0,)), ((), ())), precision=HIGH, preferred_element_type=jnp.float32
    )


def plain_body(kkt, border, first_diag, assignment, panel):
    scen_index = lax.axis_index("scen")
    own_index = lax.axis_index(GROUP)
    group_size = lax.axis_size(GROUP)
    slots, order, col_count = border.shape
    width = col_count * group_size
    scenario_ids = scen_index * slots + jnp.arange(slots, dtype=jnp.int32)
    kkt = jnp.where((assignment == scenario_ids)[:, None, None], kkt, swapped(kkt, "scen", 0))
    kkt_all = gathered_rows(gathered_rows(kkt, "col"), "row")
    gathered = lax.all_gather(border, GROUP, axis=2, tiled=True)
    eye = jnp.eye(order, dtype=jnp.bool_)
    inverses = []
    for slot in range(slots):
        full = kkt_all[slot]
        diag = jnp.where(eye, full, 0.0)
        row_inv = 1.0 / jnp.sum(diag, axis=1, keepdims=True)
        col_inv = 1.0 / jnp.sum(diag, axis=0, keepdims=True)
        approx = jnp.where(eye, 2.0 * row_inv, 0.0) - row_inv * full * col_inv
        for step in range(NEWTON - 1):
            approx = 2.0 * approx - matmul(matmul(approx, full), approx)
        inverses.append(approx)
    solved = jnp.concatenate([matmul(inverses[slot], border[slot]) for slot in range(slots)], 0)
    border_all = gathered.reshape(slots * order, width)

    panel_start = panel[0] * PW
    share = PW // group_size
    own_start = panel_start + own_index * share

    share_solved = jnp.concatenate(
        [
            matmul(inverses[slot], lax.dynamic_slice_in_dim(gathered[slot], own_start, share, 1))
            for slot in range(slots)
        ],
        0,
    )
    panel_border = lax.dynamic_slice_in_dim(border_all, panel_start, PW, 1)
    block = contract(panel_border, share_solved)
    row_span = first_diag.shape[0]
    global_rows = scen_index * row_span + jnp.arange(row_span, dtype=jnp.int32)
    share_ids = own_start + jnp.arange(share, dtype=jnp.int32)
    owned = global_rows[:, None] == share_ids[None, :]
    share_diag = jnp.sum(jnp.where(owned, first_diag[:, None], 0.0), axis=0)
    panel_ids = panel_start + jnp.arange(PW, dtype=jnp.int32)
    block = block + jnp.where(panel_ids[:, None] == share_ids[None, :], share_diag[None, :], 0.0)
    block = lax.psum(block, "scen")
    block = lax.all_gather(block, GROUP, axis=1, tiled=True)
    symmetric = 0.5 * (block + block.T)
    lower_factor = jnp.linalg.cholesky(symmetric)
    lower_inverse = lax.linalg.triangular_solve(
        lower_factor, jnp.eye(PW, dtype=jnp.float32), left_side=True, lower=True
    )
    own_inverse = lax.dynamic_slice_in_dim(lower_inverse, own_index * share, share, 0)

    def schur_columns(start, count, solved):
        tile = contract(border_all, lax.dynamic_slice_in_dim(solved, start, count, 1))
        summed = lax.psum_scatter(tile, "scen", scatter_dimension=0, tiled=True)
        global_cols = own_index * col_count + start + jnp.arange(count, dtype=jnp.int32)
        on_diag = global_rows[:, None] == global_cols[None, :]
        return summed + jnp.where(on_diag, first_diag[:, None], 0.0)

    if col_count >= PW:
        pieces = col_count // PW
        first = lax.rem(panel[0], pieces)
        schur = jnp.zeros((row_span, col_count), jnp.float32)
        panel_rows = None
        for piece in range(pieces):
            start = lax.rem(first + piece, pieces) * PW
            columns = schur_columns(start, PW, solved)
            if piece == 0:
                owns = own_index == panel[0] // pieces
                columns, solved = lax.optimization_barrier((columns, solved))
                panel_rows = lax.psum(jnp.where(owns, columns, 0.0), GROUP)
            schur = lax.dynamic_update_slice_in_dim(schur, columns, start, 1)
    else:
        schur = schur_columns(jnp.int32(0), col_count, solved)
        parts = PW // col_count
        position = own_index - panel[0] * parts
        owns = (position >= 0) & (position < parts)
        placed = jnp.zeros((row_span, PW), jnp.float32)
        placed = lax.dynamic_update_slice_in_dim(
            placed, jnp.where(owns, schur, 0.0), jnp.clip(position, 0, parts - 1) * col_count, 1
        )
        panel_rows = lax.psum(placed, GROUP)
    own_cols = lax.dot_general(
        panel_rows,
        own_inverse,
        (((1,), (1,)), ((), ())),
        precision=lax.Precision.HIGHEST,
        preferred_element_type=jnp.float32,
    )
    return (schur, own_cols)


def parts(value):
    high = value.astype(jnp.bfloat16)
    return high, (value - high.astype(jnp.float32)).astype(jnp.bfloat16)


def dot(left, right):
    return jnp.dot(left, right, preferred_element_type=jnp.float32)


def dot_rows(left, right):
    return lax.dot_general(
        left, right, (((0,), (0,)), ((), ())), preferred_element_type=jnp.float32
    )


def head_kernel(
    assignment_ref,
    panel_ref,
    extra_ref,
    kkt_ref,
    border_ref,
    x_hi,
    x_lo,
    own_ref,
    part_ref,
    far_ref,
    strip_ref,
    own_tiles,
    share,
    from_core,
    from_scen,
    swap,
    full,
    loaded,
    b_hi,
    b_lo,
    e_hi,
    e_lo,
    m_hi,
    m_lo,
    p_hi,
    z_hi,
    z_lo,
    head,
    load_sem,
    own_sems,
    swap_sems,
    y_sems,
    core_sems,
    far_sems,
    strip_sems,
    scen_sems,
    deal_sems,
):
    slots, order, _ = full.shape
    rows = kkt_ref.shape[1]
    width = x_hi.shape[1]
    half = width // 2
    panel_width = share.shape[0]
    groups = lax.axis_size(GROUP)
    S = lax.axis_size("scen")
    step = 256
    s = lax.axis_index("scen")
    core = lax.axis_index("row")
    y = lax.axis_index("col")
    g = core * 2 + y
    flip_x = s + 1 - 2 * lax.rem(s, 2)

    def group_peer(shift):
        to = lax.rem(g + shift, groups)
        return (s, to // 2, lax.rem(to, 2))

    def scen_peer(shift):
        return (lax.rem(s + shift, S), core, y)

    barrier = pltpu.get_barrier_semaphore()
    for shift in range(1, groups):
        pl.semaphore_signal(
            barrier, inc=1, device_id=group_peer(shift), device_id_type=pl.DeviceIdType.MESH
        )
    for shift in range(1, S):
        pl.semaphore_signal(
            barrier, inc=1, device_id=scen_peer(shift), device_id_type=pl.DeviceIdType.MESH
        )
    pl.semaphore_wait(barrier, groups + S - 2)

    def remote(source, target, sems, index, device):
        return pltpu.make_async_remote_copy(
            src_ref=source,
            dst_ref=target,
            send_sem=sems.at[0, index],
            recv_sem=sems.at[1, index],
            device_id=device,
            device_id_type=pl.DeviceIdType.MESH,
        )

    def swap_copy(slot):
        return remote(kkt_ref.at[slot], swap.at[slot], swap_sems, slot, (flip_x, core, y))

    own_rows = pl.ds(pl.multiple_of(g * rows, 8), rows)
    core_rows = pl.ds(pl.multiple_of(core * (2 * rows), 8), 2 * rows)

    def y_copy(slot):
        place = full.at[slot, own_rows, :]
        return remote(place, place, y_sems, slot, (s, core, 1 - y))

    def core_copy(slot):
        place = full.at[slot, core_rows, :]
        return remote(place, place, core_sems, slot, (s, 1 - core, y))

    def load(slot):
        return pltpu.make_async_copy(
            border_ref.at[pl.ds(slot * order, order), :], loaded, load_sem
        )

    far_copy = remote(border_ref, far_ref, far_sems, 0, (s, 1 - core, y))
    strip_width = strip_ref.shape[1] // 2
    cuts = [(0, order // 2), (order // 2, slots * order - order // 2)]
    strip_copies = [
        [
            remote(
                border_ref.at[pl.ds(low, count), pl.ds(p * half, strip_width)],
                strip_ref.at[pl.ds(low, count), pl.ds(p * strip_width, strip_width)],
                strip_sems,
                2 * index + p,
                group_peer(groups - 1),
            )
            for p in range(2)
        ]
        for index, (low, count) in enumerate(cuts)
    ]

    swap_copy(0).start()
    load(0).start()
    for copy in strip_copies[0]:
        copy.start()

    def select_rows(slot):
        swap_copy(slot).wait_recv()
        if slot + 1 < slots:
            swap_copy(slot + 1).start()
        same = assignment_ref[slot] == s * slots + slot
        full[slot, own_rows, :] = jnp.where(same, kkt_ref[slot], swap[slot])
        y_copy(slot).start()

    select_rows(0)
    select_rows(1)
    y_copy(0).wait_recv()
    core_copy(0).start()
    far_copy.start()

    def eye_at(start):
        row = lax.broadcasted_iota(jnp.int32, (step, order), 0) + start
        return row == lax.broadcasted_iota(jnp.int32, (step, order), 1)

    @pl.loop(0, slots)
    def _(slot):
        core_copy(slot).wait_recv()
        col_diag = jnp.zeros((1, order), jnp.float32)
        for start in range(0, order, step):
            spot = pl.ds(start, step)
            block = full[slot, spot, :]
            eye = eye_at(start)
            diag = jnp.where(eye, block, 0.0)
            col_diag = col_diag + jnp.sum(diag, axis=0, keepdims=True)
            scale = 1.0 / jnp.sum(diag, axis=1, keepdims=True)
            scaled = jnp.where(eye, 0.0, -scale * block)
            head[spot, :] = scaled
            high, low = parts(scaled)
            e_hi[spot, :] = high
            e_lo[spot, :] = low
        col_inv = 1.0 / col_diag

        @pl.loop(0, order // step)
        def _(chunk):
            spot = pl.ds(pl.multiple_of(chunk * step, step), step)
            high = e_hi[spot, :]
            value = dot(high, e_hi[...]) + dot(high, e_lo[...]) + dot(e_lo[spot, :], e_hi[...])
            head[spot, :] += value
            high, low = parts(value)
            m_hi[spot, :] = high
            m_lo[spot, :] = low

        @pl.loop(0, order // step)
        def _(chunk):
            start = pl.multiple_of(chunk * step, step)
            spot = pl.ds(start, step)
            high = e_hi[spot, :]
            value = dot(high, m_hi[...]) + dot(high, m_lo[...]) + dot(e_lo[spot, :], m_hi[...])
            head[spot, :] += value + jnp.where(eye_at(start), 1.0, 0.0)
            p_hi[spot, :] = dot(m_hi[spot, :], m_hi[...]).astype(jnp.bfloat16)

        @pl.loop(0, order // step)
        def _(chunk):
            spot = pl.ds(pl.multiple_of(chunk * step, step), step)
            value = head[spot, :]
            value = (value + dot(value.astype(jnp.bfloat16), p_hi[...])) * col_inv
            high, low = parts(value)
            z_hi[spot, :] = high
            z_lo[spot, :] = low

        here = pl.ds(pl.multiple_of(slot * order, step), order)
        load(slot).wait()

        @pl.loop(0, width // step)
        def _(chunk):
            spot = pl.ds(pl.multiple_of(chunk * step, step), step)
            high, low = parts(loaded[:, spot])
            b_hi[here, spot] = high
            b_lo[here, spot] = low
            high, low = parts(dot(z_hi[...], high) + dot(z_hi[...], low) + dot(z_lo[...], high))
            x_hi[here, spot] = high
            x_lo[here, spot] = low

        @pl.when(slot < slots - 1)
        def _():
            load(slot + 1).start()

        for done in range(slots - 1):

            @pl.when(slot == done)
            def _():
                if done + 2 < slots:
                    select_rows(done + 2)
                y_copy(done + 1).wait_recv()
                core_copy(done + 1).start()
                if done + 2 == slots:
                    for copy in strip_copies[1]:
                        copy.start()

    x = lax.rem(s, 2)

    def own_tile(parity, tile):
        spot = pl.ds(pl.multiple_of(parity * half + tile * step, step), step)
        high, low = b_hi[:, spot], b_lo[:, spot]
        to = pl.ds(tile * step, step)

        @pl.loop(0, width // step)
        def _(chunk):
            cols = pl.ds(pl.multiple_of(chunk * step, step), step)
            x_high, x_low = x_hi[:, cols], x_lo[:, cols]
            own_tiles[parity, to, cols] = (
                dot_rows(high, x_high) + dot_rows(high, x_low) + dot_rows(low, x_high)
            )

    own_copy = remote(own_tiles.at[1 - x], own_ref, own_sems, 0, (flip_x, core, y))

    left = lax.rem(panel_ref[0], 2) == 0
    owns = core == (panel_ref[0] // 2) // 2
    row = lax.broadcasted_iota(jnp.int32, (step, panel_width), 0)
    col = lax.broadcasted_iota(jnp.int32, (step, panel_width), 1)
    x_high = jnp.where(left, x_hi[:, :half], x_hi[:, half:])
    x_low = jnp.where(left, x_lo[:, :half], x_lo[:, half:])
    for start in range(0, panel_width, step):
        low_side = slice(start, start + step)
        high_side = slice(half + start, half + start + step)
        high = jnp.where(left, b_hi[:, low_side], b_hi[:, high_side])
        low = jnp.where(left, b_lo[:, low_side], b_lo[:, high_side])
        value = dot_rows(high, x_high) + dot_rows(high, x_low) + dot_rows(low, x_high)
        value = value + jnp.where(row + start == col, extra_ref[...], 0.0)
        share[low_side, :] = jnp.where(owns, value, 0.0)
    core_half = panel_width // 2
    part_rows = core_half // S

    def part_at(index):
        return pl.ds(pl.multiple_of(core * core_half + index * part_rows, 8), part_rows)

    deal = remote(
        share.at[pl.ds(pl.multiple_of((1 - core) * core_half, 8), core_half), :],
        from_core,
        deal_sems,
        0,
        (s, 1 - core, y),
    )

    def reduce_copy(shift):
        to = lax.rem(s + shift, S)
        return remote(
            share.at[part_at(to), :],
            from_scen.at[shift - 1],
            scen_sems,
            shift - 1,
            scen_peer(shift),
        )

    deal.start()
    own_tile(1 - x, 0)
    deal.wait()
    share[pl.ds(pl.multiple_of(core * core_half, 8), core_half), :] += from_core[...]
    for shift in range(1, S):
        reduce_copy(shift).start()
    own_tile(1 - x, 1)
    own_copy.start()
    own_tile(x, 0)
    own_tile(x, 1)
    value = share[part_at(s), :]
    for shift in range(1, S):
        reduce_copy(shift).wait_recv()
        value = value + from_scen[shift - 1]
    part_ref[...] = value
    for shift in range(1, S):
        reduce_copy(shift).wait_send()
    own_copy.wait()
    own_ref[...] += own_tiles[x]
    for slot in range(slots):
        swap_copy(slot).wait_send()
        y_copy(slot).wait_send()
        core_copy(slot).wait_send()
    far_copy.wait()
    for copies in strip_copies:
        for copy in copies:
            copy.wait()


def head_call(assignment, panel, extra, kkt, flat, strip_width):
    slots, rows, order = kkt.shape
    depth, width = flat.shape
    S = lax.axis_size("scen")
    f32, bf16 = jnp.float32, jnp.bfloat16
    vmem = pl.BlockSpec(memory_space=pltpu.VMEM)
    smem = pl.BlockSpec(memory_space=pltpu.SMEM)
    hbm = pl.BlockSpec(memory_space=pl.ANY)

    def sems(count):
        return pltpu.SemaphoreType.DMA((2, count))

    return pl.pallas_call(
        head_kernel,
        in_specs=[smem, smem, vmem, vmem, hbm],
        out_specs=[vmem, vmem, vmem, vmem, hbm, hbm],
        out_shape=[
            jax.ShapeDtypeStruct((depth, width), bf16),
            jax.ShapeDtypeStruct((depth, width), bf16),
            jax.ShapeDtypeStruct((PW, width), f32),
            jax.ShapeDtypeStruct((PW // 2 // S, PW), f32),
            jax.ShapeDtypeStruct((depth, width), f32),
            jax.ShapeDtypeStruct((depth, strip_width), f32),
        ],
        scratch_shapes=[
            pltpu.VMEM((2, PW, width), f32),
            pltpu.VMEM((PW, PW), f32),
            pltpu.VMEM((PW // 2, PW), f32),
            pltpu.VMEM((S - 1, PW // 2 // S, PW), f32),
            pltpu.VMEM((slots, rows, order), f32),
            pltpu.VMEM((slots, order, order), f32),
            pltpu.VMEM((order, width), f32),
            pltpu.VMEM((depth, width), bf16),
            pltpu.VMEM((depth, width), bf16),
        ]
        + [pltpu.VMEM((order, order), bf16)] * 7
        + [
            pltpu.VMEM((order, order), f32),
            pltpu.SemaphoreType.DMA,
            sems(1),
            sems(slots),
            sems(slots),
            sems(slots),
            sems(1),
            sems(4),
            sems(S - 1),
            sems(1),
        ],
        compiler_params=pltpu.CompilerParams(
            collective_id=0, has_side_effects=True, vmem_limit_bytes=60 * 1024 * 1024
        ),
        cost_estimate=pl.CostEstimate(
            flops=2 * slots * order * order * (8 * order + 3 * width) + 6 * depth * width * width,
            bytes_accessed=4 * depth * width * 3,
            transcendentals=0,
        ),
    )(assignment, panel, extra, kkt, flat)


def factor_block(s_ref, w_ref):
    size = s_ref.shape[0]
    pivots = 4
    row = lax.broadcasted_iota(jnp.int32, (size, size), 0)
    lane = lax.broadcasted_iota(jnp.int32, (size, size), 1)
    thin = lax.broadcasted_iota(jnp.int32, (1, size), 1)
    tall = lax.broadcasted_iota(jnp.int32, (size, 1), 0)
    w_ref[...] = jnp.where(row == lane, 1.0, 0.0)

    @pl.loop(0, size // pivots)
    def _(block):
        j = block * pivots
        whole = s_ref[...]
        rows = [s_ref[pl.ds(j + p, 1), :] for p in range(pivots)]
        tails = [w_ref[pl.ds(j + p, 1), :] for p in range(pivots)]
        cols = [
            jnp.sum(jnp.where(lane == j + p, whole, 0.0), axis=1, keepdims=True)
            for p in range(pivots)
        ]
        small = [
            [
                jnp.sum(jnp.where(thin == j + q, rows[p], 0.0), axis=1, keepdims=True)
                for q in range(p, pivots)
            ]
            for p in range(pivots)
        ]
        entry = lambda q, p: small[p][q - p]
        lower = {}
        tails_new, rows_new, cols_new = [], [], []
        for p in range(pivots):
            value = entry(p, p)
            for q in range(p):
                value = value - lower[p, q] * lower[p, q]
            root = lax.rsqrt(value)
            root = root * (1.5 - 0.5 * value * root * root)
            for i in range(p + 1, pivots):
                below = entry(i, p)
                for q in range(p):
                    below = below - lower[i, q] * lower[p, q]
                lower[i, p] = below * root
            u, c, v = rows[p], cols[p], tails[p]
            for q in range(p):
                u = u - lower[p, q] * rows_new[q]
                c = c - lower[p, q] * cols_new[q]
                v = v - lower[p, q] * tails_new[q]
            rows_new.append(u * root)
            cols_new.append(c * root)
            tails_new.append(v * root)
        change = jnp.zeros((size, size), jnp.float32)
        other = jnp.zeros((size, size), jnp.float32)
        for p in range(pivots):
            c = jnp.where(tall >= j + pivots, cols_new[p], 0.0)
            change = change + c * rows_new[p]
            other = other + c * tails_new[p]
        s_ref[...] = whole - change
        w_ref[...] = w_ref[...] - other
        for p in range(pivots):
            w_ref[pl.ds(j + p, 1), :] = tails_new[p]


def exact(left, right, axes=((1,), (0,))):
    return lax.dot_general(
        left,
        right,
        (axes, ((), ())),
        precision=lax.Precision.HIGHEST,
        preferred_element_type=jnp.float32,
    )


def tail_kernel(
    panel_ref,
    diag_ref,
    x_hi,
    x_lo,
    own_in,
    part_ref,
    border_ref,
    far_ref,
    early_ref,
    out_ref,
    factor_ref,
    late_ref,
    stage,
    lt_hi,
    lt_lo,
    far_tile,
    from_x_far,
    far_turned,
    cross,
    from_x,
    turned,
    own_acc,
    own_z,
    far_z,
    cross_z,
    work,
    inverse,
    s_ref,
    w_ref,
    dealt,
    from_group,
    block,
    spread_sems,
    whole_sems,
    stage_sems,
    late_sems,
    far_x_sems,
    x_sems,
    own_z_sems,
    far_z_sems,
    cross_z_sems,
    turn_send,
    turn_recv,
    far_turn_sems,
    deal_sems,
):
    depth, width = x_hi.shape
    half = width // 2
    groups = dealt.shape[0]
    strips = cross.shape[0]
    thick = cross.shape[1] // 2
    early = early_ref.shape[1] // (2 * thick)
    step = 256
    s = lax.axis_index("scen")
    core = lax.axis_index("row")
    y = lax.axis_index("col")
    S = lax.axis_size("scen")
    g = core * 2 + y
    x = lax.rem(s, 2)
    z = s // 2
    flip_x = s + 1 - 2 * x
    MESH = pl.DeviceIdType.MESH

    def group_peer(shift):
        to = lax.rem(g + shift, groups)
        return (s, to // 2, lax.rem(to, 2))

    def mirror(parity):
        return (2 * g + parity, z // 2, lax.rem(z, 2))

    barrier = pltpu.get_barrier_semaphore()
    for shift in range(1, groups):
        pl.semaphore_signal(barrier, inc=1, device_id=group_peer(shift), device_id_type=MESH)
    for shift in range(1, S):
        pl.semaphore_signal(
            barrier, inc=1, device_id=(lax.rem(s + shift, S), core, y), device_id_type=MESH
        )

    @pl.when(z != g)
    def _():
        for parity in range(2):
            pl.semaphore_signal(barrier, inc=1, device_id=mirror(parity), device_id_type=MESH)
        pl.semaphore_wait(barrier, groups + S)

    @pl.when(z == g)
    def _():
        pl.semaphore_wait(barrier, groups + S - 2)

    def remote(source, target, send, recv, device):
        return pltpu.make_async_remote_copy(
            src_ref=source,
            dst_ref=target,
            send_sem=send,
            recv_sem=recv,
            device_id=device,
            device_id_type=MESH,
        )

    class Plane:
        def __init__(self, value, first, second, sems, base, shift):
            self.value, self.first, self.second = value, first, second
            self.target = lax.rem(g + shift, groups)
            low = z - lax.rem(z, 2)
            self.keeper = jnp.minimum(jnp.maximum(self.target, low), low + 1)
            self.one = remote(
                value, first, sems.at[base], sems.at[base + 1], (self.keeper * 2 + x, core, y)
            )
            self.two = remote(
                value, second, sems.at[base + 2], sems.at[base + 3], (self.target * 2 + x, core, y)
            )

        def send(self):
            @pl.when(z != self.keeper)
            def _():
                self.one.start()

        def pass_on(self):
            @pl.when(z == self.keeper)
            def _():
                self.one.wait_recv()
                self.value[...] += self.first[...]

                @pl.when(z != self.target)
                def _():
                    self.two.start()

        def take(self):
            self.two.wait_recv()
            self.value[...] += self.second[...]

        def finish(self):
            @pl.when(z != self.keeper)
            def _():
                self.one.wait_send()

            @pl.when((z == self.keeper) & (z != self.target))
            def _():
                self.two.wait_send()

    def late_copy(strip, parity):
        return remote(
            border_ref.at[:, pl.ds(parity * half + strip * thick, thick)],
            late_ref.at[:, pl.ds(((strip - early) * 2 + parity) * thick, thick)],
            late_sems.at[0, strip - early, parity],
            late_sems.at[1, strip - early, parity],
            group_peer(groups - 1),
        )

    own = Plane(own_acc, own_z.at[0], own_z.at[1], own_z_sems, 0, 0)
    own_acc[...] = own_in[...]
    own.send()
    part_rows = part_ref.shape[0]
    core_half = block.shape[0] // 2
    own_part = pl.ds(pl.multiple_of(core * core_half + s * part_rows, 8), part_rows)
    block[own_part, :] = part_ref[...]

    def spread_copy(shift):
        return remote(
            block.at[own_part, :],
            block.at[own_part, :],
            spread_sems.at[0, shift - 1],
            spread_sems.at[1, shift - 1],
            (lax.rem(s + shift, S), core, y),
        )

    half_rows = pl.ds(pl.multiple_of(core * core_half, 8), core_half)
    whole_copy = remote(
        block.at[half_rows, :],
        block.at[half_rows, :],
        whole_sems.at[0],
        whole_sems.at[1],
        (s, 1 - core, y),
    )
    for shift in range(1, S):
        spread_copy(shift).start()
    for parity in range(2):
        late_copy(early, parity).start()

    def stage_load(slot, source, start, count, part):
        return pltpu.make_async_copy(
            source.at[:, pl.ds(start, count)],
            stage.at[slot, :, pl.ds(part * count, count)],
            stage_sems.at[slot, part],
        )

    def strip_load(slot, strip, part):
        if strip < early:
            return stage_load(slot, early_ref, part * early * thick + strip * thick, thick, part)
        return stage_load(slot, late_ref, ((strip - early) * 2 + part) * thick, thick, part)

    def far_load(slot, parity, tile):
        return stage_load(
            slot, far_ref, pl.multiple_of(parity * half + tile * step, step), step, 0
        )

    def product(slot, target, base, count):
        @pl.loop(0, depth // step)
        def _(chunk):
            spot = pl.ds(pl.multiple_of(chunk * step, step), step)
            high, low = parts(stage[slot, spot, :].T)
            lt_hi[:, spot] = high
            lt_lo[:, spot] = low

        @pl.loop(0, count // step)
        def _(chunk):
            start = pl.multiple_of(chunk * step, step)
            cols = pl.ds(pl.multiple_of(base + start, step), step)
            high, low = x_hi[:, cols], x_lo[:, cols]
            target[:, pl.ds(start, step)] = (
                dot(lt_hi[...], high) + dot(lt_hi[...], low) + dot(lt_lo[...], high)
            )

    near = g < groups // 2

    def far_side(parity):
        return jnp.where(near, parity, 1 - parity)

    def far_product(slot, parity, tile):
        product(
            slot, far_tile.at[parity, pl.ds(tile * step, step), :], far_side(parity) * half, half
        )

    far_x = remote(
        far_tile.at[1 - x], from_x_far, far_x_sems.at[0], far_x_sems.at[1], (flip_x, core, y)
    )
    loads = [
        [far_load(0, 1 - x, 0)],
        [far_load(1, 1 - x, 1)],
    ]
    for strip in range(early):
        loads.append([strip_load(strip % 2, strip, part) for part in range(2)])
    for tile in range(2):
        loads.append([far_load((early + tile) % 2, x, tile)])

    def begin(index):
        for copy in loads[index]:
            copy.start()

    def ready(index):
        for copy in loads[index]:
            copy.wait()
        if index + 1 < len(loads):
            begin(index + 1)

    def kept(strip):
        return cross.at[strip, pl.ds(pl.multiple_of(x * thick, 8), thick), :]

    def cross_x(strip):
        return remote(
            cross.at[strip, pl.ds(pl.multiple_of((1 - x) * thick, 8), thick), :],
            from_x.at[strip],
            x_sems.at[0, strip],
            x_sems.at[1, strip],
            (flip_x, core, y),
        )

    planes = [
        Plane(kept(i), cross_z.at[i, 0], cross_z.at[i, 1], cross_z_sems, 4 * i, 1)
        for i in range(strips)
    ]
    far = Plane(far_tile.at[x], far_z.at[0], far_z.at[1], far_z_sems, 0, 2)

    def join_x(strip):
        cross_x(strip).wait_recv()
        kept(strip)[...] += from_x[strip]
        planes[strip].send()

    def turn(strip, parity):
        place = out_ref.at[:, pl.ds(pl.multiple_of(x * half + strip * thick, thick), thick)]
        return remote(
            turned.at[strip, parity],
            place,
            turn_send.at[strip, parity],
            turn_recv.at[strip, x],
            mirror(parity),
        )

    offset = lax.rem(z - g + groups, groups)

    def settle(strip):
        @pl.when(offset == 1)
        def _():
            planes[strip].take()
            value = kept(strip)[...]
            out_ref[pl.ds(strip * thick, thick), :] = value
            for parity in range(2):
                turned[strip, parity] = value[:, parity * half : (parity + 1) * half].T
                turn(strip, parity).start()

    mine = far_side(x)
    far_turn = remote(
        far_turned,
        out_ref.at[:, pl.ds(pl.multiple_of(x * half, half), half)],
        far_turn_sems.at[0],
        far_turn_sems.at[1],
        (2 * g + mine, z // 2, lax.rem(z, 2)),
    )

    size = s_ref.shape[0]
    count = work.shape[0] // size

    def spot(index):
        return slice(index * size, (index + 1) * size)

    def eliminate(k):
        s_ref[...] = work[spot(k), spot(k)]
        factor_block(s_ref, w_ref)
        inverse[spot(k), spot(k)] = w_ref[...]
        if k + 1 < count:
            rest = slice((k + 1) * size, count * size)
            below = exact(work[rest, spot(k)], w_ref[...], ((1,), (1,)))
            work[rest, spot(k)] = below
            work[rest, rest] = work[rest, rest] - exact(below, below, ((1,), (1,)))
        if k > 0:
            known = slice(0, k * size)
            row = exact(work[spot(k), known], inverse[known, known])
            inverse[spot(k), known] = -exact(w_ref[...], row)

    def late_strip(strip):
        for parity in range(2):
            late_copy(strip, parity).wait_recv()
            if strip + 1 < strips:
                late_copy(strip + 1, parity).start()
        for part in range(2):
            strip_load(strip % 2, strip, part).start()
        for part in range(2):
            strip_load(strip % 2, strip, part).wait()
        product(strip % 2, cross.at[strip], 0, width)
        cross_x(strip).start()

    inverse[...] = jnp.zeros(inverse.shape, jnp.float32)
    begin(0)
    for tile in range(2):
        ready(tile)
        far_product(tile, 1 - x, tile)
    far_x.start()
    for strip in range(early):
        ready(2 + strip)
        product(strip % 2, cross.at[strip], 0, width)
        cross_x(strip).start()
    for tile in range(2):
        ready(2 + early + tile)
        far_product((early + tile) % 2, x, tile)
    far_x.wait_recv()
    far_tile[x] += from_x_far[...]
    far.send()
    own.pass_on()
    for shift in range(1, S):
        spread_copy(shift).wait()
    whole_copy.start()
    for strip in range(early):
        join_x(strip)
    late_strip(early)
    whole_copy.wait()
    work[...] = 0.5 * (block[...] + block[...].T)
    eliminate(0)
    far.pass_on()
    for strip in range(early):
        planes[strip].pass_on()
    join_x(early)
    eliminate(1)

    @pl.when(offset == 0)
    def _():
        own.take()
        row = lax.broadcasted_iota(jnp.int32, (half, width), 0) + x * half
        col = lax.broadcasted_iota(jnp.int32, (half, width), 1)
        out_ref[...] = own_acc[...] + jnp.where(row == col, diag_ref[...].T, 0.0)

    @pl.when(offset == 2)
    def _():
        far.take()
        value = far_tile[x]
        out_ref[:, pl.ds(pl.multiple_of(mine * half, half), half)] = value
        far_turned[...] = value.T
        far_turn.start()

    planes[early].pass_on()
    late_strip(early + 1)
    for strip in range(early):
        settle(strip)
    eliminate(2)
    join_x(early + 1)
    settle(early)
    eliminate(3)
    planes[early + 1].pass_on()
    settle(early + 1)

    left = lax.rem(panel_ref[0], 2) == 0
    owner = panel_ref[0] // 2
    piece = dealt.shape[2]

    def deal(shift):
        return remote(
            dealt.at[lax.rem(g + shift, groups)],
            from_group.at[shift - 1],
            deal_sems.at[0, shift - 1],
            deal_sems.at[1, shift - 1],
            group_peer(shift),
        )

    def make_factor():
        columns = jnp.where(left, out_ref[:, :half], out_ref[:, half:])
        for part in range(groups):
            dealt[part] = exact(
                columns, inverse[part * piece : (part + 1) * piece, :], ((1,), (1,))
            )
        for shift in range(1, groups):
            deal(shift).start()

    @pl.when(offset == 2)
    def _():
        remote(
            far_turned,
            out_ref.at[:, pl.ds(pl.multiple_of((1 - mine) * half, half), half)],
            far_turn_sems.at[0],
            far_turn_sems.at[1],
            mirror(0),
        ).wait_recv()
        far_turn.wait_send()

    even = (offset == 0) | (offset == 2)

    @pl.when(even)
    def _():
        make_factor()

    @pl.when(offset == 3)
    def _():
        for strip in range(strips):
            for source in range(2):
                remote(
                    turned.at[strip, 0],
                    out_ref.at[:, pl.ds(source * half + strip * thick, thick)],
                    turn_send.at[strip, 0],
                    turn_recv.at[strip, source],
                    mirror(0),
                ).wait_recv()

    @pl.when(offset == 1)
    def _():
        for strip in range(strips):
            for parity in range(2):
                turn(strip, parity).wait_send()

    @pl.when(jnp.logical_not(even))
    def _():
        make_factor()

    own.finish()
    far.finish()
    far_x.wait_send()
    for strip in range(strips):
        planes[strip].finish()
        cross_x(strip).wait_send()
    for strip in range(early, strips):
        for parity in range(2):
            late_copy(strip, parity).wait_send()
    value = jnp.where(g == owner, dealt[g], 0.0)
    for shift in range(1, groups):
        deal(shift).wait_recv()
        source = lax.rem(g - shift + groups, groups)
        value = jnp.where(source == owner, from_group[shift - 1], value)
    factor_ref[...] = value
    for shift in range(1, groups):
        deal(shift).wait_send()


def tail_call(panel, first_diag, x_hi, x_lo, own, block, flat, far, early):
    depth, width = flat.shape
    half = width // 2
    G = lax.axis_size(GROUP)
    S = lax.axis_size("scen")
    f32, bf16 = jnp.float32, jnp.bfloat16
    vmem = pl.BlockSpec(memory_space=pltpu.VMEM)
    smem = pl.BlockSpec(memory_space=pltpu.SMEM)
    hbm = pl.BlockSpec(memory_space=pl.ANY)
    thick = 128
    strips = half // thick
    late = strips - early.shape[1] // (2 * thick)
    share = PW // G
    sems = pltpu.SemaphoreType.DMA
    return pl.pallas_call(
        tail_kernel,
        in_specs=[smem, vmem, vmem, vmem, vmem, vmem, hbm, hbm, hbm],
        out_specs=[vmem, vmem, hbm],
        out_shape=[
            jax.ShapeDtypeStruct((half, width), f32),
            jax.ShapeDtypeStruct((half, share), f32),
            jax.ShapeDtypeStruct((depth, late * 2 * thick), f32),
        ],
        scratch_shapes=[
            pltpu.VMEM((2, depth, 256), f32),
            pltpu.VMEM((256, depth), bf16),
            pltpu.VMEM((256, depth), bf16),
            pltpu.VMEM((2, half, half), f32),
            pltpu.VMEM((half, half), f32),
            pltpu.VMEM((half, half), f32),
            pltpu.VMEM((strips, 2 * thick, width), f32),
            pltpu.VMEM((strips, thick, width), f32),
            pltpu.VMEM((strips, 2, half, thick), f32),
            pltpu.VMEM((half, width), f32),
            pltpu.VMEM((2, half, width), f32),
            pltpu.VMEM((2, half, half), f32),
            pltpu.VMEM((strips, 2, thick, width), f32),
            pltpu.VMEM((PW, PW), f32),
            pltpu.VMEM((PW, PW), f32),
            pltpu.VMEM((128, 128), f32),
            pltpu.VMEM((128, 128), f32),
            pltpu.VMEM((G, half, share), f32),
            pltpu.VMEM((G - 1, half, share), f32),
            pltpu.VMEM((PW, PW), f32),
            sems((2, S - 1)),
            sems((2,)),
            sems((2, 2)),
            sems((2, late, 2)),
            sems((2,)),
            sems((2, strips)),
            sems((4,)),
            sems((4,)),
            sems((4 * strips,)),
            sems((strips, 2)),
            sems((strips, 2)),
            sems((2,)),
            sems((2, G - 1)),
        ],
        compiler_params=pltpu.CompilerParams(
            collective_id=1, has_side_effects=True, vmem_limit_bytes=60 * 1024 * 1024
        ),
        cost_estimate=pl.CostEstimate(
            flops=9 * depth * width * width, bytes_accessed=4 * depth * width * 3, transcendentals=0
        ),
    )(panel, first_diag[None, :], x_hi, x_lo, own, block, flat, far, early)


def folded_body(kkt, border, first_diag, assignment, panel):
    slots, order, width = border.shape
    flat = border.reshape(slots * order, width)
    extra = jnp.where(lax.axis_index("scen") == panel[0], first_diag, 0.0)[None, :]
    x_hi, x_lo, own, block, far, strip = head_call(
        assignment, panel, extra, kkt, flat, width // 2
    )
    schur, factor, _ = tail_call(panel, first_diag, x_hi, x_lo, own, block, flat, far, strip)
    return (schur, factor)


def body(kkt, border, first_diag, assignment, panel):
    groups = lax.axis_size(GROUP)
    foldable = (
        groups == 4
        and lax.axis_size("row") == 2
        and lax.axis_size("scen") == 2 * groups
        and border.shape[2] == 2 * first_diag.shape[0]
        and first_diag.shape[0] == PW
    )
    chosen = folded_body if foldable else plain_body
    return chosen(kkt, border, first_diag, assignment, panel)


def solution(mesh):
    in_specs = (
        P("scen", ("row", "col"), None),
        P("scen", None, ("row", "col")),
        P("scen"),
        P("scen"),
        P(),
    )
    out_specs = (P("scen", ("row", "col")), P("scen", ("row", "col")))
    return jax.shard_map(body, mesh=mesh, in_specs=in_specs, out_specs=out_specs, check_vma=False)
```

```python
import jax
import jax.numpy as jnp
from jax import lax
from jax.experimental import pallas as pl
from jax.experimental.pallas import tpu as pltpu
from jax.sharding import PartitionSpec as P

PW = 512
NEWTON = 3


HIGH = lax.Precision.HIGH
GROUP = ("row", "col")


def swapped(value, axis, distance):
    mask = 2**distance
    pairs = [(source, source ^ mask) for source in range(lax.axis_size(axis))]
    return lax.ppermute(value, axis, pairs)


def gathered_rows(value, axis):
    count = lax.axis_size(axis)
    index = lax.axis_index(axis)
    rows = value.shape[1]
    whole = jnp.zeros((value.shape[0], rows * count, value.shape[2]), value.dtype)
    whole = lax.dynamic_update_slice_in_dim(whole, value, index * rows, 1)
    for shift in range(1, count):
        pairs = [(source, (source + shift) % count) for source in range(count)]
        origin = lax.rem(index - shift + count, count)
        whole = lax.dynamic_update_slice_in_dim(
            whole, lax.ppermute(value, axis, pairs), origin * rows, 1
        )
    return whole


def matmul(left, right, precision=HIGH):
    return jnp.dot(left, right, precision=precision, preferred_element_type=jnp.float32)


def contract(left, right):
    return lax.dot_general(
        left, right, (((0,), (0,)), ((), ())), precision=HIGH, preferred_element_type=jnp.float32
    )


def plain_body(kkt, border, first_diag, assignment, panel):
    scen_index = lax.axis_index("scen")
    own_index = lax.axis_index(GROUP)
    group_size = lax.axis_size(GROUP)
    slots, order, col_count = border.shape
    width = col_count * group_size
    scenario_ids = scen_index * slots + jnp.arange(slots, dtype=jnp.int32)
    kkt = jnp.where((assignment == scenario_ids)[:, None, None], kkt, swapped(kkt, "scen", 0))
    kkt_all = gathered_rows(gathered_rows(kkt, "col"), "row")
    gathered = lax.all_gather(border, GROUP, axis=2, tiled=True)
    eye = jnp.eye(order, dtype=jnp.bool_)
    inverses = []
    for slot in range(slots):
        full = kkt_all[slot]
        diag = jnp.where(eye, full, 0.0)
        row_inv = 1.0 / jnp.sum(diag, axis=1, keepdims=True)
        col_inv = 1.0 / jnp.sum(diag, axis=0, keepdims=True)
        approx = jnp.where(eye, 2.0 * row_inv, 0.0) - row_inv * full * col_inv
        for step in range(NEWTON - 1):
            approx = 2.0 * approx - matmul(matmul(approx, full), approx)
        inverses.append(approx)
    solved = jnp.concatenate([matmul(inverses[slot], border[slot]) for slot in range(slots)], 0)
    border_all = gathered.reshape(slots * order, width)

    panel_start = panel[0] * PW
    share = PW // group_size
    own_start = panel_start + own_index * share

    share_solved = jnp.concatenate(
        [
            matmul(inverses[slot], lax.dynamic_slice_in_dim(gathered[slot], own_start, share, 1))
            for slot in range(slots)
        ],
        0,
    )
    panel_border = lax.dynamic_slice_in_dim(border_all, panel_start, PW, 1)
    block = contract(panel_border, share_solved)
    row_span = first_diag.shape[0]
    global_rows = scen_index * row_span + jnp.arange(row_span, dtype=jnp.int32)
    share_ids = own_start + jnp.arange(share, dtype=jnp.int32)
    owned = global_rows[:, None] == share_ids[None, :]
    share_diag = jnp.sum(jnp.where(owned, first_diag[:, None], 0.0), axis=0)
    panel_ids = panel_start + jnp.arange(PW, dtype=jnp.int32)
    block = block + jnp.where(panel_ids[:, None] == share_ids[None, :], share_diag[None, :], 0.0)
    block = lax.psum(block, "scen")
    block = lax.all_gather(block, GROUP, axis=1, tiled=True)
    symmetric = 0.5 * (block + block.T)
    lower_factor = jnp.linalg.cholesky(symmetric)
    lower_inverse = lax.linalg.triangular_solve(
        lower_factor, jnp.eye(PW, dtype=jnp.float32), left_side=True, lower=True
    )
    own_inverse = lax.dynamic_slice_in_dim(lower_inverse, own_index * share, share, 0)

    def schur_columns(start, count, solved):
        tile = contract(border_all, lax.dynamic_slice_in_dim(solved, start, count, 1))
        summed = lax.psum_scatter(tile, "scen", scatter_dimension=0, tiled=True)
        global_cols = own_index * col_count + start + jnp.arange(count, dtype=jnp.int32)
        on_diag = global_rows[:, None] == global_cols[None, :]
        return summed + jnp.where(on_diag, first_diag[:, None], 0.0)

    if col_count >= PW:
        pieces = col_count // PW
        first = lax.rem(panel[0], pieces)
        schur = jnp.zeros((row_span, col_count), jnp.float32)
        panel_rows = None
        for piece in range(pieces):
            start = lax.rem(first + piece, pieces) * PW
            columns = schur_columns(start, PW, solved)
            if piece == 0:
                owns = own_index == panel[0] // pieces
                columns, solved = lax.optimization_barrier((columns, solved))
                panel_rows = lax.psum(jnp.where(owns, columns, 0.0), GROUP)
            schur = lax.dynamic_update_slice_in_dim(schur, columns, start, 1)
    else:
        schur = schur_columns(jnp.int32(0), col_count, solved)
        parts = PW // col_count
        position = own_index - panel[0] * parts
        owns = (position >= 0) & (position < parts)
        placed = jnp.zeros((row_span, PW), jnp.float32)
        placed = lax.dynamic_update_slice_in_dim(
            placed, jnp.where(owns, schur, 0.0), jnp.clip(position, 0, parts - 1) * col_count, 1
        )
        panel_rows = lax.psum(placed, GROUP)
    own_cols = lax.dot_general(
        panel_rows,
        own_inverse,
        (((1,), (1,)), ((), ())),
        precision=lax.Precision.HIGHEST,
        preferred_element_type=jnp.float32,
    )
    return (schur, own_cols)


def parts(value):
    high = value.astype(jnp.bfloat16)
    return high, (value - high.astype(jnp.float32)).astype(jnp.bfloat16)


def dot(left, right):
    return jnp.dot(left, right, preferred_element_type=jnp.float32)


def dot_rows(left, right):
    return lax.dot_general(
        left, right, (((0,), (0,)), ((), ())), preferred_element_type=jnp.float32
    )


def head_kernel(
    assignment_ref,
    panel_ref,
    extra_ref,
    kkt_ref,
    border_ref,
    x_hi,
    x_lo,
    own_ref,
    part_ref,
    far_ref,
    strip_ref,
    own_tiles,
    share,
    from_core,
    from_scen,
    swap,
    full,
    loaded,
    b_hi,
    b_lo,
    e_hi,
    e_lo,
    m_hi,
    m_lo,
    p_hi,
    z_hi,
    z_lo,
    head,
    load_sem,
    own_sems,
    swap_sems,
    y_sems,
    core_sems,
    far_sems,
    strip_sems,
    scen_sems,
    deal_sems,
):
    slots, order, _ = full.shape
    rows = kkt_ref.shape[1]
    width = x_hi.shape[1]
    half = width // 2
    panel_width = share.shape[0]
    groups = lax.axis_size(GROUP)
    S = lax.axis_size("scen")
    step = 256
    s = lax.axis_index("scen")
    core = lax.axis_index("row")
    y = lax.axis_index("col")
    g = core * 2 + y
    flip_x = s + 1 - 2 * lax.rem(s, 2)

    def group_peer(shift):
        to = lax.rem(g + shift, groups)
        return (s, to // 2, lax.rem(to, 2))

    def scen_peer(shift):
        return (lax.rem(s + shift, S), core, y)

    barrier = pltpu.get_barrier_semaphore()
    for shift in range(1, groups):
        pl.semaphore_signal(
            barrier, inc=1, device_id=group_peer(shift), device_id_type=pl.DeviceIdType.MESH
        )
    for shift in range(1, S):
        pl.semaphore_signal(
            barrier, inc=1, device_id=scen_peer(shift), device_id_type=pl.DeviceIdType.MESH
        )
    pl.semaphore_wait(barrier, groups + S - 2)

    def remote(source, target, sems, index, device):
        return pltpu.make_async_remote_copy(
            src_ref=source,
            dst_ref=target,
            send_sem=sems.at[0, index],
            recv_sem=sems.at[1, index],
            device_id=device,
            device_id_type=pl.DeviceIdType.MESH,
        )

    def swap_copy(slot):
        return remote(kkt_ref.at[slot], swap.at[slot], swap_sems, slot, (flip_x, core, y))

    own_rows = pl.ds(pl.multiple_of(g * rows, 8), rows)
    core_rows = pl.ds(pl.multiple_of(core * (2 * rows), 8), 2 * rows)

    def y_copy(slot):
        place = full.at[slot, own_rows, :]
        return remote(place, place, y_sems, slot, (s, core, 1 - y))

    def core_copy(slot):
        place = full.at[slot, core_rows, :]
        return remote(place, place, core_sems, slot, (s, 1 - core, y))

    def load(slot):
        return pltpu.make_async_copy(
            border_ref.at[pl.ds(slot * order, order), :], loaded, load_sem
        )

    far_copy = remote(border_ref, far_ref, far_sems, 0, (s, 1 - core, y))
    strip_width = strip_ref.shape[1] // 2
    cuts = [(0, order // 2), (order // 2, slots * order - order // 2)]
    strip_copies = [
        [
            remote(
                border_ref.at[pl.ds(low, count), pl.ds(p * half, strip_width)],
                strip_ref.at[pl.ds(low, count), pl.ds(p * strip_width, strip_width)],
                strip_sems,
                2 * index + p,
                group_peer(groups - 1),
            )
            for p in range(2)
        ]
        for index, (low, count) in enumerate(cuts)
    ]

    swap_copy(0).start()
    load(0).start()
    for copy in strip_copies[0]:
        copy.start()

    def select_rows(slot):
        swap_copy(slot).wait_recv()
        if slot + 1 < slots:
            swap_copy(slot + 1).start()
        same = assignment_ref[slot] == s * slots + slot
        full[slot, own_rows, :] = jnp.where(same, kkt_ref[slot], swap[slot])
        y_copy(slot).start()

    select_rows(0)
    select_rows(1)
    y_copy(0).wait_recv()
    core_copy(0).start()
    far_copy.start()

    def eye_at(start):
        row = lax.broadcasted_iota(jnp.int32, (step, order), 0) + start
        return row == lax.broadcasted_iota(jnp.int32, (step, order), 1)

    @pl.loop(0, slots)
    def _(slot):
        core_copy(slot).wait_recv()
        col_diag = jnp.zeros((1, order), jnp.float32)
        for start in range(0, order, step):
            spot = pl.ds(start, step)
            block = full[slot, spot, :]
            eye = eye_at(start)
            diag = jnp.where(eye, block, 0.0)
            col_diag = col_diag + jnp.sum(diag, axis=0, keepdims=True)
            scale = 1.0 / jnp.sum(diag, axis=1, keepdims=True)
            scaled = jnp.where(eye, 0.0, -scale * block)
            head[spot, :] = scaled
            high, low = parts(scaled)
            e_hi[spot, :] = high
            e_lo[spot, :] = low
        col_inv = 1.0 / col_diag

        @pl.loop(0, order // step)
        def _(chunk):
            spot = pl.ds(pl.multiple_of(chunk * step, step), step)
            high = e_hi[spot, :]
            value = dot(high, e_hi[...]) + dot(high, e_lo[...]) + dot(e_lo[spot, :], e_hi[...])
            head[spot, :] += value
            high, low = parts(value)
            m_hi[spot, :] = high
            m_lo[spot, :] = low

        @pl.loop(0, order // step)
        def _(chunk):
            start = pl.multiple_of(chunk * step, step)
            spot = pl.ds(start, step)
            high = e_hi[spot, :]
            value = dot(high, m_hi[...]) + dot(high, m_lo[...]) + dot(e_lo[spot, :], m_hi[...])
            head[spot, :] += value + jnp.where(eye_at(start), 1.0, 0.0)
            p_hi[spot, :] = dot(m_hi[spot, :], m_hi[...]).astype(jnp.bfloat16)

        @pl.loop(0, order // step)
        def _(chunk):
            spot = pl.ds(pl.multiple_of(chunk * step, step), step)
            value = head[spot, :]
            value = (value + dot(value.astype(jnp.bfloat16), p_hi[...])) * col_inv
            high, low = parts(value)
            z_hi[spot, :] = high
            z_lo[spot, :] = low

        here = pl.ds(pl.multiple_of(slot * order, step), order)
        load(slot).wait()

        @pl.loop(0, width // step)
        def _(chunk):
            spot = pl.ds(pl.multiple_of(chunk * step, step), step)
            high, low = parts(loaded[:, spot])
            b_hi[here, spot] = high
            b_lo[here, spot] = low
            high, low = parts(dot(z_hi[...], high) + dot(z_hi[...], low) + dot(z_lo[...], high))
            x_hi[here, spot] = high
            x_lo[here, spot] = low

        @pl.when(slot < slots - 1)
        def _():
            load(slot + 1).start()

        for done in range(slots - 1):

            @pl.when(slot == done)
            def _():
                if done + 2 < slots:
                    select_rows(done + 2)
                y_copy(done + 1).wait_recv()
                core_copy(done + 1).start()
                if done + 2 == slots:
                    for copy in strip_copies[1]:
                        copy.start()

    x = lax.rem(s, 2)

    def own_tile(parity, tile):
        spot = pl.ds(pl.multiple_of(parity * half + tile * step, step), step)
        high, low = b_hi[:, spot], b_lo[:, spot]
        to = pl.ds(tile * step, step)

        @pl.loop(0, width // step)
        def _(chunk):
            cols = pl.ds(pl.multiple_of(chunk * step, step), step)
            x_high, x_low = x_hi[:, cols], x_lo[:, cols]
            own_tiles[parity, to, cols] = (
                dot_rows(high, x_high) + dot_rows(high, x_low) + dot_rows(low, x_high)
            )

    own_copies = [
        remote(
            own_tiles.at[1 - x, pl.ds(tile * step, step), :],
            own_ref.at[pl.ds(tile * step, step), :],
            own_sems,
            tile,
            (flip_x, core, y),
        )
        for tile in range(half // step)
    ]
    for tile, copy in enumerate(own_copies):
        own_tile(1 - x, tile)
        copy.start()

    left = lax.rem(panel_ref[0], 2) == 0
    owns = core == (panel_ref[0] // 2) // 2
    row = lax.broadcasted_iota(jnp.int32, (step, panel_width), 0)
    col = lax.broadcasted_iota(jnp.int32, (step, panel_width), 1)
    x_high = jnp.where(left, x_hi[:, :half], x_hi[:, half:])
    x_low = jnp.where(left, x_lo[:, :half], x_lo[:, half:])
    for start in range(0, panel_width, step):
        low_side = slice(start, start + step)
        high_side = slice(half + start, half + start + step)
        high = jnp.where(left, b_hi[:, low_side], b_hi[:, high_side])
        low = jnp.where(left, b_lo[:, low_side], b_lo[:, high_side])
        value = dot_rows(high, x_high) + dot_rows(high, x_low) + dot_rows(low, x_high)
        value = value + jnp.where(row + start == col, extra_ref[...], 0.0)
        share[low_side, :] = jnp.where(owns, value, 0.0)
    core_half = panel_width // 2
    part_rows = core_half // S

    def part_at(index):
        return pl.ds(pl.multiple_of(core * core_half + index * part_rows, 8), part_rows)

    deal = remote(
        share.at[pl.ds(pl.multiple_of((1 - core) * core_half, 8), core_half), :],
        from_core,
        deal_sems,
        0,
        (s, 1 - core, y),
    )

    def reduce_copy(shift):
        to = lax.rem(s + shift, S)
        return remote(
            share.at[part_at(to), :],
            from_scen.at[shift - 1],
            scen_sems,
            shift - 1,
            scen_peer(shift),
        )

    deal.start()
    own_tile(x, 0)
    deal.wait()
    share[pl.ds(pl.multiple_of(core * core_half, 8), core_half), :] += from_core[...]
    for shift in range(1, S):
        reduce_copy(shift).start()
    own_tile(x, 1)
    value = share[part_at(s), :]
    for shift in range(1, S):
        reduce_copy(shift).wait_recv()
        value = value + from_scen[shift - 1]
    part_ref[...] = value
    for shift in range(1, S):
        reduce_copy(shift).wait_send()
    for copy in own_copies:
        copy.wait()
    own_ref[...] += own_tiles[x]
    for slot in range(slots):
        swap_copy(slot).wait_send()
        y_copy(slot).wait_send()
        core_copy(slot).wait_send()
    far_copy.wait()
    for copies in strip_copies:
        for copy in copies:
            copy.wait()


def head_call(assignment, panel, extra, kkt, flat, strip_width):
    slots, rows, order = kkt.shape
    depth, width = flat.shape
    S = lax.axis_size("scen")
    f32, bf16 = jnp.float32, jnp.bfloat16
    vmem = pl.BlockSpec(memory_space=pltpu.VMEM)
    smem = pl.BlockSpec(memory_space=pltpu.SMEM)
    hbm = pl.BlockSpec(memory_space=pl.ANY)

    def sems(count):
        return pltpu.SemaphoreType.DMA((2, count))

    return pl.pallas_call(
        head_kernel,
        in_specs=[smem, smem, vmem, vmem, hbm],
        out_specs=[vmem, vmem, vmem, vmem, hbm, hbm],
        out_shape=[
            jax.ShapeDtypeStruct((depth, width), bf16),
            jax.ShapeDtypeStruct((depth, width), bf16),
            jax.ShapeDtypeStruct((PW, width), f32),
            jax.ShapeDtypeStruct((PW // 2 // S, PW), f32),
            jax.ShapeDtypeStruct((depth, width), f32),
            jax.ShapeDtypeStruct((depth, strip_width), f32),
        ],
        scratch_shapes=[
            pltpu.VMEM((2, PW, width), f32),
            pltpu.VMEM((PW, PW), f32),
            pltpu.VMEM((PW // 2, PW), f32),
            pltpu.VMEM((S - 1, PW // 2 // S, PW), f32),
            pltpu.VMEM((slots, rows, order), f32),
            pltpu.VMEM((slots, order, order), f32),
            pltpu.VMEM((order, width), f32),
            pltpu.VMEM((depth, width), bf16),
            pltpu.VMEM((depth, width), bf16),
        ]
        + [pltpu.VMEM((order, order), bf16)] * 7
        + [
            pltpu.VMEM((order, order), f32),
            pltpu.SemaphoreType.DMA,
            sems(2),
            sems(slots),
            sems(slots),
            sems(slots),
            sems(1),
            sems(4),
            sems(S - 1),
            sems(1),
        ],
        compiler_params=pltpu.CompilerParams(
            collective_id=0, has_side_effects=True, vmem_limit_bytes=60 * 1024 * 1024
        ),
        cost_estimate=pl.CostEstimate(
            flops=2 * slots * order * order * (8 * order + 3 * width) + 6 * depth * width * width,
            bytes_accessed=4 * depth * width * 3,
            transcendentals=0,
        ),
    )(assignment, panel, extra, kkt, flat)


def factor_block(s_ref, w_ref):
    size = s_ref.shape[0]
    pivots = 4
    row = lax.broadcasted_iota(jnp.int32, (size, size), 0)
    lane = lax.broadcasted_iota(jnp.int32, (size, size), 1)
    thin = lax.broadcasted_iota(jnp.int32, (1, size), 1)
    tall = lax.broadcasted_iota(jnp.int32, (size, 1), 0)
    w_ref[...] = jnp.where(row == lane, 1.0, 0.0)

    @pl.loop(0, size // pivots)
    def _(block):
        j = block * pivots
        whole = s_ref[...]
        rows = [s_ref[pl.ds(j + p, 1), :] for p in range(pivots)]
        tails = [w_ref[pl.ds(j + p, 1), :] for p in range(pivots)]
        cols = [
            jnp.sum(jnp.where(lane == j + p, whole, 0.0), axis=1, keepdims=True)
            for p in range(pivots)
        ]
        small = [
            [
                jnp.sum(jnp.where(thin == j + q, rows[p], 0.0), axis=1, keepdims=True)
                for q in range(p, pivots)
            ]
            for p in range(pivots)
        ]
        entry = lambda q, p: small[p][q - p]
        lower = {}
        tails_new, rows_new, cols_new = [], [], []
        for p in range(pivots):
            value = entry(p, p)
            for q in range(p):
                value = value - lower[p, q] * lower[p, q]
            root = lax.rsqrt(value)
            root = root * (1.5 - 0.5 * value * root * root)
            for i in range(p + 1, pivots):
                below = entry(i, p)
                for q in range(p):
                    below = below - lower[i, q] * lower[p, q]
                lower[i, p] = below * root
            u, c, v = rows[p], cols[p], tails[p]
            for q in range(p):
                u = u - lower[p, q] * rows_new[q]
                c = c - lower[p, q] * cols_new[q]
                v = v - lower[p, q] * tails_new[q]
            rows_new.append(u * root)
            cols_new.append(c * root)
            tails_new.append(v * root)
        change = jnp.zeros((size, size), jnp.float32)
        other = jnp.zeros((size, size), jnp.float32)
        for p in range(pivots):
            c = jnp.where(tall >= j + pivots, cols_new[p], 0.0)
            change = change + c * rows_new[p]
            other = other + c * tails_new[p]
        s_ref[...] = whole - change
        w_ref[...] = w_ref[...] - other
        for p in range(pivots):
            w_ref[pl.ds(j + p, 1), :] = tails_new[p]


def exact(left, right, axes=((1,), (0,))):
    return lax.dot_general(
        left,
        right,
        (axes, ((), ())),
        precision=lax.Precision.HIGHEST,
        preferred_element_type=jnp.float32,
    )


def tail_kernel(
    panel_ref,
    diag_ref,
    x_hi,
    x_lo,
    own_in,
    part_ref,
    border_ref,
    far_ref,
    early_ref,
    out_ref,
    factor_ref,
    late_ref,
    stage,
    lt_hi,
    lt_lo,
    far_tile,
    from_x_far,
    far_turned,
    cross,
    from_x,
    turned,
    own_acc,
    own_z,
    far_z,
    cross_z,
    work,
    inverse,
    s_ref,
    w_ref,
    dealt,
    from_group,
    block,
    spread_sems,
    whole_sems,
    stage_sems,
    late_sems,
    far_x_sems,
    x_sems,
    own_z_sems,
    far_z_sems,
    cross_z_sems,
    turn_send,
    turn_recv,
    far_turn_sems,
    deal_sems,
):
    depth, width = x_hi.shape
    half = width // 2
    groups = dealt.shape[0]
    strips = cross.shape[0]
    thick = cross.shape[1] // 2
    early = early_ref.shape[1] // (2 * thick)
    step = 256
    s = lax.axis_index("scen")
    core = lax.axis_index("row")
    y = lax.axis_index("col")
    S = lax.axis_size("scen")
    g = core * 2 + y
    x = lax.rem(s, 2)
    z = s // 2
    flip_x = s + 1 - 2 * x
    MESH = pl.DeviceIdType.MESH

    def group_peer(shift):
        to = lax.rem(g + shift, groups)
        return (s, to // 2, lax.rem(to, 2))

    def mirror(parity):
        return (2 * g + parity, z // 2, lax.rem(z, 2))

    barrier = pltpu.get_barrier_semaphore()
    for shift in range(1, groups):
        pl.semaphore_signal(barrier, inc=1, device_id=group_peer(shift), device_id_type=MESH)
    for shift in range(1, S):
        pl.semaphore_signal(
            barrier, inc=1, device_id=(lax.rem(s + shift, S), core, y), device_id_type=MESH
        )

    @pl.when(z != g)
    def _():
        for parity in range(2):
            pl.semaphore_signal(barrier, inc=1, device_id=mirror(parity), device_id_type=MESH)
        pl.semaphore_wait(barrier, groups + S)

    @pl.when(z == g)
    def _():
        pl.semaphore_wait(barrier, groups + S - 2)

    def remote(source, target, send, recv, device):
        return pltpu.make_async_remote_copy(
            src_ref=source,
            dst_ref=target,
            send_sem=send,
            recv_sem=recv,
            device_id=device,
            device_id_type=MESH,
        )

    class Plane:
        def __init__(self, value, first, second, sems, base, shift):
            self.value, self.first, self.second = value, first, second
            self.target = lax.rem(g + shift, groups)
            low = z - lax.rem(z, 2)
            self.keeper = jnp.minimum(jnp.maximum(self.target, low), low + 1)
            self.one = remote(
                value, first, sems.at[base], sems.at[base + 1], (self.keeper * 2 + x, core, y)
            )
            self.two = remote(
                value, second, sems.at[base + 2], sems.at[base + 3], (self.target * 2 + x, core, y)
            )

        def send(self):
            @pl.when(z != self.keeper)
            def _():
                self.one.start()

        def pass_on(self):
            @pl.when(z == self.keeper)
            def _():
                self.one.wait_recv()
                self.value[...] += self.first[...]

                @pl.when(z != self.target)
                def _():
                    self.two.start()

        def take(self):
            self.two.wait_recv()
            self.value[...] += self.second[...]

        def finish(self):
            @pl.when(z != self.keeper)
            def _():
                self.one.wait_send()

            @pl.when((z == self.keeper) & (z != self.target))
            def _():
                self.two.wait_send()

    def late_copy(strip, parity):
        return remote(
            border_ref.at[:, pl.ds(parity * half + strip * thick, thick)],
            late_ref.at[:, pl.ds(((strip - early) * 2 + parity) * thick, thick)],
            late_sems.at[0, strip - early, parity],
            late_sems.at[1, strip - early, parity],
            group_peer(groups - 1),
        )

    own = Plane(own_acc, own_z.at[0], own_z.at[1], own_z_sems, 0, 0)
    own_acc[...] = own_in[...]
    own.send()
    part_rows = part_ref.shape[0]
    core_half = block.shape[0] // 2
    own_part = pl.ds(pl.multiple_of(core * core_half + s * part_rows, 8), part_rows)
    block[own_part, :] = part_ref[...]

    def spread_copy(shift):
        return remote(
            block.at[own_part, :],
            block.at[own_part, :],
            spread_sems.at[0, shift - 1],
            spread_sems.at[1, shift - 1],
            (lax.rem(s + shift, S), core, y),
        )

    half_rows = pl.ds(pl.multiple_of(core * core_half, 8), core_half)
    whole_copy = remote(
        block.at[half_rows, :],
        block.at[half_rows, :],
        whole_sems.at[0],
        whole_sems.at[1],
        (s, 1 - core, y),
    )
    for shift in range(1, S):
        spread_copy(shift).start()
    for parity in range(2):
        late_copy(early, parity).start()

    def stage_load(slot, source, start, count, part):
        return pltpu.make_async_copy(
            source.at[:, pl.ds(start, count)],
            stage.at[slot, :, pl.ds(part * count, count)],
            stage_sems.at[slot, part],
        )

    def strip_load(slot, strip, part):
        if strip < early:
            return stage_load(slot, early_ref, part * early * thick + strip * thick, thick, part)
        return stage_load(slot, late_ref, ((strip - early) * 2 + part) * thick, thick, part)

    def far_load(slot, parity, tile):
        return stage_load(
            slot, far_ref, pl.multiple_of(parity * half + tile * step, step), step, 0
        )

    def product(slot, target, base, count):
        @pl.loop(0, depth // step)
        def _(chunk):
            spot = pl.ds(pl.multiple_of(chunk * step, step), step)
            high, low = parts(stage[slot, spot, :].T)
            lt_hi[:, spot] = high
            lt_lo[:, spot] = low

        @pl.loop(0, count // step)
        def _(chunk):
            start = pl.multiple_of(chunk * step, step)
            cols = pl.ds(pl.multiple_of(base + start, step), step)
            high, low = x_hi[:, cols], x_lo[:, cols]
            target[:, pl.ds(start, step)] = (
                dot(lt_hi[...], high) + dot(lt_hi[...], low) + dot(lt_lo[...], high)
            )

    near = g < groups // 2

    def far_side(parity):
        return jnp.where(near, parity, 1 - parity)

    def far_product(slot, parity, tile):
        product(
            slot, far_tile.at[parity, pl.ds(tile * step, step), :], far_side(parity) * half, half
        )

    far_x = remote(
        far_tile.at[1 - x], from_x_far, far_x_sems.at[0], far_x_sems.at[1], (flip_x, core, y)
    )
    loads = [
        [far_load(0, 1 - x, 0)],
        [far_load(1, 1 - x, 1)],
    ]
    for strip in range(early):
        loads.append([strip_load(strip % 2, strip, part) for part in range(2)])
    for tile in range(2):
        loads.append([far_load((early + tile) % 2, x, tile)])

    def begin(index):
        for copy in loads[index]:
            copy.start()

    def ready(index):
        for copy in loads[index]:
            copy.wait()
        if index + 1 < len(loads):
            begin(index + 1)

    def kept(strip):
        return cross.at[strip, pl.ds(pl.multiple_of(x * thick, 8), thick), :]

    def cross_x(strip):
        return remote(
            cross.at[strip, pl.ds(pl.multiple_of((1 - x) * thick, 8), thick), :],
            from_x.at[strip],
            x_sems.at[0, strip],
            x_sems.at[1, strip],
            (flip_x, core, y),
        )

    planes = [
        Plane(kept(i), cross_z.at[i, 0], cross_z.at[i, 1], cross_z_sems, 4 * i, 1)
        for i in range(strips)
    ]
    far = Plane(far_tile.at[x], far_z.at[0], far_z.at[1], far_z_sems, 0, 2)

    def join_x(strip):
        cross_x(strip).wait_recv()
        kept(strip)[...] += from_x[strip]
        planes[strip].send()

    def turn(strip, parity):
        place = out_ref.at[:, pl.ds(pl.multiple_of(x * half + strip * thick, thick), thick)]
        return remote(
            turned.at[strip, parity],
            place,
            turn_send.at[strip, parity],
            turn_recv.at[strip, x],
            mirror(parity),
        )

    offset = lax.rem(z - g + groups, groups)

    def settle(strip):
        @pl.when(offset == 1)
        def _():
            planes[strip].take()
            value = kept(strip)[...]
            out_ref[pl.ds(strip * thick, thick), :] = value
            for parity in range(2):
                turned[strip, parity] = value[:, parity * half : (parity + 1) * half].T
                turn(strip, parity).start()

    mine = far_side(x)
    far_turn = remote(
        far_turned,
        out_ref.at[:, pl.ds(pl.multiple_of(x * half, half), half)],
        far_turn_sems.at[0],
        far_turn_sems.at[1],
        (2 * g + mine, z // 2, lax.rem(z, 2)),
    )

    size = s_ref.shape[0]
    count = work.shape[0] // size

    def spot(index):
        return slice(index * size, (index + 1) * size)

    def eliminate(k):
        s_ref[...] = work[spot(k), spot(k)]
        factor_block(s_ref, w_ref)
        inverse[spot(k), spot(k)] = w_ref[...]
        if k + 1 < count:
            rest = slice((k + 1) * size, count * size)
            below = exact(work[rest, spot(k)], w_ref[...], ((1,), (1,)))
            work[rest, spot(k)] = below
            work[rest, rest] = work[rest, rest] - exact(below, below, ((1,), (1,)))
        if k > 0:
            known = slice(0, k * size)
            row = exact(work[spot(k), known], inverse[known, known])
            inverse[spot(k), known] = -exact(w_ref[...], row)

    def late_strip(strip):
        for parity in range(2):
            late_copy(strip, parity).wait_recv()
        for part in range(2):
            strip_load(strip % 2, strip, part).start()
        for part in range(2):
            strip_load(strip % 2, strip, part).wait()
        product(strip % 2, cross.at[strip], 0, width)
        cross_x(strip).start()

    inverse[...] = jnp.zeros(inverse.shape, jnp.float32)
    begin(0)
    for tile in range(2):
        ready(tile)
        far_product(tile, 1 - x, tile)
    far_x.start()
    for strip in range(early):
        ready(2 + strip)
        product(strip % 2, cross.at[strip], 0, width)
        cross_x(strip).start()
    for tile in range(2):
        ready(2 + early + tile)
        far_product((early + tile) % 2, x, tile)
    for strip in range(early + 1, strips):
        for parity in range(2):
            late_copy(strip, parity).start()
    far_x.wait_recv()
    far_tile[x] += from_x_far[...]
    far.send()
    own.pass_on()
    for shift in range(1, S):
        spread_copy(shift).wait()
    whole_copy.start()
    for strip in range(early):
        join_x(strip)
    late_strip(early)
    whole_copy.wait()
    work[...] = 0.5 * (block[...] + block[...].T)
    eliminate(0)
    far.pass_on()
    for strip in range(early):
        planes[strip].pass_on()
    join_x(early)
    eliminate(1)

    @pl.when(offset == 0)
    def _():
        own.take()
        row = lax.broadcasted_iota(jnp.int32, (half, width), 0) + x * half
        col = lax.broadcasted_iota(jnp.int32, (half, width), 1)
        out_ref[...] = own_acc[...] + jnp.where(row == col, diag_ref[...].T, 0.0)

    @pl.when(offset == 2)
    def _():
        far.take()
        value = far_tile[x]
        out_ref[:, pl.ds(pl.multiple_of(mine * half, half), half)] = value
        far_turned[...] = value.T
        far_turn.start()

    planes[early].pass_on()
    late_strip(early + 1)
    for strip in range(early):
        settle(strip)
    eliminate(2)
    join_x(early + 1)
    settle(early)
    eliminate(3)
    planes[early + 1].pass_on()
    settle(early + 1)

    left = lax.rem(panel_ref[0], 2) == 0
    owner = panel_ref[0] // 2
    piece = dealt.shape[2]

    def deal(shift):
        return remote(
            dealt.at[lax.rem(g + shift, groups)],
            from_group.at[shift - 1],
            deal_sems.at[0, shift - 1],
            deal_sems.at[1, shift - 1],
            group_peer(shift),
        )

    def make_factor():
        columns = jnp.where(left, out_ref[:, :half], out_ref[:, half:])
        for part in range(groups):
            dealt[part] = exact(
                columns, inverse[part * piece : (part + 1) * piece, :], ((1,), (1,))
            )
        for shift in range(1, groups):
            deal(shift).start()

    @pl.when(offset == 2)
    def _():
        remote(
            far_turned,
            out_ref.at[:, pl.ds(pl.multiple_of((1 - mine) * half, half), half)],
            far_turn_sems.at[0],
            far_turn_sems.at[1],
            mirror(0),
        ).wait_recv()
        far_turn.wait_send()

    even = (offset == 0) | (offset == 2)

    @pl.when(even)
    def _():
        make_factor()

    @pl.when(offset == 3)
    def _():
        for strip in range(strips):
            for source in range(2):
                remote(
                    turned.at[strip, 0],
                    out_ref.at[:, pl.ds(source * half + strip * thick, thick)],
                    turn_send.at[strip, 0],
                    turn_recv.at[strip, source],
                    mirror(0),
                ).wait_recv()

    @pl.when(offset == 1)
    def _():
        for strip in range(strips):
            for parity in range(2):
                turn(strip, parity).wait_send()

    @pl.when(jnp.logical_not(even))
    def _():
        make_factor()

    own.finish()
    far.finish()
    far_x.wait_send()
    for strip in range(strips):
        planes[strip].finish()
        cross_x(strip).wait_send()
    for strip in range(early, strips):
        for parity in range(2):
            late_copy(strip, parity).wait_send()
    value = jnp.where(g == owner, dealt[g], 0.0)
    for shift in range(1, groups):
        deal(shift).wait_recv()
        source = lax.rem(g - shift + groups, groups)
        value = jnp.where(source == owner, from_group[shift - 1], value)
    factor_ref[...] = value
    for shift in range(1, groups):
        deal(shift).wait_send()


def tail_call(panel, first_diag, x_hi, x_lo, own, block, flat, far, early):
    depth, width = flat.shape
    half = width // 2
    G = lax.axis_size(GROUP)
    S = lax.axis_size("scen")
    f32, bf16 = jnp.float32, jnp.bfloat16
    vmem = pl.BlockSpec(memory_space=pltpu.VMEM)
    smem = pl.BlockSpec(memory_space=pltpu.SMEM)
    hbm = pl.BlockSpec(memory_space=pl.ANY)
    thick = 128
    strips = half // thick
    late = strips - early.shape[1] // (2 * thick)
    share = PW // G
    sems = pltpu.SemaphoreType.DMA
    return pl.pallas_call(
        tail_kernel,
        in_specs=[smem, vmem, vmem, vmem, vmem, vmem, hbm, hbm, hbm],
        out_specs=[vmem, vmem, hbm],
        out_shape=[
            jax.ShapeDtypeStruct((half, width), f32),
            jax.ShapeDtypeStruct((half, share), f32),
            jax.ShapeDtypeStruct((depth, late * 2 * thick), f32),
        ],
        scratch_shapes=[
            pltpu.VMEM((2, depth, 256), f32),
            pltpu.VMEM((256, depth), bf16),
            pltpu.VMEM((256, depth), bf16),
            pltpu.VMEM((2, half, half), f32),
            pltpu.VMEM((half, half), f32),
            pltpu.VMEM((half, half), f32),
            pltpu.VMEM((strips, 2 * thick, width), f32),
            pltpu.VMEM((strips, thick, width), f32),
            pltpu.VMEM((strips, 2, half, thick), f32),
            pltpu.VMEM((half, width), f32),
            pltpu.VMEM((2, half, width), f32),
            pltpu.VMEM((2, half, half), f32),
            pltpu.VMEM((strips, 2, thick, width), f32),
            pltpu.VMEM((PW, PW), f32),
            pltpu.VMEM((PW, PW), f32),
            pltpu.VMEM((128, 128), f32),
            pltpu.VMEM((128, 128), f32),
            pltpu.VMEM((G, half, share), f32),
            pltpu.VMEM((G - 1, half, share), f32),
            pltpu.VMEM((PW, PW), f32),
            sems((2, S - 1)),
            sems((2,)),
            sems((2, 2)),
            sems((2, late, 2)),
            sems((2,)),
            sems((2, strips)),
            sems((4,)),
            sems((4,)),
            sems((4 * strips,)),
            sems((strips, 2)),
            sems((strips, 2)),
            sems((2,)),
            sems((2, G - 1)),
        ],
        compiler_params=pltpu.CompilerParams(
            collective_id=1, has_side_effects=True, vmem_limit_bytes=60 * 1024 * 1024
        ),
        cost_estimate=pl.CostEstimate(
            flops=9 * depth * width * width, bytes_accessed=4 * depth * width * 3, transcendentals=0
        ),
    )(panel, first_diag[None, :], x_hi, x_lo, own, block, flat, far, early)


def folded_body(kkt, border, first_diag, assignment, panel):
    slots, order, width = border.shape
    flat = border.reshape(slots * order, width)
    extra = jnp.where(lax.axis_index("scen") == panel[0], first_diag, 0.0)[None, :]
    x_hi, x_lo, own, block, far, strip = head_call(
        assignment, panel, extra, kkt, flat, width // 2
    )
    schur, factor, _ = tail_call(panel, first_diag, x_hi, x_lo, own, block, flat, far, strip)
    return (schur, factor)


def body(kkt, border, first_diag, assignment, panel):
    groups = lax.axis_size(GROUP)
    foldable = (
        groups == 4
        and lax.axis_size("row") == 2
        and lax.axis_size("scen") == 2 * groups
        and border.shape[2] == 2 * first_diag.shape[0]
        and first_diag.shape[0] == PW
    )
    chosen = folded_body if foldable else plain_body
    return chosen(kkt, border, first_diag, assignment, panel)


def solution(mesh):
    in_specs = (
        P("scen", ("row", "col"), None),
        P("scen", None, ("row", "col")),
        P("scen"),
        P("scen"),
        P(),
    )
    out_specs = (P("scen", ("row", "col")), P("scen", ("row", "col")))
    return jax.shard_map(body, mesh=mesh, in_specs=in_specs, out_specs=out_specs, check_vma=False)
```

```python
import jax
import jax.numpy as jnp
from jax import lax
from jax.experimental import pallas as pl
from jax.experimental.pallas import tpu as pltpu
from jax.sharding import PartitionSpec as P

PW = 512
NEWTON = 3


HIGH = lax.Precision.HIGH
GROUP = ("row", "col")


def swapped(value, axis, distance):
    mask = 2**distance
    pairs = [(source, source ^ mask) for source in range(lax.axis_size(axis))]
    return lax.ppermute(value, axis, pairs)


def gathered_rows(value, axis):
    count = lax.axis_size(axis)
    index = lax.axis_index(axis)
    rows = value.shape[1]
    whole = jnp.zeros((value.shape[0], rows * count, value.shape[2]), value.dtype)
    whole = lax.dynamic_update_slice_in_dim(whole, value, index * rows, 1)
    for shift in range(1, count):
        pairs = [(source, (source + shift) % count) for source in range(count)]
        origin = lax.rem(index - shift + count, count)
        whole = lax.dynamic_update_slice_in_dim(
            whole, lax.ppermute(value, axis, pairs), origin * rows, 1
        )
    return whole


def matmul(left, right, precision=HIGH):
    return jnp.dot(left, right, precision=precision, preferred_element_type=jnp.float32)


def contract(left, right):
    return lax.dot_general(
        left, right, (((0,), (0,)), ((), ())), precision=HIGH, preferred_element_type=jnp.float32
    )


def plain_body(kkt, border, first_diag, assignment, panel):
    scen_index = lax.axis_index("scen")
    own_index = lax.axis_index(GROUP)
    group_size = lax.axis_size(GROUP)
    slots, order, col_count = border.shape
    width = col_count * group_size
    scenario_ids = scen_index * slots + jnp.arange(slots, dtype=jnp.int32)
    kkt = jnp.where((assignment == scenario_ids)[:, None, None], kkt, swapped(kkt, "scen", 0))
    kkt_all = gathered_rows(gathered_rows(kkt, "col"), "row")
    gathered = lax.all_gather(border, GROUP, axis=2, tiled=True)
    eye = jnp.eye(order, dtype=jnp.bool_)
    inverses = []
    for slot in range(slots):
        full = kkt_all[slot]
        diag = jnp.where(eye, full, 0.0)
        row_inv = 1.0 / jnp.sum(diag, axis=1, keepdims=True)
        col_inv = 1.0 / jnp.sum(diag, axis=0, keepdims=True)
        approx = jnp.where(eye, 2.0 * row_inv, 0.0) - row_inv * full * col_inv
        for step in range(NEWTON - 1):
            approx = 2.0 * approx - matmul(matmul(approx, full), approx)
        inverses.append(approx)
    solved = jnp.concatenate([matmul(inverses[slot], border[slot]) for slot in range(slots)], 0)
    border_all = gathered.reshape(slots * order, width)

    panel_start = panel[0] * PW
    share = PW // group_size
    own_start = panel_start + own_index * share

    share_solved = jnp.concatenate(
        [
            matmul(inverses[slot], lax.dynamic_slice_in_dim(gathered[slot], own_start, share, 1))
            for slot in range(slots)
        ],
        0,
    )
    panel_border = lax.dynamic_slice_in_dim(border_all, panel_start, PW, 1)
    block = contract(panel_border, share_solved)
    row_span = first_diag.shape[0]
    global_rows = scen_index * row_span + jnp.arange(row_span, dtype=jnp.int32)
    share_ids = own_start + jnp.arange(share, dtype=jnp.int32)
    owned = global_rows[:, None] == share_ids[None, :]
    share_diag = jnp.sum(jnp.where(owned, first_diag[:, None], 0.0), axis=0)
    panel_ids = panel_start + jnp.arange(PW, dtype=jnp.int32)
    block = block + jnp.where(panel_ids[:, None] == share_ids[None, :], share_diag[None, :], 0.0)
    block = lax.psum(block, "scen")
    block = lax.all_gather(block, GROUP, axis=1, tiled=True)
    symmetric = 0.5 * (block + block.T)
    lower_factor = jnp.linalg.cholesky(symmetric)
    lower_inverse = lax.linalg.triangular_solve(
        lower_factor, jnp.eye(PW, dtype=jnp.float32), left_side=True, lower=True
    )
    own_inverse = lax.dynamic_slice_in_dim(lower_inverse, own_index * share, share, 0)

    def schur_columns(start, count, solved):
        tile = contract(border_all, lax.dynamic_slice_in_dim(solved, start, count, 1))
        summed = lax.psum_scatter(tile, "scen", scatter_dimension=0, tiled=True)
        global_cols = own_index * col_count + start + jnp.arange(count, dtype=jnp.int32)
        on_diag = global_rows[:, None] == global_cols[None, :]
        return summed + jnp.where(on_diag, first_diag[:, None], 0.0)

    if col_count >= PW:
        pieces = col_count // PW
        first = lax.rem(panel[0], pieces)
        schur = jnp.zeros((row_span, col_count), jnp.float32)
        panel_rows = None
        for piece in range(pieces):
            start = lax.rem(first + piece, pieces) * PW
            columns = schur_columns(start, PW, solved)
            if piece == 0:
                owns = own_index == panel[0] // pieces
                columns, solved = lax.optimization_barrier((columns, solved))
                panel_rows = lax.psum(jnp.where(owns, columns, 0.0), GROUP)
            schur = lax.dynamic_update_slice_in_dim(schur, columns, start, 1)
    else:
        schur = schur_columns(jnp.int32(0), col_count, solved)
        parts = PW // col_count
        position = own_index - panel[0] * parts
        owns = (position >= 0) & (position < parts)
        placed = jnp.zeros((row_span, PW), jnp.float32)
        placed = lax.dynamic_update_slice_in_dim(
            placed, jnp.where(owns, schur, 0.0), jnp.clip(position, 0, parts - 1) * col_count, 1
        )
        panel_rows = lax.psum(placed, GROUP)
    own_cols = lax.dot_general(
        panel_rows,
        own_inverse,
        (((1,), (1,)), ((), ())),
        precision=lax.Precision.HIGHEST,
        preferred_element_type=jnp.float32,
    )
    return (schur, own_cols)


def parts(value):
    high = value.astype(jnp.bfloat16)
    return high, (value - high.astype(jnp.float32)).astype(jnp.bfloat16)


def dot(left, right):
    return jnp.dot(left, right, preferred_element_type=jnp.float32)


def dot_rows(left, right):
    return lax.dot_general(
        left, right, (((0,), (0,)), ((), ())), preferred_element_type=jnp.float32
    )


def head_kernel(
    assignment_ref,
    panel_ref,
    extra_ref,
    kkt_ref,
    border_ref,
    x_hi,
    x_lo,
    own_ref,
    part_ref,
    far_ref,
    strip_ref,
    own_tiles,
    share,
    from_core,
    from_scen,
    swap,
    full,
    loaded,
    b_hi,
    b_lo,
    e_hi,
    e_lo,
    m_hi,
    m_lo,
    p_hi,
    z_hi,
    z_lo,
    head,
    load_sem,
    own_sems,
    swap_sems,
    y_sems,
    core_sems,
    far_sems,
    strip_sems,
    scen_sems,
    deal_sems,
):
    slots, order, _ = full.shape
    rows = kkt_ref.shape[1]
    width = x_hi.shape[1]
    half = width // 2
    panel_width = share.shape[0]
    groups = lax.axis_size(GROUP)
    S = lax.axis_size("scen")
    step = 256
    s = lax.axis_index("scen")
    core = lax.axis_index("row")
    y = lax.axis_index("col")
    g = core * 2 + y
    flip_x = s + 1 - 2 * lax.rem(s, 2)

    def group_peer(shift):
        to = lax.rem(g + shift, groups)
        return (s, to // 2, lax.rem(to, 2))

    def scen_peer(shift):
        return (lax.rem(s + shift, S), core, y)

    barrier = pltpu.get_barrier_semaphore()
    for shift in range(1, groups):
        pl.semaphore_signal(
            barrier, inc=1, device_id=group_peer(shift), device_id_type=pl.DeviceIdType.MESH
        )
    for shift in range(1, S):
        pl.semaphore_signal(
            barrier, inc=1, device_id=scen_peer(shift), device_id_type=pl.DeviceIdType.MESH
        )
    pl.semaphore_wait(barrier, groups + S - 2)

    def remote(source, target, sems, index, device):
        return pltpu.make_async_remote_copy(
            src_ref=source,
            dst_ref=target,
            send_sem=sems.at[0, index],
            recv_sem=sems.at[1, index],
            device_id=device,
            device_id_type=pl.DeviceIdType.MESH,
        )

    def swap_copy(slot):
        return remote(kkt_ref.at[slot], swap.at[slot], swap_sems, slot, (flip_x, core, y))

    own_rows = pl.ds(pl.multiple_of(g * rows, 8), rows)
    core_rows = pl.ds(pl.multiple_of(core * (2 * rows), 8), 2 * rows)

    def y_copy(slot):
        place = full.at[slot, own_rows, :]
        return remote(place, place, y_sems, slot, (s, core, 1 - y))

    def core_copy(slot):
        place = full.at[slot, core_rows, :]
        return remote(place, place, core_sems, slot, (s, 1 - core, y))

    def load(slot):
        return pltpu.make_async_copy(
            border_ref.at[pl.ds(slot * order, order), :], loaded, load_sem
        )

    far_copy = remote(border_ref, far_ref, far_sems, 0, (s, 1 - core, y))
    strip_width = strip_ref.shape[1] // 2
    cuts = [(0, order), (order, (slots - 1) * order)]
    strip_copies = [
        [
            remote(
                border_ref.at[pl.ds(low, count), pl.ds(p * half, strip_width)],
                strip_ref.at[pl.ds(low, count), pl.ds(p * strip_width, strip_width)],
                strip_sems,
                2 * index + p,
                group_peer(groups - 1),
            )
            for p in range(2)
        ]
        for index, (low, count) in enumerate(cuts)
    ]

    swap_copy(0).start()
    load(0).start()
    for copy in strip_copies[0]:
        copy.start()

    def select_rows(slot):
        swap_copy(slot).wait_recv()
        if slot + 1 < slots:
            swap_copy(slot + 1).start()
        same = assignment_ref[slot] == s * slots + slot
        full[slot, own_rows, :] = jnp.where(same, kkt_ref[slot], swap[slot])
        y_copy(slot).start()

    select_rows(0)
    select_rows(1)
    y_copy(0).wait_recv()
    core_copy(0).start()
    far_copy.start()

    def eye_at(start):
        row = lax.broadcasted_iota(jnp.int32, (step, order), 0) + start
        return row == lax.broadcasted_iota(jnp.int32, (step, order), 1)

    @pl.loop(0, slots)
    def _(slot):
        core_copy(slot).wait_recv()
        col_diag = jnp.zeros((1, order), jnp.float32)
        for start in range(0, order, step):
            spot = pl.ds(start, step)
            block = full[slot, spot, :]
            eye = eye_at(start)
            diag = jnp.where(eye, block, 0.0)
            col_diag = col_diag + jnp.sum(diag, axis=0, keepdims=True)
            scale = 1.0 / jnp.sum(diag, axis=1, keepdims=True)
            scaled = jnp.where(eye, 0.0, -scale * block)
            head[spot, :] = scaled
            high, low = parts(scaled)
            e_hi[spot, :] = high
            e_lo[spot, :] = low
        col_inv = 1.0 / col_diag

        @pl.loop(0, order // step)
        def _(chunk):
            spot = pl.ds(pl.multiple_of(chunk * step, step), step)
            high = e_hi[spot, :]
            value = dot(high, e_hi[...]) + dot(high, e_lo[...]) + dot(e_lo[spot, :], e_hi[...])
            head[spot, :] += value
            high, low = parts(value)
            m_hi[spot, :] = high
            m_lo[spot, :] = low

        @pl.loop(0, order // step)
        def _(chunk):
            start = pl.multiple_of(chunk * step, step)
            spot = pl.ds(start, step)
            high = e_hi[spot, :]
            value = dot(high, m_hi[...]) + dot(high, m_lo[...]) + dot(e_lo[spot, :], m_hi[...])
            head[spot, :] += value + jnp.where(eye_at(start), 1.0, 0.0)
            p_hi[spot, :] = dot(m_hi[spot, :], m_hi[...]).astype(jnp.bfloat16)

        @pl.loop(0, order // step)
        def _(chunk):
            spot = pl.ds(pl.multiple_of(chunk * step, step), step)
            value = head[spot, :]
            value = (value + dot(value.astype(jnp.bfloat16), p_hi[...])) * col_inv
            high, low = parts(value)
            z_hi[spot, :] = high
            z_lo[spot, :] = low

        here = pl.ds(pl.multiple_of(slot * order, step), order)
        load(slot).wait()

        @pl.loop(0, width // step)
        def _(chunk):
            spot = pl.ds(pl.multiple_of(chunk * step, step), step)
            high, low = parts(loaded[:, spot])
            b_hi[here, spot] = high
            b_lo[here, spot] = low
            high, low = parts(dot(z_hi[...], high) + dot(z_hi[...], low) + dot(z_lo[...], high))
            x_hi[here, spot] = high
            x_lo[here, spot] = low

        @pl.when(slot < slots - 1)
        def _():
            load(slot + 1).start()

        for done in range(slots - 1):

            @pl.when(slot == done)
            def _():
                if done + 2 < slots:
                    select_rows(done + 2)
                y_copy(done + 1).wait_recv()
                core_copy(done + 1).start()
                if done + 2 == slots:
                    for copy in strip_copies[1]:
                        copy.start()

    x = lax.rem(s, 2)

    def own_tile(parity, tile):
        spot = pl.ds(pl.multiple_of(parity * half + tile * step, step), step)
        high, low = b_hi[:, spot], b_lo[:, spot]
        to = pl.ds(tile * step, step)

        @pl.loop(0, width // step)
        def _(chunk):
            cols = pl.ds(pl.multiple_of(chunk * step, step), step)
            x_high, x_low = x_hi[:, cols], x_lo[:, cols]
            own_tiles[parity, to, cols] = (
                dot_rows(high, x_high) + dot_rows(high, x_low) + dot_rows(low, x_high)
            )

    own_copies = [
        remote(
            own_tiles.at[1 - x, pl.ds(tile * step, step), :],
            own_ref.at[pl.ds(tile * step, step), :],
            own_sems,
            tile,
            (flip_x, core, y),
        )
        for tile in range(half // step)
    ]
    for tile, copy in enumerate(own_copies):
        own_tile(1 - x, tile)
        copy.start()

    left = lax.rem(panel_ref[0], 2) == 0
    owns = core == (panel_ref[0] // 2) // 2
    row = lax.broadcasted_iota(jnp.int32, (step, panel_width), 0)
    col = lax.broadcasted_iota(jnp.int32, (step, panel_width), 1)
    x_high = jnp.where(left, x_hi[:, :half], x_hi[:, half:])
    x_low = jnp.where(left, x_lo[:, :half], x_lo[:, half:])
    for start in range(0, panel_width, step):
        low_side = slice(start, start + step)
        high_side = slice(half + start, half + start + step)
        high = jnp.where(left, b_hi[:, low_side], b_hi[:, high_side])
        low = jnp.where(left, b_lo[:, low_side], b_lo[:, high_side])
        value = dot_rows(high, x_high) + dot_rows(high, x_low) + dot_rows(low, x_high)
        value = value + jnp.where(row + start == col, extra_ref[...], 0.0)
        share[low_side, :] = jnp.where(owns, value, 0.0)
    core_half = panel_width // 2
    part_rows = core_half // S

    def part_at(index):
        return pl.ds(pl.multiple_of(core * core_half + index * part_rows, 8), part_rows)

    deal = remote(
        share.at[pl.ds(pl.multiple_of((1 - core) * core_half, 8), core_half), :],
        from_core,
        deal_sems,
        0,
        (s, 1 - core, y),
    )

    def reduce_copy(shift):
        to = lax.rem(s + shift, S)
        return remote(
            share.at[part_at(to), :],
            from_scen.at[shift - 1],
            scen_sems,
            shift - 1,
            scen_peer(shift),
        )

    deal.start()
    own_tile(x, 0)
    deal.wait()
    share[pl.ds(pl.multiple_of(core * core_half, 8), core_half), :] += from_core[...]
    for shift in range(1, S):
        reduce_copy(shift).start()
    own_tile(x, 1)
    value = share[part_at(s), :]
    for shift in range(1, S):
        reduce_copy(shift).wait_recv()
        value = value + from_scen[shift - 1]
    part_ref[...] = value
    for shift in range(1, S):
        reduce_copy(shift).wait_send()
    for copy in own_copies:
        copy.wait()
    own_ref[...] += own_tiles[x]
    for slot in range(slots):
        swap_copy(slot).wait_send()
        y_copy(slot).wait_send()
        core_copy(slot).wait_send()
    far_copy.wait()
    for copies in strip_copies:
        for copy in copies:
            copy.wait()


def head_call(assignment, panel, extra, kkt, flat, strip_width):
    slots, rows, order = kkt.shape
    depth, width = flat.shape
    S = lax.axis_size("scen")
    f32, bf16 = jnp.float32, jnp.bfloat16
    vmem = pl.BlockSpec(memory_space=pltpu.VMEM)
    smem = pl.BlockSpec(memory_space=pltpu.SMEM)
    hbm = pl.BlockSpec(memory_space=pl.ANY)

    def sems(count):
        return pltpu.SemaphoreType.DMA((2, count))

    return pl.pallas_call(
        head_kernel,
        in_specs=[smem, smem, vmem, vmem, hbm],
        out_specs=[vmem, vmem, vmem, vmem, hbm, hbm],
        out_shape=[
            jax.ShapeDtypeStruct((depth, width), bf16),
            jax.ShapeDtypeStruct((depth, width), bf16),
            jax.ShapeDtypeStruct((PW, width), f32),
            jax.ShapeDtypeStruct((PW // 2 // S, PW), f32),
            jax.ShapeDtypeStruct((depth, width), f32),
            jax.ShapeDtypeStruct((depth, strip_width), f32),
        ],
        scratch_shapes=[
            pltpu.VMEM((2, PW, width), f32),
            pltpu.VMEM((PW, PW), f32),
            pltpu.VMEM((PW // 2, PW), f32),
            pltpu.VMEM((S - 1, PW // 2 // S, PW), f32),
            pltpu.VMEM((slots, rows, order), f32),
            pltpu.VMEM((slots, order, order), f32),
            pltpu.VMEM((order, width), f32),
            pltpu.VMEM((depth, width), bf16),
            pltpu.VMEM((depth, width), bf16),
        ]
        + [pltpu.VMEM((order, order), bf16)] * 7
        + [
            pltpu.VMEM((order, order), f32),
            pltpu.SemaphoreType.DMA,
            sems(2),
            sems(slots),
            sems(slots),
            sems(slots),
            sems(1),
            sems(4),
            sems(S - 1),
            sems(1),
        ],
        compiler_params=pltpu.CompilerParams(
            collective_id=0, has_side_effects=True, vmem_limit_bytes=60 * 1024 * 1024
        ),
        cost_estimate=pl.CostEstimate(
            flops=2 * slots * order * order * (8 * order + 3 * width) + 6 * depth * width * width,
            bytes_accessed=4 * depth * width * 3,
            transcendentals=0,
        ),
    )(assignment, panel, extra, kkt, flat)


def factor_block(s_ref, w_ref):
    size = s_ref.shape[0]
    pivots = 4
    row = lax.broadcasted_iota(jnp.int32, (size, size), 0)
    lane = lax.broadcasted_iota(jnp.int32, (size, size), 1)
    thin = lax.broadcasted_iota(jnp.int32, (1, size), 1)
    tall = lax.broadcasted_iota(jnp.int32, (size, 1), 0)
    w_ref[...] = jnp.where(row == lane, 1.0, 0.0)

    @pl.loop(0, size // pivots)
    def _(block):
        j = block * pivots
        whole = s_ref[...]
        rows = [s_ref[pl.ds(j + p, 1), :] for p in range(pivots)]
        tails = [w_ref[pl.ds(j + p, 1), :] for p in range(pivots)]
        cols = [
            jnp.sum(jnp.where(lane == j + p, whole, 0.0), axis=1, keepdims=True)
            for p in range(pivots)
        ]
        small = [
            [
                jnp.sum(jnp.where(thin == j + q, rows[p], 0.0), axis=1, keepdims=True)
                for q in range(p, pivots)
            ]
            for p in range(pivots)
        ]
        entry = lambda q, p: small[p][q - p]
        lower = {}
        tails_new, rows_new, cols_new = [], [], []
        for p in range(pivots):
            value = entry(p, p)
            for q in range(p):
                value = value - lower[p, q] * lower[p, q]
            root = lax.rsqrt(value)
            root = root * (1.5 - 0.5 * value * root * root)
            for i in range(p + 1, pivots):
                below = entry(i, p)
                for q in range(p):
                    below = below - lower[i, q] * lower[p, q]
                lower[i, p] = below * root
            u, c, v = rows[p], cols[p], tails[p]
            for q in range(p):
                u = u - lower[p, q] * rows_new[q]
                c = c - lower[p, q] * cols_new[q]
                v = v - lower[p, q] * tails_new[q]
            rows_new.append(u * root)
            cols_new.append(c * root)
            tails_new.append(v * root)
        change = jnp.zeros((size, size), jnp.float32)
        other = jnp.zeros((size, size), jnp.float32)
        for p in range(pivots):
            c = jnp.where(tall >= j + pivots, cols_new[p], 0.0)
            change = change + c * rows_new[p]
            other = other + c * tails_new[p]
        s_ref[...] = whole - change
        w_ref[...] = w_ref[...] - other
        for p in range(pivots):
            w_ref[pl.ds(j + p, 1), :] = tails_new[p]


def exact(left, right, axes=((1,), (0,))):
    return lax.dot_general(
        left,
        right,
        (axes, ((), ())),
        precision=lax.Precision.HIGHEST,
        preferred_element_type=jnp.float32,
    )


def tail_kernel(
    panel_ref,
    diag_ref,
    x_hi,
    x_lo,
    own_in,
    part_ref,
    border_ref,
    far_ref,
    early_ref,
    out_ref,
    factor_ref,
    late_ref,
    stage,
    lt_hi,
    lt_lo,
    far_tile,
    from_x_far,
    far_turned,
    cross,
    from_x,
    turned,
    own_acc,
    own_z,
    far_z,
    cross_z,
    work,
    inverse,
    s_ref,
    w_ref,
    dealt,
    from_group,
    block,
    spread_sems,
    whole_sems,
    stage_sems,
    late_sems,
    far_x_sems,
    x_sems,
    own_z_sems,
    far_z_sems,
    cross_z_sems,
    turn_send,
    turn_recv,
    far_turn_sems,
    deal_sems,
):
    depth, width = x_hi.shape
    half = width // 2
    groups = dealt.shape[0]
    strips = cross.shape[0]
    thick = cross.shape[1] // 2
    early = early_ref.shape[1] // (2 * thick)
    step = 256
    s = lax.axis_index("scen")
    core = lax.axis_index("row")
    y = lax.axis_index("col")
    S = lax.axis_size("scen")
    g = core * 2 + y
    x = lax.rem(s, 2)
    z = s // 2
    flip_x = s + 1 - 2 * x
    MESH = pl.DeviceIdType.MESH

    def group_peer(shift):
        to = lax.rem(g + shift, groups)
        return (s, to // 2, lax.rem(to, 2))

    def mirror(parity):
        return (2 * g + parity, z // 2, lax.rem(z, 2))

    barrier = pltpu.get_barrier_semaphore()
    for shift in range(1, groups):
        pl.semaphore_signal(barrier, inc=1, device_id=group_peer(shift), device_id_type=MESH)
    for shift in range(1, S):
        pl.semaphore_signal(
            barrier, inc=1, device_id=(lax.rem(s + shift, S), core, y), device_id_type=MESH
        )

    @pl.when(z != g)
    def _():
        for parity in range(2):
            pl.semaphore_signal(barrier, inc=1, device_id=mirror(parity), device_id_type=MESH)
        pl.semaphore_wait(barrier, groups + S)

    @pl.when(z == g)
    def _():
        pl.semaphore_wait(barrier, groups + S - 2)

    def remote(source, target, send, recv, device):
        return pltpu.make_async_remote_copy(
            src_ref=source,
            dst_ref=target,
            send_sem=send,
            recv_sem=recv,
            device_id=device,
            device_id_type=MESH,
        )

    class Plane:
        def __init__(self, value, first, second, sems, base, shift):
            self.value, self.first, self.second = value, first, second
            self.target = lax.rem(g + shift, groups)
            low = z - lax.rem(z, 2)
            self.keeper = jnp.minimum(jnp.maximum(self.target, low), low + 1)
            self.one = remote(
                value, first, sems.at[base], sems.at[base + 1], (self.keeper * 2 + x, core, y)
            )
            self.two = remote(
                value, second, sems.at[base + 2], sems.at[base + 3], (self.target * 2 + x, core, y)
            )

        def send(self):
            @pl.when(z != self.keeper)
            def _():
                self.one.start()

        def pass_on(self):
            @pl.when(z == self.keeper)
            def _():
                self.one.wait_recv()
                self.value[...] += self.first[...]

                @pl.when(z != self.target)
                def _():
                    self.two.start()

        def take(self):
            self.two.wait_recv()
            self.value[...] += self.second[...]

        def finish(self):
            @pl.when(z != self.keeper)
            def _():
                self.one.wait_send()

            @pl.when((z == self.keeper) & (z != self.target))
            def _():
                self.two.wait_send()

    def late_copy(strip, parity):
        return remote(
            border_ref.at[:, pl.ds(parity * half + strip * thick, thick)],
            late_ref.at[:, pl.ds(((strip - early) * 2 + parity) * thick, thick)],
            late_sems.at[0, strip - early, parity],
            late_sems.at[1, strip - early, parity],
            group_peer(groups - 1),
        )

    own = Plane(own_acc, own_z.at[0], own_z.at[1], own_z_sems, 0, 0)
    own_acc[...] = own_in[...]
    own.send()
    part_rows = part_ref.shape[0]
    core_half = block.shape[0] // 2
    own_part = pl.ds(pl.multiple_of(core * core_half + s * part_rows, 8), part_rows)
    block[own_part, :] = part_ref[...]

    def spread_copy(shift):
        return remote(
            block.at[own_part, :],
            block.at[own_part, :],
            spread_sems.at[0, shift - 1],
            spread_sems.at[1, shift - 1],
            (lax.rem(s + shift, S), core, y),
        )

    half_rows = pl.ds(pl.multiple_of(core * core_half, 8), core_half)
    whole_copy = remote(
        block.at[half_rows, :],
        block.at[half_rows, :],
        whole_sems.at[0],
        whole_sems.at[1],
        (s, 1 - core, y),
    )
    for shift in range(1, S):
        spread_copy(shift).start()
    for parity in range(2):
        late_copy(early, parity).start()

    def stage_load(slot, source, start, count, part):
        return pltpu.make_async_copy(
            source.at[:, pl.ds(start, count)],
            stage.at[slot, :, pl.ds(part * count, count)],
            stage_sems.at[slot, part],
        )

    def strip_load(slot, strip, part):
        if strip < early:
            return stage_load(slot, early_ref, part * early * thick + strip * thick, thick, part)
        return stage_load(slot, late_ref, ((strip - early) * 2 + part) * thick, thick, part)

    def far_load(slot, parity, tile):
        return stage_load(
            slot, far_ref, pl.multiple_of(parity * half + tile * step, step), step, 0
        )

    def product(slot, target, base, count):
        @pl.loop(0, depth // step)
        def _(chunk):
            spot = pl.ds(pl.multiple_of(chunk * step, step), step)
            high, low = parts(stage[slot, spot, :].T)
            lt_hi[:, spot] = high
            lt_lo[:, spot] = low

        @pl.loop(0, count // step)
        def _(chunk):
            start = pl.multiple_of(chunk * step, step)
            cols = pl.ds(pl.multiple_of(base + start, step), step)
            high, low = x_hi[:, cols], x_lo[:, cols]
            target[:, pl.ds(start, step)] = (
                dot(lt_hi[...], high) + dot(lt_hi[...], low) + dot(lt_lo[...], high)
            )

    near = g < groups // 2

    def far_side(parity):
        return jnp.where(near, parity, 1 - parity)

    def far_product(slot, parity, tile):
        product(
            slot, far_tile.at[parity, pl.ds(tile * step, step), :], far_side(parity) * half, half
        )

    far_x = remote(
        far_tile.at[1 - x], from_x_far, far_x_sems.at[0], far_x_sems.at[1], (flip_x, core, y)
    )
    loads = [
        [far_load(0, 1 - x, 0)],
        [far_load(1, 1 - x, 1)],
    ]
    for strip in range(early):
        loads.append([strip_load(strip % 2, strip, part) for part in range(2)])
    for tile in range(2):
        loads.append([far_load((early + tile) % 2, x, tile)])

    def begin(index):
        for copy in loads[index]:
            copy.start()

    def ready(index):
        for copy in loads[index]:
            copy.wait()
        if index + 1 < len(loads):
            begin(index + 1)

    def kept(strip):
        return cross.at[strip, pl.ds(pl.multiple_of(x * thick, 8), thick), :]

    def cross_x(strip):
        return remote(
            cross.at[strip, pl.ds(pl.multiple_of((1 - x) * thick, 8), thick), :],
            from_x.at[strip],
            x_sems.at[0, strip],
            x_sems.at[1, strip],
            (flip_x, core, y),
        )

    planes = [
        Plane(kept(i), cross_z.at[i, 0], cross_z.at[i, 1], cross_z_sems, 4 * i, 1)
        for i in range(strips)
    ]
    far = Plane(far_tile.at[x], far_z.at[0], far_z.at[1], far_z_sems, 0, 2)

    def join_x(strip):
        cross_x(strip).wait_recv()
        kept(strip)[...] += from_x[strip]
        planes[strip].send()

    def turn(strip, parity):
        place = out_ref.at[:, pl.ds(pl.multiple_of(x * half + strip * thick, thick), thick)]
        return remote(
            turned.at[strip, parity],
            place,
            turn_send.at[strip, parity],
            turn_recv.at[strip, x],
            mirror(parity),
        )

    offset = lax.rem(z - g + groups, groups)

    def settle(strip):
        @pl.when(offset == 1)
        def _():
            planes[strip].take()
            value = kept(strip)[...]
            out_ref[pl.ds(strip * thick, thick), :] = value
            for parity in range(2):
                turned[strip, parity] = value[:, parity * half : (parity + 1) * half].T
                turn(strip, parity).start()

    mine = far_side(x)
    far_turn = remote(
        far_turned,
        out_ref.at[:, pl.ds(pl.multiple_of(x * half, half), half)],
        far_turn_sems.at[0],
        far_turn_sems.at[1],
        (2 * g + mine, z // 2, lax.rem(z, 2)),
    )

    size = s_ref.shape[0]
    count = work.shape[0] // size

    def spot(index):
        return slice(index * size, (index + 1) * size)

    def eliminate(k):
        s_ref[...] = work[spot(k), spot(k)]
        factor_block(s_ref, w_ref)
        inverse[spot(k), spot(k)] = w_ref[...]
        if k + 1 < count:
            rest = slice((k + 1) * size, count * size)
            below = exact(work[rest, spot(k)], w_ref[...], ((1,), (1,)))
            work[rest, spot(k)] = below
            work[rest, rest] = work[rest, rest] - exact(below, below, ((1,), (1,)))
        if k > 0:
            known = slice(0, k * size)
            row = exact(work[spot(k), known], inverse[known, known])
            inverse[spot(k), known] = -exact(w_ref[...], row)

    def late_strip(strip):
        for parity in range(2):
            late_copy(strip, parity).wait_recv()
        for part in range(2):
            strip_load(strip % 2, strip, part).start()
        for part in range(2):
            strip_load(strip % 2, strip, part).wait()
        product(strip % 2, cross.at[strip], 0, width)
        cross_x(strip).start()

    inverse[...] = jnp.zeros(inverse.shape, jnp.float32)
    begin(0)
    for tile in range(2):
        ready(tile)
        far_product(tile, 1 - x, tile)
    far_x.start()
    for strip in range(early):
        ready(2 + strip)
        product(strip % 2, cross.at[strip], 0, width)
        cross_x(strip).start()
    for tile in range(2):
        ready(2 + early + tile)
        far_product((early + tile) % 2, x, tile)
    for strip in range(early + 1, strips):
        for parity in range(2):
            late_copy(strip, parity).start()
    far_x.wait_recv()
    far_tile[x] += from_x_far[...]
    far.send()
    own.pass_on()
    for shift in range(1, S):
        spread_copy(shift).wait()
    whole_copy.start()
    for strip in range(early):
        join_x(strip)
    late_strip(early)
    whole_copy.wait()
    work[...] = 0.5 * (block[...] + block[...].T)
    eliminate(0)
    far.pass_on()
    for strip in range(early):
        planes[strip].pass_on()
    join_x(early)
    eliminate(1)

    @pl.when(offset == 0)
    def _():
        own.take()
        row = lax.broadcasted_iota(jnp.int32, (half, width), 0) + x * half
        col = lax.broadcasted_iota(jnp.int32, (half, width), 1)
        out_ref[...] = own_acc[...] + jnp.where(row == col, diag_ref[...].T, 0.0)

    @pl.when(offset == 2)
    def _():
        far.take()
        value = far_tile[x]
        out_ref[:, pl.ds(pl.multiple_of(mine * half, half), half)] = value
        far_turned[...] = value.T
        far_turn.start()

    planes[early].pass_on()
    late_strip(early + 1)
    for strip in range(early):
        settle(strip)
    eliminate(2)
    join_x(early + 1)
    settle(early)
    eliminate(3)
    planes[early + 1].pass_on()
    settle(early + 1)

    left = lax.rem(panel_ref[0], 2) == 0
    owner = panel_ref[0] // 2
    piece = dealt.shape[2]

    def deal(shift):
        return remote(
            dealt.at[lax.rem(g + shift, groups)],
            from_group.at[shift - 1],
            deal_sems.at[0, shift - 1],
            deal_sems.at[1, shift - 1],
            group_peer(shift),
        )

    def make_factor():
        columns = jnp.where(left, out_ref[:, :half], out_ref[:, half:])
        for part in range(groups):
            dealt[part] = exact(
                columns, inverse[part * piece : (part + 1) * piece, :], ((1,), (1,))
            )
        for shift in range(1, groups):
            deal(shift).start()

    @pl.when(offset == 2)
    def _():
        remote(
            far_turned,
            out_ref.at[:, pl.ds(pl.multiple_of((1 - mine) * half, half), half)],
            far_turn_sems.at[0],
            far_turn_sems.at[1],
            mirror(0),
        ).wait_recv()
        far_turn.wait_send()

    even = (offset == 0) | (offset == 2)

    @pl.when(even)
    def _():
        make_factor()

    @pl.when(offset == 3)
    def _():
        for strip in range(strips):
            for source in range(2):
                remote(
                    turned.at[strip, 0],
                    out_ref.at[:, pl.ds(source * half + strip * thick, thick)],
                    turn_send.at[strip, 0],
                    turn_recv.at[strip, source],
                    mirror(0),
                ).wait_recv()

    @pl.when(offset == 1)
    def _():
        for strip in range(strips):
            for parity in range(2):
                turn(strip, parity).wait_send()

    @pl.when(jnp.logical_not(even))
    def _():
        make_factor()

    own.finish()
    far.finish()
    far_x.wait_send()
    for strip in range(strips):
        planes[strip].finish()
        cross_x(strip).wait_send()
    for strip in range(early, strips):
        for parity in range(2):
            late_copy(strip, parity).wait_send()
    value = jnp.where(g == owner, dealt[g], 0.0)
    for shift in range(1, groups):
        deal(shift).wait_recv()
        source = lax.rem(g - shift + groups, groups)
        value = jnp.where(source == owner, from_group[shift - 1], value)
    factor_ref[...] = value
    for shift in range(1, groups):
        deal(shift).wait_send()


def tail_call(panel, first_diag, x_hi, x_lo, own, block, flat, far, early):
    depth, width = flat.shape
    half = width // 2
    G = lax.axis_size(GROUP)
    S = lax.axis_size("scen")
    f32, bf16 = jnp.float32, jnp.bfloat16
    vmem = pl.BlockSpec(memory_space=pltpu.VMEM)
    smem = pl.BlockSpec(memory_space=pltpu.SMEM)
    hbm = pl.BlockSpec(memory_space=pl.ANY)
    thick = 128
    strips = half // thick
    late = strips - early.shape[1] // (2 * thick)
    share = PW // G
    sems = pltpu.SemaphoreType.DMA
    return pl.pallas_call(
        tail_kernel,
        in_specs=[smem, vmem, vmem, vmem, vmem, vmem, hbm, hbm, hbm],
        out_specs=[vmem, vmem, hbm],
        out_shape=[
            jax.ShapeDtypeStruct((half, width), f32),
            jax.ShapeDtypeStruct((half, share), f32),
            jax.ShapeDtypeStruct((depth, late * 2 * thick), f32),
        ],
        scratch_shapes=[
            pltpu.VMEM((2, depth, 256), f32),
            pltpu.VMEM((256, depth), bf16),
            pltpu.VMEM((256, depth), bf16),
            pltpu.VMEM((2, half, half), f32),
            pltpu.VMEM((half, half), f32),
            pltpu.VMEM((half, half), f32),
            pltpu.VMEM((strips, 2 * thick, width), f32),
            pltpu.VMEM((strips, thick, width), f32),
            pltpu.VMEM((strips, 2, half, thick), f32),
            pltpu.VMEM((half, width), f32),
            pltpu.VMEM((2, half, width), f32),
            pltpu.VMEM((2, half, half), f32),
            pltpu.VMEM((strips, 2, thick, width), f32),
            pltpu.VMEM((PW, PW), f32),
            pltpu.VMEM((PW, PW), f32),
            pltpu.VMEM((128, 128), f32),
            pltpu.VMEM((128, 128), f32),
            pltpu.VMEM((G, half, share), f32),
            pltpu.VMEM((G - 1, half, share), f32),
            pltpu.VMEM((PW, PW), f32),
            sems((2, S - 1)),
            sems((2,)),
            sems((2, 2)),
            sems((2, late, 2)),
            sems((2,)),
            sems((2, strips)),
            sems((4,)),
            sems((4,)),
            sems((4 * strips,)),
            sems((strips, 2)),
            sems((strips, 2)),
            sems((2,)),
            sems((2, G - 1)),
        ],
        compiler_params=pltpu.CompilerParams(
            collective_id=1, has_side_effects=True, vmem_limit_bytes=60 * 1024 * 1024
        ),
        cost_estimate=pl.CostEstimate(
            flops=9 * depth * width * width, bytes_accessed=4 * depth * width * 3, transcendentals=0
        ),
    )(panel, first_diag[None, :], x_hi, x_lo, own, block, flat, far, early)


def folded_body(kkt, border, first_diag, assignment, panel):
    slots, order, width = border.shape
    flat = border.reshape(slots * order, width)
    extra = jnp.where(lax.axis_index("scen") == panel[0], first_diag, 0.0)[None, :]
    x_hi, x_lo, own, block, far, strip = head_call(
        assignment, panel, extra, kkt, flat, width // 2
    )
    schur, factor, _ = tail_call(panel, first_diag, x_hi, x_lo, own, block, flat, far, strip)
    return (schur, factor)


def body(kkt, border, first_diag, assignment, panel):
    groups = lax.axis_size(GROUP)
    foldable = (
        groups == 4
        and lax.axis_size("row") == 2
        and lax.axis_size("scen") == 2 * groups
        and border.shape[2] == 2 * first_diag.shape[0]
        and first_diag.shape[0] == PW
    )
    chosen = folded_body if foldable else plain_body
    return chosen(kkt, border, first_diag, assignment, panel)


def solution(mesh):
    in_specs = (
        P("scen", ("row", "col"), None),
        P("scen", None, ("row", "col")),
        P("scen"),
        P("scen"),
        P(),
    )
    out_specs = (P("scen", ("row", "col")), P("scen", ("row", "col")))
    return jax.shard_map(body, mesh=mesh, in_specs=in_specs, out_specs=out_specs, check_vma=False)
```
